128 devices in a mesh: blk: 16 (over z_lo, x, core), dp: 8 (over z_hi, y).
Axes of the slice: x: 4, y: 4, z: 4 (z_hi: 2, z_lo: 2; z = z_hi * 2 + z_lo), core: 2. Of those that a mesh axis runs over, the one named last changes fastest.
Arguments:
- saved_query: bfloat16 [8, 4096, 640], P('dp', 'blk'), may hold values from -180 to 180
- saved_key: bfloat16 [8, 4096, 640], P('dp', 'blk'), may hold values from -6 to 6
- saved_value: bfloat16 [8, 4096, 640], P('dp', 'blk'), may hold values from -6 to 6
- out_weight: bfloat16 [640, 1280], replicated, may hold values from -0.15625 to 0.15625
- llm_grad: bfloat16 [8192, 5120], P(('blk', 'dp')), may hold values from -24 to 24
- row_source: int32 [8, 1024], P('dp', 'blk'), may hold values from 0 to 8191, as said below
- page_start: int32 [8, 16], P('dp', 'blk'), may hold values from 0 to 15, as said below
- page_size: int32 [8, 16], P('dp', 'blk'), may hold values from 1 to 15, as said below
Outputs:
- query_grad: bfloat16 [8, 4096, 640], P('dp', 'blk')
- key_grad: bfloat16 [8, 4096, 640], P('dp', 'blk')
- value_grad: bfloat16 [8, 4096, 640], P('dp', 'blk')
- weight_grad: float32 [1280, 640], P('blk', 'dp')
The draws below stay inside these ranges and needn't reach their ends.
Inputs may be any that keep to these rules, and one draw needn't show every extreme that they name: `row_source`: A permutation of the rows of llm_grad. For the device at blk index b of lane l, its merged rows j * 256 // (4 * 8) onward, 256 // (4 * 8) of them, come from the rows held by the llm_grad shard of index b * 8 + j, in any order. Pages tile each lane as runs of whole blocks: for every block, page_start and page_size give the run that contains it, and all blocks of a run carry the same two numbers. In every lane the first page spans more than half of the blocks. `page_size`: see page_start.
All inputs are finite; a program needn't handle non-finite values.
Results may differ from the reference program's by a relative error of at most 0.02.
Values may be sent and summed in bfloat16 or wider, within the bound.
A program may use at most 128 MiB of HBM per device.

```python
import math
import jax
import jax.numpy as jnp
from jax import lax

D = 1280
HEADS = 8
HD = 80
MERGE = 4
TOK_DEV = 256
HF = 640
SEQ = 4096
MROWS = 8192
N_BLK = 16
N_DP = 8


def pair_fields(key):
    folded = jax.random.fold_in(key, 7)
    split_keys = jax.random.split(folded, 2)
    key_field = jnp.clip(jax.random.normal(split_keys[0], (N_DP, SEQ, HF), jnp.float32), -6.0, 6.0)
    query_field = jnp.clip(jax.random.normal(split_keys[1], (N_DP, SEQ, HF), jnp.float32), -6.0, 6.0)
    return (query_field, key_field)


def draw_saved_query(key, part):
    return pair_fields(key)[0].astype(jnp.bfloat16)


def draw_saved_key(key, part):
    return pair_fields(key)[1].astype(jnp.bfloat16)


def page_layout(key):
    folded = jax.random.fold_in(key, 11)
    split_keys = jax.random.split(folded, 2)
    half_cycle = N_BLK // 2
    lane_index = jnp.arange(N_DP)
    leading = half_cycle + 1 + jax.random.randint(split_keys[0], (N_DP,), 0, N_BLK - half_cycle - 1)
    leading = jnp.where(lane_index == 0, N_BLK - 1, leading)
    coins = jax.random.randint(split_keys[1], (N_DP, N_BLK), 0, 2)
    position = jnp.arange(N_BLK)[None, :]
    after_first = position > leading[:, None]
    cut_here = (position == 0) | (position == leading[:, None]) | after_first & (coins == 1) | (position == N_BLK - 1) & (position >= leading[:, None])
    starts = lax.cummax(jnp.where(cut_here, position, 0), axis=1)
    marks = jnp.where(cut_here, position, N_BLK)
    following = jnp.concatenate([marks[:, 1:], jnp.full((N_DP, 1), N_BLK, marks.dtype)], axis=1)
    ending = lax.cummin(following, axis=1, reverse=True)
    return (starts.astype(jnp.int32), (ending - starts).astype(jnp.int32))


def draw_page_start(key, part):
    return page_layout(key)[0]


def draw_page_size(key, part):
    return page_layout(key)[1]


def draw_row_source(key, part):
    folded = jax.random.fold_in(key, 13)
    merged_rows = TOK_DEV // MERGE
    portion = merged_rows // N_DP
    owner_count = N_BLK * N_DP

    def shuffled(owner_index):
        return jax.random.permutation(jax.random.fold_in(folded, owner_index), merged_rows)
    orders = jax.vmap(shuffled)(jnp.arange(owner_count))
    orders = orders.reshape(N_BLK, N_DP, N_DP, portion)
    global_rows = orders + jnp.arange(owner_count).reshape(N_BLK, N_DP, 1, 1) * merged_rows
    return jnp.transpose(global_rows, (2, 0, 1, 3)).reshape(N_DP, N_BLK * merged_rows).astype(jnp.int32)


def strengthened(entries, stream_key, source, target, blocks, factor):
    def block_of(axis_at):
        return (jnp.arange(entries.shape[axis_at]) // (entries.shape[axis_at] // blocks)).reshape((-1,) + (1,) * (entries.ndim - 1 - axis_at))

    one_side = jax.random.permutation(stream_key, blocks)[block_of(target)]
    second = (block_of(target) + blocks // 2) % blocks
    return jnp.where((block_of(source) == one_side) | (block_of(source) == second), factor * entries, entries)


def levels(key, dims, shards, low, high):
    def one(dim, blocks):
        steps = jax.random.uniform(jax.random.fold_in(jax.random.fold_in(key, 6), dim), (blocks,), jnp.float32, low / len(shards), high / len(shards))
        return jnp.repeat(jnp.exp(steps), dims[dim] // blocks).reshape((-1,) + (1,) * (len(dims) - dim - 1))

    level = one(*shards[0])
    for cut in shards[1:]:
        level = level * one(*cut)
    return level


def gaussian(stream_key, extent, deviation, bound, cuts=(), kind=jnp.bfloat16):
    factor_of = levels(stream_key, extent, cuts, -0.22, 0.18) if cuts else 1.0
    values = jax.random.normal(stream_key, extent, jnp.float32) * deviation * factor_of
    return jnp.minimum(jnp.maximum(values, -bound), bound).astype(kind)


def bell_draw_with(own_key, dims, deviation, most, cuts, heavy, held_as=jnp.bfloat16):
    result = deviation * jax.random.normal(own_key, dims, jnp.float32)
    if cuts:
        result = result * levels(own_key, dims, cuts, -0.22, 0.18)
    return jnp.clip(strengthened(result, jax.random.fold_in(own_key, 3), *heavy), -most, most).astype(held_as)


def setup_inputs(seed: int = 0) -> dict:
    streams_of = jax.random.split(jax.random.key(seed), 9)
    return {
        "saved_query": draw_saved_query(jax.random.fold_in(streams_of[8], 71), 0),
        "saved_key": draw_saved_key(jax.random.fold_in(streams_of[8], 71), 0),
        "saved_value": gaussian(streams_of[2], (N_DP, SEQ, HF), 1.0, 6.0, ((0, 8), (1, 16))),
        "out_weight": gaussian(streams_of[3], (HF, D), D ** -0.5, 0.15625),
        "llm_grad": bell_draw_with(streams_of[4], (MROWS, MERGE * D), 1.0, 24.0, ((0, 128),), (0, 1, 128, 5.5)),
        "row_source": draw_row_source(jax.random.fold_in(streams_of[8], 71), 0),
        "page_start": draw_page_start(jax.random.fold_in(streams_of[8], 71), 0),
        "page_size": draw_page_size(jax.random.fold_in(streams_of[8], 71), 0),
    }


def round_low(values):
    return lax.optimization_barrier(values.astype(jnp.bfloat16)).astype(jnp.float32)

def reference(saved_query, saved_key, saved_value, out_weight, llm_grad, row_source, page_start, page_size):
    scaling = 1.0 / math.sqrt(HD)
    lane_count = saved_query.shape[0]
    seq_len = saved_query.shape[1]
    feat_width = saved_query.shape[2]
    model_width = out_weight.shape[1]
    merged = jnp.take(llm_grad, row_source.reshape(-1), axis=0)
    grad_out = merged.reshape(lane_count, seq_len, model_width)
    d_attn = jnp.dot(grad_out.reshape(-1, model_width), out_weight.T, preferred_element_type=jnp.float32)
    d_attn = d_attn.astype(jnp.bfloat16).reshape(lane_count, seq_len, feat_width)
    owner_block = jnp.arange(seq_len, dtype=jnp.int32) // TOK_DEV

    def lane_pass(inputs):
        q_lane, k_lane, v_lane, g_lane, do_lane, starts, page_sizes = inputs
        k_heads = k_lane.astype(jnp.float32).reshape(seq_len, HEADS, HD)
        v_heads = v_lane.astype(jnp.float32).reshape(seq_len, HEADS, HD)

        def block_step(carried, block_index):
            key_acc, value_acc, weight_acc = carried
            first_row = (block_index * TOK_DEV).astype(jnp.int32)
            q_block = lax.dynamic_slice_in_dim(q_lane, first_row, TOK_DEV, 0).astype(jnp.float32).reshape(TOK_DEV, HEADS, HD)
            do_block = lax.dynamic_slice_in_dim(do_lane, first_row, TOK_DEV, 0)
            do_heads = do_block.astype(jnp.float32).reshape(TOK_DEV, HEADS, HD)
            g_block = lax.dynamic_slice_in_dim(g_lane, first_row, TOK_DEV, 0)
            visible = (owner_block >= starts[block_index]) & (owner_block < starts[block_index] + page_sizes[block_index])
            visible = visible[None, None, :]
            scores = jnp.einsum('thd,shd->hts', q_block, k_heads) * scaling
            masked = jnp.where(visible, scores, -1e+30)
            highest = lax.optimization_barrier(jnp.max(masked, axis=2, keepdims=True))
            log_total = highest + jnp.log(lax.optimization_barrier(jnp.sum(jnp.exp(masked - highest), axis=2, keepdims=True)))
            attn_probs = jnp.where(visible, jnp.exp(scores - log_total), 0.0)
            probs_low = round_low(attn_probs)
            context = jnp.einsum('hts,shd->thd', probs_low, v_heads).reshape(TOK_DEV, feat_width).astype(jnp.bfloat16)
            row_delta = lax.optimization_barrier(jnp.sum(do_heads * context.astype(jnp.float32).reshape(TOK_DEV, HEADS, HD), axis=2)).T
            d_probs = jnp.einsum('thd,shd->hts', do_heads, v_heads)
            d_scores = round_low(attn_probs * (d_probs - row_delta[:, :, None]))
            q_grad = (jnp.einsum('hts,shd->thd', d_scores, k_heads).reshape(TOK_DEV, feat_width) * scaling).astype(jnp.bfloat16)
            key_acc = key_acc + jnp.einsum('hts,thd->shd', d_scores, q_block).reshape(seq_len, feat_width) * scaling
            value_acc = value_acc + jnp.einsum('hts,thd->shd', probs_low, do_heads).reshape(seq_len, feat_width)
            weight_acc = weight_acc + jnp.dot(g_block.T, context, preferred_element_type=jnp.float32)
            return ((key_acc, value_acc, weight_acc), q_grad)
        empty_rows = jnp.zeros((seq_len, feat_width), jnp.float32)
        empty_weight = jnp.zeros((model_width, feat_width), jnp.float32)
        totals, q_grads = lax.scan(block_step, (empty_rows, empty_rows, empty_weight), jnp.arange(N_BLK, dtype=jnp.int32))
        return (q_grads.reshape(seq_len, feat_width), totals[0].astype(jnp.bfloat16), totals[1].astype(jnp.bfloat16), totals[2])
    results = lax.map(lane_pass, (saved_query, saved_key, saved_value, grad_out, d_attn, page_start, page_size))
    return (results[0], results[1], results[2], lax.optimization_barrier(jnp.sum(results[3], axis=0)))
```

```python
import functools
import math

import jax
import jax.numpy as jnp
from jax import lax
from jax.experimental import pallas as pl
from jax.experimental.pallas import tpu as pltpu
from jax.sharding import PartitionSpec as P

HEADS = 8
HD = 80
MERGE = 4
TOK = 256
HF = HEADS * HD
NB = 16
ND = 8
PORTION = TOK // MERGE // ND
LANES = 128
HALF = TOK // 2
F32, BF16 = jnp.float32, jnp.bfloat16
FAR = -1e30
VM = pltpu.VMEM


def eye(n):
    return (lax.broadcasted_iota(jnp.int32, (n, n), 0) == lax.broadcasted_iota(jnp.int32, (n, n), 1)).astype(BF16)


def dot(a, b):
    return lax.dot_general(a, b, (((1,), (0,)), ((), ())), preferred_element_type=F32)


def dot_t(a, b):
    return lax.dot_general(a, b, (((1,), (1,)), ((), ())), preferred_element_type=F32)


def flip(x):
    return dot_t(eye(x.shape[1]), x)


def attention_kernel(tile, chunk, qT, kv, doT, page, dqT, dkvT, ctxT, krow, vrow, kT, sc, ps, ds, kacc, vacc):
    seq = kv.shape[2]
    queries = qT.shape[1]
    width = page.shape[1] // (seq // 256)
    scaling = 1.0 / math.sqrt(HD)
    c2 = scaling / math.log(2.0)
    tiles = seq // tile
    ident = eye(256)

    def prep(i, _):
        cols = pl.ds(pl.multiple_of(i * 256, 256), 256)
        pcols = pl.ds(pl.multiple_of(i * width, 128), 128)
        kT[0:80, cols] = kv[0, :, cols]
        kT[80:96, pl.ds(pl.multiple_of(i * 256, 128), 128)] = page[:, pcols]
        kT[80:96, pl.ds(pl.multiple_of(i * 256 + 128, 128), 128)] = page[:, pcols]
        krow[cols, :] = dot_t(ident, kT[:, cols]).astype(BF16)
        vrow[cols, :] = dot_t(ident, kv[1, :, cols]).astype(BF16)
        kacc[cols, :] = jnp.zeros((256, HD), F32)
        vacc[cols, :] = jnp.zeros((256, HD), F32)
        return 0

    lax.fori_loop(0, seq // 256, prep, 0)

    def one(i, _):
        cols = pl.ds(pl.multiple_of(i * chunk, chunk), chunk)
        q = qT[:, cols]
        far = (1.0 - page[:, cols].astype(F32)) * FAR
        qx = jnp.concatenate([q, far.astype(BF16)], axis=0)
        top = jnp.full((8, chunk), -3e38, F32)
        for j in range(tiles):
            rows = pl.ds(j * tile, tile)
            s = dot(krow[rows, :], qx)
            sc[rows, :] = s
            top = jnp.maximum(top, jnp.max(s.reshape(tile // 8, 8, chunk), axis=0))
        top = jnp.max(top, axis=0, keepdims=True) * c2
        total = jnp.zeros((8, chunk), F32)
        out = jnp.zeros((HD, chunk), F32)
        for j in range(tiles):
            rows = pl.ds(j * tile, tile)
            p = jnp.exp2(sc[rows, :] * c2 - top)
            total = total + jnp.sum(p.reshape(tile // 8, 8, chunk), axis=0)
            p = p.astype(BF16)
            ps[rows, :] = p
            out = out + dot(kv[1, :, rows], p)
        inv = 1.0 / jnp.sum(total, axis=0, keepdims=True)
        ctx = (out * inv).astype(BF16)
        ctxT[:, cols] = ctx
        do = doT[:, cols]
        dof = do.astype(F32)
        delta = jnp.sum(dof * ctx.astype(F32), axis=0, keepdims=True)
        don = dot_t(ident, (dof * inv).astype(BF16)).astype(BF16)
        qn = dot_t(ident, (q.astype(F32) * inv).astype(BF16)).astype(BF16)
        dq = jnp.zeros((HD, chunk), F32)
        for j in range(tiles):
            rows = pl.ds(j * tile, tile)
            p = ps[rows, :]
            dp = dot(vrow[rows, :], do)
            d = (p.astype(F32) * (dp - delta)).astype(BF16)
            vacc[rows, :] += dot(p, don)
            kacc[rows, :] += dot(d, qn)
            dq = dq + dot(kv[0, :, rows], d)
        dqT[:, cols] = (dq * (inv * scaling)).astype(BF16)
        return 0

    lax.fori_loop(0, queries // chunk, one, 0)
    small = eye(HD)

    def finish(i, _):
        cols = pl.ds(pl.multiple_of(i * 256, 256), 256)
        dkvT[0, :, cols] = dot_t(small, (kacc[cols, :] * scaling).astype(BF16)).astype(BF16)
        dkvT[1, :, cols] = dot_t(small, vacc[cols, :].astype(BF16)).astype(BF16)
        return 0

    lax.fori_loop(0, seq // 256, finish, 0)


def attention(qT, kv, doT, page, tile=512, chunk=256):
    seq = kv.shape[2]
    queries = qT.shape[1]
    return pl.pallas_call(
        functools.partial(attention_kernel, tile, chunk),
        out_shape=[
            jax.ShapeDtypeStruct((HD, queries), BF16),
            jax.ShapeDtypeStruct((2, HD, seq), BF16),
            jax.ShapeDtypeStruct((HD, queries), BF16),
        ],
        in_specs=[pl.BlockSpec(memory_space=VM)] * 4,
        out_specs=[pl.BlockSpec(memory_space=VM)] * 3,
        scratch_shapes=[
            VM((seq, 96), BF16), VM((seq, HD), BF16), VM((96, seq), BF16),
            VM((seq, chunk), F32), VM((seq, chunk), BF16), VM((seq, chunk), BF16),
            VM((seq, HD), F32), VM((seq, HD), F32),
        ],
        compiler_params=pltpu.CompilerParams(vmem_limit_bytes=56 * 2**20),
    )(qT, kv, doT, page)


def greet(blk, dp):
    barrier = pltpu.get_barrier_semaphore()

    def signal_blk(r, _):
        pl.semaphore_signal(barrier, inc=1, device_id={"blk": lax.rem(blk + r, NB)})
        return 0

    def signal_dp(r, _):
        pl.semaphore_signal(barrier, inc=1, device_id={"dp": lax.rem(dp + r, ND)})
        return 0

    lax.fori_loop(1, ND, signal_dp, 0)
    lax.fori_loop(1, NB, signal_blk, 0)
    return barrier


def each(low, high, act):
    def step(r, _):
        act(r)
        return 0

    lax.fori_loop(low, high, step, 0)


def place(index, size, align):
    return pl.ds(pl.multiple_of(index * size, align), size)


def remote(src, dst, send, recv, where):
    return pltpu.make_async_remote_copy(
        src_ref=src, dst_ref=dst, send_sem=send, recv_sem=recv, device_id=where
    )


def dispatch_kernel(
    q, k, v, w, llm, code, page_own,
    qT, kv, doT, page, grad,
    q_own, kv_own, codes, do_rows, do_mine, do_own,
    code_s, code_r, page_s, page_r, q_s, q_r, kv_s, kv_r, do_s, do_r, dt_s, dt_r, relay_s, relay_r, local,
):
    blk, dp = lax.axis_index("blk"), lax.axis_index("dp")
    core = lax.rem(blk, 2)
    sibling = blk + 1 - 2 * core
    head = blk // 2
    barrier = greet(blk, dp)
    ident = eye(LANES)
    for i in range(HF // LANES):
        rows = pl.ds(i * LANES, LANES)
        q_own[rows, :] = dot_t(ident, q[:, i * LANES : (i + 1) * LANES]).astype(BF16)
        kv_own[0, rows, :] = dot_t(ident, k[:, i * LANES : (i + 1) * LANES]).astype(BF16)
        kv_own[1, rows, :] = dot_t(ident, v[:, i * LANES : (i + 1) * LANES]).astype(BF16)
    codes[pl.ds(dp, 1)] = code[pl.ds(dp, 1)]
    pl.semaphore_wait(barrier, NB + ND - 2)

    def code_copy(r):
        to = lax.rem(dp + r, ND)
        return remote(code.at[to], codes.at[dp], code_s.at[r], code_r.at[r], {"dp": to})

    def page_copy(r):
        to = lax.rem(blk + r, NB)
        return remote(page_own, page.at[:, place(blk, HALF, HALF)], page_s.at[r], page_r.at[r], {"blk": to})

    def q_copy(r):
        to = lax.rem(blk + r, NB)
        src = q_own.at[place(to // 2, HD, 16), place(lax.rem(to, 2), HALF, HALF)]
        return remote(src, qT.at[:, place(blk, HALF, HALF)], q_s.at[r], q_r.at[r], {"blk": to})

    def kv_copy(r):
        to = lax.rem(blk + r, NB)
        kind = lax.rem(to, 2)
        src = kv_own.at[kind, place(to // 2, HD, 16), :]
        return remote(src, kv.at[kind, :, place(blk, TOK, TOK)], kv_s.at[r], kv_r.at[r], {"blk": to})

    def relay_copy(r):
        block = kv.at[core, :, place(lax.rem(blk + NB - r, NB), TOK, TOK)]
        return remote(block, block, relay_s.at[r], relay_r.at[r], {"blk": sibling})

    def do_copy(r):
        to = lax.rem(dp + r, ND)
        return remote(
            do_rows.at[place(to, 4 * PORTION, 32), :], do_mine.at[place(dp, 4 * PORTION, 32), :],
            do_s.at[r], do_r.at[r], {"dp": to},
        )

    def dt_copy(r):
        to = lax.rem(blk + r, NB)
        src = do_own.at[place(to // 2, HD, 16), place(lax.rem(to, 2), HALF, HALF)]
        return remote(src, doT.at[:, place(blk, HALF, HALF)], dt_s.at[r], dt_r.at[r], {"blk": to})

    each(1, ND, lambda r: code_copy(r).start())

    def first(r):
        kv_copy(r).start()
        q_copy(r).start()
        page_copy(r).start()

    each(1, NB, first)
    mine = [
        pltpu.make_async_copy(kv_own.at[core, place(head, HD, 16), :], kv.at[core, :, place(blk, TOK, TOK)], local.at[0]),
        pltpu.make_async_copy(
            q_own.at[place(head, HD, 16), place(core, HALF, HALF)], qT.at[:, place(blk, HALF, HALF)], local.at[1]
        ),
        pltpu.make_async_copy(page_own, page.at[:, place(blk, HALF, HALF)], local.at[2]),
    ]
    for copy in mine:
        copy.start()
    for copy in mine:
        copy.wait()
    relay_copy(0).start()

    each(1, ND, lambda r: code_copy(r).wait_recv())
    asked = codes[...].reshape(ND * PORTION, LANES).astype(F32).astype(BF16)
    tok = lax.broadcasted_iota(jnp.int32, (TOK, ND * PORTION), 0)
    spread = (tok // MERGE == lax.broadcasted_iota(jnp.int32, (TOK, ND * PORTION), 1)).astype(BF16)
    row = dot(spread, asked)
    lane = lax.broadcasted_iota(jnp.int32, (TOK, LANES), 1).astype(F32)
    part = lax.rem(lax.broadcasted_iota(jnp.int32, (TOK, LANES), 0), MERGE)
    width = w.shape[1]
    rows = jnp.zeros((TOK, width), F32)
    for m in range(MERGE):
        hot = jnp.where((row == lane) & (part == m), 1.0, 0.0).astype(BF16)
        rows = rows + dot(hot[:, : llm.shape[0]], llm[:, m * width : (m + 1) * width])
    rows = rows.astype(BF16)
    grad[...] = rows
    do_rows[...] = dot_t(rows, w[...]).astype(BF16)

    def relay(r):
        kv_copy(r).wait_recv()
        relay_copy(r).start()

    each(1, 4, relay)
    each(1, ND, lambda r: do_copy(r).start())
    do_mine[place(dp, 4 * PORTION, 32), :] = do_rows[place(dp, 4 * PORTION, 32), :]
    each(4, NB // 2, relay)
    each(1, ND, lambda r: do_copy(r).wait_recv())
    for i in range(HF // LANES):
        do_own[pl.ds(i * LANES, LANES), :] = dot_t(ident, do_mine[:, i * LANES : (i + 1) * LANES]).astype(BF16)
    each(NB // 2, NB // 2 + 2, relay)
    each(1, NB, lambda r: dt_copy(r).start())
    own = pltpu.make_async_copy(
        do_own.at[place(head, HD, 16), place(core, HALF, HALF)], doT.at[:, place(blk, HALF, HALF)], local.at[3]
    )
    own.start()
    each(NB // 2 + 2, NB, relay)
    own.wait()

    def last(r):
        q_copy(r).wait_recv()
        page_copy(r).wait_recv()
        dt_copy(r).wait_recv()
        q_copy(r).wait_send()
        page_copy(r).wait_send()
        kv_copy(r).wait_send()
        dt_copy(r).wait_send()

    each(1, NB, last)
    each(0, NB, lambda r: relay_copy(r).wait())

    def last_dp(r):
        code_copy(r).wait_send()
        do_copy(r).wait_send()

    each(1, ND, last_dp)


def dispatch(q, k, v, w, llm, code, page_own):
    seq = NB * TOK
    dma = pltpu.SemaphoreType.DMA
    return pl.pallas_call(
        dispatch_kernel,
        out_shape=[
            jax.ShapeDtypeStruct((HD, seq // 2), BF16),
            jax.ShapeDtypeStruct((2, HD, seq), BF16),
            jax.ShapeDtypeStruct((HD, seq // 2), BF16),
            jax.ShapeDtypeStruct((NB, seq // 2), BF16),
            jax.ShapeDtypeStruct((TOK, w.shape[1]), BF16),
        ],
        in_specs=[pl.BlockSpec(memory_space=VM)] * 7,
        out_specs=[pl.BlockSpec(memory_space=VM)] * 5,
        scratch_shapes=[
            VM((HF, TOK), BF16), VM((2, HF, TOK), BF16), VM((ND, PORTION, LANES), jnp.int32),
            VM((TOK, HF), BF16), VM((TOK, HF), BF16), VM((HF, TOK), BF16),
            dma((ND,)), dma((ND,)), dma((NB,)), dma((NB,)), dma((NB,)), dma((NB,)), dma((NB,)), dma((NB,)),
            dma((ND,)), dma((ND,)), dma((NB,)), dma((NB,)), dma((NB,)), dma((NB,)), dma((4,)),
        ],
        compiler_params=pltpu.CompilerParams(
            collective_id=0, has_side_effects=True, vmem_limit_bytes=32 * 2**20
        ),
    )(q, k, v, w, llm, code, page_own)


def collect_kernel(
    dqT, dkvT, ctxT, grad,
    q_out, k_out, v_out, w_out,
    ctx_own, ctx_rows, ctx_mine, dq_own, dkv_own, partner, summed, pair_out, pair_in, pair, lanes_in, turned, blocks_in,
    c_s, c_r, q_s, q_r, x_s, x_r, kv_s, kv_r, r_s, r_r, p_s, p_r, l_s, l_r, b_s, b_r, local,
):
    blk, dp = lax.axis_index("blk"), lax.axis_index("dp")
    core = lax.rem(blk, 2)
    sibling = blk + 1 - 2 * core
    head = blk // 2
    barrier = greet(blk, dp)
    pl.semaphore_wait(barrier, NB + ND - 2)
    mine_at = (place(head, HD, 16), place(core, HALF, HALF))

    def c_copy(r):
        to = lax.rem(blk + r, NB)
        return remote(ctxT.at[:, place(to, HALF, HALF)], ctx_own.at[mine_at], c_s.at[r], c_r.at[r], {"blk": to})

    def q_copy(r):
        to = lax.rem(blk + r, NB)
        return remote(dqT.at[:, place(to, HALF, HALF)], dq_own.at[mine_at], q_s.at[r], q_r.at[r], {"blk": to})

    def x_copy(r):
        block = place(lax.rem(sibling + r, NB), TOK, TOK)
        return remote(dkvT.at[1 - core, :, block], partner.at[:, block], x_s.at[r], x_r.at[r], {"blk": sibling})

    def kv_copy(r):
        to = lax.rem(blk + r, NB)
        return remote(
            summed.at[:, place(to, TOK, TOK)], dkv_own.at[core, place(head, HD, 16), :],
            kv_s.at[r], kv_r.at[r], {"blk": to},
        )

    def r_copy(r):
        to = lax.rem(dp + r, ND)
        return remote(
            ctx_rows.at[place(to, 4 * PORTION, 32), :], ctx_mine.at[place(dp, 4 * PORTION, 32), :],
            r_s.at[r], r_r.at[r], {"dp": to},
        )

    each(1, NB, lambda r: c_copy(r).start())
    each(0, NB, lambda r: x_copy(r).start())
    mine = [
        pltpu.make_async_copy(ctxT.at[:, place(blk, HALF, HALF)], ctx_own.at[mine_at], local.at[0]),
        pltpu.make_async_copy(dqT.at[:, place(blk, HALF, HALF)], dq_own.at[mine_at], local.at[1]),
    ]
    for copy in mine:
        copy.start()

    def add_up(r):
        block = place(lax.rem(blk + r, NB), TOK, TOK)
        x_copy(r).wait_recv()
        summed[:, block] = (dkvT[core, :, block].astype(F32) + partner[:, block].astype(F32)).astype(BF16)

    add_up(1)

    def add_and_send(r):
        add_up(r)
        kv_copy(r - 1).start()

    each(2, NB, add_and_send)
    add_up(0)
    kv_copy(NB - 1).start()
    each(1, NB, lambda r: q_copy(r).start())
    own = pltpu.make_async_copy(
        summed.at[:, place(blk, TOK, TOK)], dkv_own.at[core, place(head, HD, 16), :], local.at[2]
    )
    own.start()
    for copy in mine:
        copy.wait()

    each(1, NB, lambda r: c_copy(r).wait_recv())
    big = eye(TOK)
    ctx_rows[...] = dot_t(big, ctx_own[...]).astype(BF16)
    ctx_mine[place(dp, 4 * PORTION, 32), :] = ctx_rows[place(dp, 4 * PORTION, 32), :]
    each(1, ND, lambda r: r_copy(r).start())
    each(1, ND, lambda r: r_copy(r).wait_recv())
    ident = eye(LANES)
    wide = grad.shape[1] // 2
    for i in range(HF // LANES):
        turn = dot_t(ident, ctx_mine[:, i * LANES : (i + 1) * LANES]).astype(BF16)
        part = dot(turn, grad[...])
        rows = pl.ds(i * LANES, LANES)
        pair_out[0, rows, :] = part[:, :wide].astype(BF16)
        pair_out[1, rows, :] = part[:, wide:].astype(BF16)

    def p_copy(r):
        rows = place(lax.rem(dp + r, ND), HD, 16)
        return remote(pair_out.at[1 - core, rows, :], pair_in.at[rows, :], p_s.at[r], p_r.at[r], {"blk": sibling})

    def l_copy(r):
        to = lax.rem(dp + r, ND)
        return remote(pair.at[place(to, HD, 16), :], lanes_in.at[r], l_s.at[r], l_r.at[r], {"dp": to})

    each(0, ND, lambda r: p_copy(r).start())

    def pair_up(r):
        rows = place(lax.rem(dp + r, ND), HD, 16)
        p_copy(r).wait_recv()
        pair[rows, :] = (pair_out[core, rows, :].astype(F32) + pair_in[rows, :].astype(F32)).astype(BF16)

    pair_up(1)

    def pair_and_send(r):
        pair_up(r)
        l_copy(r - 1).start()

    each(2, ND, pair_and_send)
    pair_up(0)
    l_copy(ND - 1).start()
    total = pair[place(dp, HD, 16), :].astype(F32)
    for r in range(1, ND):
        l_copy(r).wait_recv()
        total = total + lanes_in[r].astype(F32)
    total = total.astype(BF16)
    for i in range(wide // LANES):
        turned[pl.ds(i * LANES, LANES), :] = dot_t(ident, total[:, i * LANES : (i + 1) * LANES]).astype(BF16)

    def b_copy(i):
        return remote(
            turned.at[place(i, HD, 16), :], blocks_in.at[head], b_s.at[i], b_r.at[head], {"blk": NB // 2 * core + i}
        )

    def b_wait(i):
        return remote(turned.at[place(i, HD, 16), :], blocks_in.at[i], b_s.at[i], b_r.at[i], {"blk": sibling})

    def b_send(i):
        @pl.when(NB // 2 * core + i != blk)
        def _():
            b_copy(i).start()

    each(0, NB // 2, b_send)
    source_core = blk // (NB // 2)
    inside = lax.rem(blk, NB // 2)

    @pl.when(source_core == core)
    def _():
        blocks_in[pl.ds(head, 1)] = turned[place(inside, HD, 16), :][None]

    own.wait()

    def rest(r):
        q_copy(r).wait_recv()
        kv_copy(r).wait_recv()

    each(1, NB, rest)
    q_out[...] = dot_t(big, dq_own[...]).astype(BF16)
    k_out[...] = dot_t(big, dkv_own[0]).astype(BF16)
    v_out[...] = dot_t(big, dkv_own[1]).astype(BF16)

    def b_recv(i):
        @pl.when(2 * i + source_core != blk)
        def _():
            b_wait(i).wait_recv()

    each(0, NB // 2, b_recv)
    whole = jnp.zeros((HD, HD), F32)
    for i in range(NB // 2):
        whole = whole + blocks_in[i].astype(F32)
    w_out[...] = whole

    def b_sent(i):
        @pl.when(NB // 2 * core + i != blk)
        def _():
            b_copy(i).wait_send()

    each(0, NB // 2, b_sent)

    def sent(r):
        c_copy(r).wait_send()
        q_copy(r).wait_send()
        kv_copy(r).wait_send()

    each(1, NB, sent)
    each(0, NB, lambda r: x_copy(r).wait_send())
    each(0, ND, lambda r: p_copy(r).wait_send())

    def sent_dp(r):
        r_copy(r).wait_send()
        l_copy(r).wait_send()

    each(1, ND, sent_dp)


def collect(dqT, dkvT, ctxT, grad):
    seq = NB * TOK
    wide = grad.shape[1] // 2
    dma = pltpu.SemaphoreType.DMA
    return pl.pallas_call(
        collect_kernel,
        out_shape=[jax.ShapeDtypeStruct((TOK, HF), BF16)] * 3 + [jax.ShapeDtypeStruct((HD, HD), F32)],
        in_specs=[pl.BlockSpec(memory_space=VM)] * 4,
        out_specs=[pl.BlockSpec(memory_space=VM)] * 4,
        scratch_shapes=[
            VM((HF, TOK), BF16), VM((TOK, HF), BF16), VM((TOK, HF), BF16), VM((HF, TOK), BF16),
            VM((2, HF, TOK), BF16), VM((HD, seq), BF16), VM((HD, seq), BF16),
            VM((2, HF, wide), BF16), VM((HF, wide), BF16), VM((HF, wide), BF16), VM((ND, HD, wide), BF16),
            VM((wide, HD), BF16), VM((NB // 2, HD, HD), BF16),
            dma((NB,)), dma((NB,)), dma((NB,)), dma((NB,)), dma((NB,)), dma((NB,)), dma((NB,)), dma((NB,)),
            dma((ND,)), dma((ND,)), dma((ND,)), dma((ND,)), dma((ND,)), dma((ND,)),
            dma((NB // 2,)), dma((NB // 2,)), dma((3,)),
        ],
        compiler_params=pltpu.CompilerParams(
            collective_id=1, has_side_effects=True, vmem_limit_bytes=32 * 2**20
        ),
    )(dqT, dkvT, ctxT, grad)


def body(saved_query, saved_key, saved_value, out_weight, llm_grad, row_source, page_start, page_size):
    blk = lax.axis_index("blk")
    rows = llm_grad.shape[0]
    holder = (blk * ND + jnp.arange(ND, dtype=jnp.int32)) * rows
    code = row_source[0].reshape(ND, PORTION) - holder[:, None]
    code = jnp.broadcast_to(code[:, :, None], (ND, PORTION, LANES))
    first = (jnp.arange(NB, dtype=jnp.int32) == page_start[0, 0]).astype(BF16)
    page_own = jnp.broadcast_to(first[:, None], (NB, HALF))
    qT, kv, doT, page, grad = dispatch(
        saved_query[0], saved_key[0], saved_value[0], out_weight, llm_grad, code, page_own
    )
    dqT, dkvT, ctxT = attention(qT, kv, doT, page)
    query_grad, key_grad, value_grad, weight_grad = collect(dqT, dkvT, ctxT, grad)
    return (query_grad[None], key_grad[None], value_grad[None], weight_grad)


def solution(mesh):
    in_specs = (
        P("dp", "blk", None),
        P("dp", "blk", None),
        P("dp", "blk", None),
        P(),
        P(("blk", "dp"), None),
        P("dp", "blk"),
        P("dp", "blk"),
        P("dp", "blk"),
    )
    out_specs = (P("dp", "blk", None), P("dp", "blk", None), P("dp", "blk", None), P("blk", "dp"))
    return jax.shard_map(body, mesh=mesh, in_specs=in_specs, out_specs=out_specs, check_vma=False)
```

```python
import math

import jax
import jax.numpy as jnp
from jax import lax
from jax.experimental import pallas as pl
from jax.experimental.pallas import tpu as pltpu
from jax.sharding import PartitionSpec as P

HEADS = 8
HD = 80
MERGE = 4
TOK = 256
HF = HEADS * HD
NB = 16
ND = 8
PORTION = TOK // MERGE // ND
SENT = TOK // ND
LANES = 128
HALF = TOK // 2
SEQ = NB * TOK
QUERIES = SEQ // 2
CHUNK = 256
CHUNKS = QUERIES // CHUNK
TILE = 512
PAIR = 2 * TOK
PAIRS = SEQ // PAIR
DEEP = HD + NB
SCALE = 1.0 / math.sqrt(HD)
EXP2 = SCALE / math.log(2.0)
F32, BF16 = jnp.float32, jnp.bfloat16
FAR = -1e30
VM = pltpu.VMEM


def eye(n):
    return (lax.broadcasted_iota(jnp.int32, (n, n), 0) == lax.broadcasted_iota(jnp.int32, (n, n), 1)).astype(BF16)


def dot(a, b):
    return lax.dot_general(a, b, (((1,), (0,)), ((), ())), preferred_element_type=F32)


def dot_t(a, b):
    return lax.dot_general(a, b, (((1,), (1,)), ((), ())), preferred_element_type=F32)


def each(low, high, act):
    def step(r, _):
        act(r)
        return 0

    lax.fori_loop(low, high, step, 0)


def place(index, size, align):
    return pl.ds(pl.multiple_of(index * size, align), size)


def remote(src, dst, send, recv, where):
    return pltpu.make_async_remote_copy(
        src_ref=src, dst_ref=dst, send_sem=send, recv_sem=recv, device_id=where
    )


def layer_kernel(
    q, k, v, w, llm, code, page_own,
    q_out, k_out, v_out, w_out,
    own, do_own, codes, do_rows, do_mine, grad,
    qT, kT, vT, doT, page, krow, vrow, sa, sb, ps, ds, don, qn, stat, dqa, ctxT, dqT,
    part, partner, summed, ctx_own, ctx_rows, ctx_mine, dq_own, dkv_own,
    pair_out, pair_in, pair, lanes_in, turned, blocks_in,
    code_s, code_r, page_s, page_r, q_s, q_r, k_s, k_r, v_s, v_r, do_s, do_r, dt_s, dt_r, kk_s, kk_r, vv_s, vv_r,
    c_s, c_r, dq_s, dq_r, x_s, x_r, kv_s, kv_r, r_s, r_r, p_s, p_r, l_s, l_r, b_s, b_r, local,
):
    blk, dp = lax.axis_index("blk"), lax.axis_index("dp")
    core = lax.rem(blk, 2)
    sibling = blk + 1 - 2 * core
    head = blk // 2
    width = w.shape[1]
    wide = width // 2

    barrier = pltpu.get_barrier_semaphore()
    each(1, ND, lambda r: pl.semaphore_signal(barrier, inc=1, device_id={"dp": lax.rem(dp + r, ND)}))
    each(1, NB, lambda r: pl.semaphore_signal(barrier, inc=1, device_id={"blk": lax.rem(blk + r, NB)}))
    ident = eye(LANES)
    big = eye(TOK)
    small = eye(HD)
    for n, x in enumerate((k, v, q)):
        for i in range(HF // LANES):
            own[n, pl.ds(i * LANES, LANES), :] = dot_t(ident, x[:, i * LANES : (i + 1) * LANES]).astype(BF16)
    codes[pl.ds(dp, 1)] = code[pl.ds(dp, 1)]
    pl.semaphore_wait(barrier, NB + ND - 2)

    def towards(r):
        return lax.rem(blk + r, NB)

    def piece(n, to):
        return own.at[n, place(to // 2, HD, 16), place(lax.rem(to, 2), HALF, HALF)]

    def code_copy(r):
        to = lax.rem(dp + r, ND)
        return remote(code.at[to], codes.at[dp], code_s.at[r], code_r.at[r], {"dp": to})

    def page_copy(r):
        return remote(
            page_own, page.at[:, place(blk, HALF, HALF)], page_s.at[r], page_r.at[r], {"blk": towards(r)}
        )

    def key_lanes(block, side):
        return pl.ds(pl.multiple_of(block * TOK + side * HALF, HALF), HALF)

    def k_copy(r):
        to = towards(r)
        dst = kT.at[pl.ds(0, HD), key_lanes(blk, lax.rem(to, 2))]
        return remote(piece(0, to), dst, k_s.at[r], k_r.at[r], {"blk": to})

    def v_copy(r):
        to = towards(r)
        return remote(piece(1, to), vT.at[:, key_lanes(blk, lax.rem(to, 2))], v_s.at[r], v_r.at[r], {"blk": to})

    def q_copy(r):
        to = towards(r)
        return remote(piece(2, to), qT.at[:, place(blk, HALF, HALF)], q_s.at[r], q_r.at[r], {"blk": to})

    def kk_copy(r):
        half = kT.at[pl.ds(0, HD), key_lanes(lax.rem(blk + NB - r, NB), core)]
        return remote(half, half, kk_s.at[r], kk_r.at[r], {"blk": sibling})

    def vv_copy(r):
        half = vT.at[:, key_lanes(lax.rem(blk + NB - r, NB), core)]
        return remote(half, half, vv_s.at[r], vv_r.at[r], {"blk": sibling})

    def do_copy(r):
        to = lax.rem(dp + r, ND)
        return remote(
            do_rows.at[place(to, SENT, 32), :], do_mine.at[place(dp, SENT, 32), :], do_s.at[r], do_r.at[r], {"dp": to}
        )

    def dt_copy(r):
        to = towards(r)
        src = do_own.at[place(to // 2, HD, 16), place(lax.rem(to, 2), HALF, HALF)]
        return remote(src, doT.at[:, place(blk, HALF, HALF)], dt_s.at[r], dt_r.at[r], {"blk": to})

    mine_at = (place(head, HD, 16), place(core, HALF, HALF))

    def c_copy(r):
        to = towards(r)
        return remote(ctxT.at[:, place(to, HALF, HALF)], ctx_own.at[mine_at], c_s.at[r], c_r.at[r], {"blk": to})

    def dq_copy(r):
        to = towards(r)
        return remote(dqT.at[:, place(to, HALF, HALF)], dq_own.at[mine_at], dq_s.at[r], dq_r.at[r], {"blk": to})

    def x_copy(block):
        lanes = key_lanes(block, 1 - core)
        return remote(
            part.at[:, :, lanes], partner.at[:, :, place(block, HALF, HALF)], x_s.at[block], x_r.at[block],
            {"blk": sibling},
        )

    def kv_copy(block):
        r = lax.rem(block + NB - blk, NB)
        return remote(
            summed.at[:, :, place(block, HALF, HALF)], dkv_own.at[:, mine_at[0], mine_at[1]],
            kv_s.at[r], kv_r.at[r], {"blk": block},
        )

    def r_copy(r):
        to = lax.rem(dp + r, ND)
        return remote(
            ctx_rows.at[place(to, SENT, 32), :], ctx_mine.at[place(dp, SENT, 32), :], r_s.at[r], r_r.at[r], {"dp": to}
        )

    def p_copy(r):
        rows = place(lax.rem(dp + r, ND), HD, 16)
        return remote(pair_out.at[1 - core, rows, :], pair_in.at[rows, :], p_s.at[r], p_r.at[r], {"blk": sibling})

    def l_copy(r):
        to = lax.rem(dp + r, ND)
        return remote(pair.at[place(to, HD, 16), :], lanes_in.at[r], l_s.at[r], l_r.at[r], {"dp": to})

    def b_copy(i):
        return remote(
            turned.at[place(i, HD, 16), :], blocks_in.at[head], b_s.at[i], b_r.at[head], {"blk": NB // 2 * core + i}
        )

    def b_wait(i):
        return remote(turned.at[place(i, HD, 16), :], blocks_in.at[i], b_s.at[i], b_r.at[i], {"blk": sibling})

    each(1, ND, lambda r: code_copy(r).start())

    def send_keys(r):
        page_copy(r).start()
        k_copy(r).start()

    each(1, NB, send_keys)
    each(1, NB, lambda r: v_copy(r).start())
    each(1, NB, lambda r: q_copy(r).start())
    mine = [
        pltpu.make_async_copy(piece(0, blk), kT.at[pl.ds(0, HD), key_lanes(blk, core)], local.at[0]),
        pltpu.make_async_copy(piece(1, blk), vT.at[:, key_lanes(blk, core)], local.at[1]),
        pltpu.make_async_copy(piece(2, blk), qT.at[:, place(blk, HALF, HALF)], local.at[2]),
        pltpu.make_async_copy(page_own, page.at[:, place(blk, HALF, HALF)], local.at[3]),
    ]
    for copy in mine:
        copy.start()
    for copy in mine:
        copy.wait()
    kk_copy(0).start()
    vv_copy(0).start()

    each(1, ND, lambda r: code_copy(r).wait_recv())
    asked = codes[...].reshape(ND * PORTION, LANES).astype(F32).astype(BF16)
    tok = lax.broadcasted_iota(jnp.int32, (TOK, ND * PORTION), 0)
    spread = (tok // MERGE == lax.broadcasted_iota(jnp.int32, (TOK, ND * PORTION), 1)).astype(BF16)
    row = dot(spread, asked)
    lane = lax.broadcasted_iota(jnp.int32, (TOK, LANES), 1).astype(F32)
    turn_of = lax.rem(lax.broadcasted_iota(jnp.int32, (TOK, LANES), 0), MERGE)
    rows = jnp.zeros((TOK, width), F32)
    for m in range(MERGE):
        hot = jnp.where((row == lane) & (turn_of == m), 1.0, 0.0).astype(BF16)
        rows = rows + dot(hot[:, : llm.shape[0]], llm[:, m * width : (m + 1) * width])
    rows = rows.astype(BF16)
    grad[...] = rows
    do_rows[...] = dot_t(rows, w[...]).astype(BF16)

    def relay_key(r):
        k_copy(r).wait_recv()
        kk_copy(r).start()
        page_copy(r).wait_recv()

    def key_block(r):
        kk_copy(r).wait_recv()
        block = lax.rem(sibling + NB - r, NB)
        cols = place(block, TOK, TOK)
        mark = page[:, place(block, HALF, HALF)]
        kT[HD:DEEP, key_lanes(block, 0)] = mark
        kT[HD:DEEP, key_lanes(block, 1)] = mark
        krow[cols, :] = dot_t(big, kT[:, cols]).astype(BF16)

    relay_key(1)
    relay_key(2)
    each(1, ND, lambda r: do_copy(r).start())
    do_mine[place(dp, SENT, 32), :] = do_rows[place(dp, SENT, 32), :]

    def relay_and_key(r):
        relay_key(r)
        key_block(r - 2)

    each(3, NB, relay_and_key)
    key_block(NB - 2)
    key_block(NB - 1)
    key_block(0)

    def chunk_at(i):
        return lax.rem(head + CHUNKS - i, CHUNKS)

    def wait_q(i):
        for off in (NB, NB - 1):
            r = lax.rem(core + 2 * i + off, NB)

            @pl.when(r != 0)
            def _():
                q_copy(r).wait_recv()

    def query(i):
        cols = place(chunk_at(i), CHUNK, CHUNK)
        far = (1.0 - page[:, cols].astype(F32)) * FAR
        return jnp.concatenate([qT[:, cols], far.astype(BF16)], axis=0)

    def mix(cur, now, nxt, then, top):
        qx = query(then)
        cols = place(chunk_at(now), CHUNK, CHUNK)
        new = jnp.full((8, CHUNK), -3e38, F32)
        total = jnp.zeros((8, CHUNK), F32)
        out = jnp.zeros((HD, CHUNK), F32)
        for j in range(SEQ // TILE):
            rows = pl.ds(j * TILE, TILE)
            s = dot(krow[rows, :], qx)
            nxt[rows, :] = s
            new = jnp.maximum(new, jnp.max(s.reshape(TILE // 8, 8, CHUNK), axis=0))
            if cur is not None:
                p = jnp.exp2(cur[rows, :] * EXP2 - top)
                total = total + jnp.sum(p.reshape(TILE // 8, 8, CHUNK), axis=0)
                p = p.astype(BF16)
                ps[rows, cols] = p
                out = out + dot(vT[:, rows], p)
        if cur is not None:
            inv = 1.0 / jnp.sum(total, axis=0, keepdims=True)
            ctxT[:, cols] = (out * inv).astype(BF16)
            stat[0:1, cols] = inv
        return jnp.max(new, axis=0, keepdims=True) * EXP2

    def send_context(i):
        for e in (0, 1):
            r = lax.rem(4 * NB - core - 2 * i + e, NB)

            @pl.when(r != 0)
            def _():
                c_copy(r).start()

    wait_q(0)
    top = mix(None, 0, sa, 0, None)

    def relay_value(r):
        v_copy(r).wait_recv()
        vv_copy(r).start()

    def value_block(r):
        vv_copy(r).wait_recv()
        cols = place(lax.rem(sibling + NB - r, NB), TOK, TOK)
        vrow[cols, :] = dot_t(big, vT[:, cols]).astype(BF16)

    relay_value(1)
    relay_value(2)

    def relay_and_value(r):
        relay_value(r)
        value_block(r - 2)

    each(3, NB, relay_and_value)
    value_block(NB - 2)
    value_block(NB - 1)
    value_block(0)

    def forward(i, top):
        wait_q(2 * i + 1)
        top = mix(sa, 2 * i, sb, 2 * i + 1, top)

        @pl.when(i > 0)
        def _():
            send_context(2 * i - 1)

        @pl.when(i < CHUNKS // 2 - 1)
        def _():
            wait_q(2 * i + 2)

        top = mix(sb, 2 * i + 1, sa, lax.rem(2 * i + 2, CHUNKS), top)
        send_context(2 * i)

        @pl.when(i == 0)
        def _():
            each(1, ND, lambda r: do_copy(r).wait_recv())
            for n in range(HF // LANES):
                lanes = slice(n * LANES, (n + 1) * LANES)
                do_own[pl.ds(n * LANES, LANES), :] = dot_t(ident, do_mine[:, lanes]).astype(BF16)
            each(1, NB, lambda r: dt_copy(r).start())
            pltpu.make_async_copy(
                do_own.at[mine_at], doT.at[:, place(blk, HALF, HALF)], local.at[4]
            ).start()

        return top

    lax.fori_loop(0, CHUNKS // 2, forward, top)
    send_context(CHUNKS - 1)
    own_context = pltpu.make_async_copy(ctxT.at[:, place(blk, HALF, HALF)], ctx_own.at[mine_at], local.at[5])
    own_context.start()
    pltpu.make_async_copy(do_own.at[mine_at], doT.at[:, place(blk, HALF, HALF)], local.at[4]).wait()
    each(1, NB, lambda r: dt_copy(r).wait_recv())

    def middle(i):
        cols = place(i, CHUNK, CHUNK)
        inv = stat[0:1, cols]
        dof = doT[:, cols].astype(F32)
        stat[1:2, cols] = jnp.sum(dof * ctxT[:, cols].astype(F32), axis=0, keepdims=True)
        don[cols, :] = dot_t(big, (dof * inv).astype(BF16)).astype(BF16)
        qn[cols, :] = dot_t(big, (qT[:, cols].astype(F32) * inv).astype(BF16)).astype(BF16)
        dqa[:, cols] = jnp.zeros((HD, CHUNK), F32)

    each(0, CHUNKS, middle)

    def chip_at(j):
        return lax.rem(head + 1 + j, PAIRS)

    def cross(j):
        for e in (0, 1):
            x_copy(2 * chip_at(j) + e).start()

    def add_up(j):
        for e in (0, 1):
            block = 2 * chip_at(j) + e
            x_copy(block).wait_recv()
            at = place(block, HALF, HALF)
            summed[:, :, at] = (
                part[:, :, key_lanes(block, core)].astype(F32) + partner[:, :, at].astype(F32)
            ).astype(BF16)

    def hand_out(j):
        for e in (0, 1):
            kv_copy(2 * chip_at(j) + e).start()

    def turn_context():
        own_context.wait()
        each(1, NB, lambda r: c_copy(r).wait_recv())
        ctx_rows[...] = dot_t(big, ctx_own[...]).astype(BF16)
        ctx_mine[place(dp, SENT, 32), :] = ctx_rows[place(dp, SENT, 32), :]
        each(1, ND, lambda r: r_copy(r).start())

    def weight_part():
        each(1, ND, lambda r: r_copy(r).wait_recv())
        for n in range(HF // LANES):
            turn = dot_t(ident, ctx_mine[:, n * LANES : (n + 1) * LANES]).astype(BF16)
            term = dot(turn, grad[...])
            at = pl.ds(n * LANES, LANES)
            pair_out[0, at, :] = term[:, :wide].astype(BF16)
            pair_out[1, at, :] = term[:, wide:].astype(BF16)
        each(0, ND, lambda r: p_copy(r).start())

    def pair_up(r):
        at = place(lax.rem(dp + r, ND), HD, 16)
        p_copy(r).wait_recv()
        pair[at, :] = (pair_out[core, at, :].astype(F32) + pair_in[at, :].astype(F32)).astype(BF16)

    def weight_lanes():
        pair_up(1)

        def step(r):
            pair_up(r)
            l_copy(r - 1).start()

        each(2, ND, step)
        pair_up(0)
        l_copy(ND - 1).start()

    def backward(j):
        @pl.when(j > 0)
        def _():
            cross(j - 1)

        rows = place(chip_at(j), PAIR, PAIR)
        values = vrow[rows, :]
        for i in range(CHUNKS):
            cols = pl.ds(i * CHUNK, CHUNK)
            dp_part = dot(values, doT[:, cols])
            ds[:, cols] = (ps[rows, cols].astype(F32) * (dp_part - stat[1:2, cols])).astype(BF16)
        dv = dot(ps[rows, :], don[...])
        dk = dot(ds[...], qn[...])
        dqa[...] += dot(kT[0:HD, rows], ds[...])
        part[0, :, rows] = dot_t(small, (dk * SCALE).astype(BF16)).astype(BF16)
        part[1, :, rows] = dot_t(small, dv.astype(BF16)).astype(BF16)

        @pl.when(j > 1)
        def _():
            hand_out(j - 2)

        @pl.when(j > 0)
        def _():
            add_up(j - 1)

        pl.when(j == 0)(turn_context)
        pl.when(j == 2)(weight_part)
        pl.when(j == 3)(weight_lanes)

    each(0, PAIRS, backward)
    cross(PAIRS - 1)
    hand_out(PAIRS - 2)
    dqT[...] = (dqa[...] * (stat[0:1, :] * SCALE)).astype(BF16)
    add_up(PAIRS - 1)
    each(1, NB, lambda r: dq_copy(r).start())
    own_dq = pltpu.make_async_copy(dqT.at[:, place(blk, HALF, HALF)], dq_own.at[mine_at], local.at[6])
    own_dq.start()
    kv_copy(sibling).start()
    own_dkv = pltpu.make_async_copy(
        summed.at[:, :, place(blk, HALF, HALF)], dkv_own.at[:, mine_at[0], mine_at[1]], local.at[7]
    )
    own_dkv.start()

    total = pair[place(dp, HD, 16), :].astype(F32)
    for r in range(1, ND):
        l_copy(r).wait_recv()
        total = total + lanes_in[r].astype(F32)
    total = total.astype(BF16)
    for i in range(wide // LANES):
        turned[pl.ds(i * LANES, LANES), :] = dot_t(ident, total[:, i * LANES : (i + 1) * LANES]).astype(BF16)

    def b_send(i):
        @pl.when(NB // 2 * core + i != blk)
        def _():
            b_copy(i).start()

    each(0, NB // 2, b_send)
    source_core = blk // (NB // 2)

    @pl.when(source_core == core)
    def _():
        blocks_in[pl.ds(head, 1)] = turned[place(lax.rem(blk, NB // 2), HD, 16), :][None]

    own_dkv.wait()

    def kv_arrived(r):
        kv_copy(lax.rem(blk + r, NB)).wait_recv()

    each(1, NB, kv_arrived)
    k_out[...] = dot_t(big, dkv_own[0]).astype(BF16)
    v_out[...] = dot_t(big, dkv_own[1]).astype(BF16)
    own_dq.wait()
    each(1, NB, lambda r: dq_copy(r).wait_recv())
    q_out[...] = dot_t(big, dq_own[...]).astype(BF16)

    def b_recv(i):
        @pl.when(2 * i + source_core != blk)
        def _():
            b_wait(i).wait_recv()

    each(0, NB // 2, b_recv)
    whole = jnp.zeros((HD, HD), F32)
    for i in range(NB // 2):
        whole = whole + blocks_in[i].astype(F32)
    w_out[...] = whole

    def b_sent(i):
        @pl.when(NB // 2 * core + i != blk)
        def _():
            b_copy(i).wait_send()

    each(0, NB // 2, b_sent)

    def sent(r):
        for copy in (page_copy, k_copy, v_copy, q_copy, dt_copy, c_copy, dq_copy):
            copy(r).wait_send()
        kv_copy(lax.rem(blk + r, NB)).wait_send()

    each(1, NB, sent)

    def sent_over(r):
        kk_copy(r).wait_send()
        vv_copy(r).wait_send()
        x_copy(r).wait_send()

    each(0, NB, sent_over)
    each(0, ND, lambda r: p_copy(r).wait_send())

    def sent_dp(r):
        for copy in (code_copy, do_copy, r_copy, l_copy):
            copy(r).wait_send()

    each(1, ND, sent_dp)


def layer(q, k, v, w, llm, code, page_own):
    dma = pltpu.SemaphoreType.DMA
    wide = w.shape[1] // 2
    nb, nd = [dma((NB,))] * 2, [dma((ND,))] * 2
    return pl.pallas_call(
        layer_kernel,
        out_shape=[jax.ShapeDtypeStruct((TOK, HF), BF16)] * 3 + [jax.ShapeDtypeStruct((HD, HD), F32)],
        in_specs=[pl.BlockSpec(memory_space=VM)] * 7,
        out_specs=[pl.BlockSpec(memory_space=VM)] * 4,
        scratch_shapes=[
            VM((3, HF, TOK), BF16), VM((HF, TOK), BF16), VM((ND, PORTION, LANES), jnp.int32),
            VM((TOK, HF), BF16), VM((TOK, HF), BF16), VM((TOK, w.shape[1]), BF16),
            VM((HD, QUERIES), BF16), VM((DEEP, SEQ), BF16), VM((HD, SEQ), BF16), VM((HD, QUERIES), BF16),
            VM((NB, QUERIES), BF16), VM((SEQ, DEEP), BF16), VM((SEQ, HD), BF16),
            VM((SEQ, CHUNK), F32), VM((SEQ, CHUNK), F32), VM((SEQ, QUERIES), BF16), VM((PAIR, QUERIES), BF16),
            VM((QUERIES, HD), BF16), VM((QUERIES, HD), BF16), VM((8, QUERIES), F32), VM((HD, QUERIES), F32),
            VM((HD, QUERIES), BF16), VM((HD, QUERIES), BF16),
            VM((2, HD, SEQ), BF16), VM((2, HD, QUERIES), BF16), VM((2, HD, QUERIES), BF16),
            VM((HF, TOK), BF16), VM((TOK, HF), BF16), VM((TOK, HF), BF16), VM((HF, TOK), BF16),
            VM((2, HF, TOK), BF16),
            VM((2, HF, wide), BF16), VM((HF, wide), BF16), VM((HF, wide), BF16), VM((ND, HD, wide), BF16),
            VM((wide, HD), BF16), VM((NB // 2, HD, HD), BF16),
            *nd, *nb, *nb, *nb, *nb, *nd, *nb, *nb, *nb,
            *nb, *nb, *nb, *nb, *nd, *nd, *nd, *nd, dma((8,)),
        ],
        compiler_params=pltpu.CompilerParams(
            collective_id=0, has_side_effects=True, vmem_limit_bytes=60 * 2**20
        ),
    )(q, k, v, w, llm, code, page_own)


def body(saved_query, saved_key, saved_value, out_weight, llm_grad, row_source, page_start, page_size):
    blk = lax.axis_index("blk")
    rows = llm_grad.shape[0]
    holder = (blk * ND + jnp.arange(ND, dtype=jnp.int32)) * rows
    code = row_source[0].reshape(ND, PORTION) - holder[:, None]
    code = jnp.broadcast_to(code[:, :, None], (ND, PORTION, LANES))
    first = (jnp.arange(NB, dtype=jnp.int32) == page_start[0, 0]).astype(BF16)
    page_own = jnp.broadcast_to(first[:, None], (NB, HALF))
    query_grad, key_grad, value_grad, weight_grad = layer(
        saved_query[0], saved_key[0], saved_value[0], out_weight, llm_grad, code, page_own
    )
    return (query_grad[None], key_grad[None], value_grad[None], weight_grad)


def solution(mesh):
    in_specs = (
        P("dp", "blk", None),
        P("dp", "blk", None),
        P("dp", "blk", None),
        P(),
        P(("blk", "dp"), None),
        P("dp", "blk"),
        P("dp", "blk"),
        P("dp", "blk"),
    )
    out_specs = (P("dp", "blk", None), P("dp", "blk", None), P("dp", "blk", None), P("blk", "dp"))
    return jax.shard_map(body, mesh=mesh, in_specs=in_specs, out_specs=out_specs, check_vma=False)
```

```python
import math

import jax
import jax.numpy as jnp
from jax import lax
from jax.experimental import pallas as pl
from jax.experimental.pallas import tpu as pltpu
from jax.sharding import PartitionSpec as P

HEADS = 8
HD = 80
MERGE = 4
TOK = 256
HF = HEADS * HD
NB = 16
ND = 8
NY = 4
NX = 4
PORTION = TOK // MERGE // ND
SENT = TOK // ND
LANES = 128
HALF = TOK // 2
SEQ = NB * TOK
QUERIES = SEQ // 2
CHUNK = 256
CHUNKS = QUERIES // CHUNK
TILE = 512
PAIR = 2 * TOK
PAIRS = SEQ // PAIR
DEEP = HD + NB
SCALE = 1.0 / math.sqrt(HD)
EXP2 = SCALE / math.log(2.0)
F32, BF16 = jnp.float32, jnp.bfloat16
FAR = -1e30
VM = pltpu.VMEM


def eye(n):
    return (lax.broadcasted_iota(jnp.int32, (n, n), 0) == lax.broadcasted_iota(jnp.int32, (n, n), 1)).astype(BF16)


def dot(a, b):
    return lax.dot_general(a, b, (((1,), (0,)), ((), ())), preferred_element_type=F32)


def dot_t(a, b):
    return lax.dot_general(a, b, (((1,), (1,)), ((), ())), preferred_element_type=F32)


def each(low, high, act):
    def step(r, _):
        act(r)
        return 0

    lax.fori_loop(low, high, step, 0)


def place(index, size, align):
    return pl.ds(pl.multiple_of(index * size, align), size)


def remote(src, dst, send, recv, where):
    return pltpu.make_async_remote_copy(
        src_ref=src, dst_ref=dst, send_sem=send, recv_sem=recv, device_id=where
    )


def layer_kernel(
    q_hbm, k_hbm, v_hbm, w_hbm, llm_hbm, sources_hbm, first_block,
    dq_own, dkv_own, blocks_in,
    q, k, v, w, llm, sources,
    own, do_own, codes, do_rows, do_mine, grad, grad_mine, grad_far, code_own, page_own, pages,
    qT, kT, vT, doT, page, krow, vrow, sa, sb, ps, ds, don, qn, stat, dqa, ctxT, dqT,
    part, partner, summed, ctx_own,
    ctx_far, pair, lanes_in, lane_sum, lane_out, z_in, turned,
    code_s, code_r, page_s, page_r, q_s, q_r, k_s, k_r, v_s, v_r, do_s, do_r, dt_s, dt_r, kk_s, kk_r, vv_s, vv_r,
    c_s, c_r, dq_s, dq_r, x_s, x_r, kv_s, kv_r, r_s, r_r, l_s, l_r, b_s, b_r, one_s, one_r, local, load,
):
    blk, dp = lax.axis_index("blk"), lax.axis_index("dp")
    core = lax.rem(blk, 2)
    sibling = blk + 1 - 2 * core
    head = blk // 2
    width = w.shape[1]
    wide = width // 2
    z_hi, y = dp // NY, lax.rem(dp, NY)
    z_lo, x_at = head // NX, lax.rem(head, NX)

    arguments = ((k_hbm, k), (v_hbm, v), (q_hbm, q), (llm_hbm, llm), (w_hbm, w), (sources_hbm, sources))
    loads = [pltpu.make_async_copy(src, dst, load.at[n]) for n, (src, dst) in enumerate(arguments)]
    for copy in loads:
        copy.start()

    barrier = pltpu.get_barrier_semaphore()
    each(1, ND, lambda r: pl.semaphore_signal(barrier, inc=1, device_id={"dp": lax.rem(dp + r, ND)}))
    each(1, NB, lambda r: pl.semaphore_signal(barrier, inc=1, device_id={"blk": lax.rem(blk + r, NB)}))
    ident = eye(LANES)
    big = eye(TOK)
    small = eye(HD)
    for n, x in enumerate((k, v, q)):
        loads[n].wait()
        for i in range(HF // LANES):
            own[n, pl.ds(i * LANES, LANES), :] = dot_t(ident, x[:, i * LANES : (i + 1) * LANES]).astype(BF16)
    loads[5].wait()
    code_own[...] = jnp.concatenate([sources[...], sources[...]], axis=1)
    codes[pl.ds(dp, 1)] = code_own[...][None]
    page_own[...] = jnp.broadcast_to(first_block[...].astype(F32), (1, LANES))
    pages[pl.ds(blk, 1)] = page_own[...][None]
    pl.semaphore_wait(barrier, NB + ND - 2)

    def towards(r):
        return lax.rem(blk + r, NB)

    def piece(n, to):
        return own.at[n, place(to // 2, HD, 16), place(lax.rem(to, 2), HALF, HALF)]

    def code_copy(r):
        to = lax.rem(dp + r, ND)
        return remote(code_own, codes.at[dp], code_s.at[r], code_r.at[r], {"dp": to})

    def page_copy(r):
        return remote(page_own, pages.at[blk], page_s.at[r], page_r.at[r], {"blk": towards(r)})

    def key_lanes(block, side):
        return pl.ds(pl.multiple_of(block * TOK + side * HALF, HALF), HALF)

    def k_copy(r):
        to = towards(r)
        dst = kT.at[pl.ds(0, HD), key_lanes(blk, lax.rem(to, 2))]
        return remote(piece(0, to), dst, k_s.at[r], k_r.at[r], {"blk": to})

    def v_copy(r):
        to = towards(r)
        return remote(piece(1, to), vT.at[:, key_lanes(blk, lax.rem(to, 2))], v_s.at[r], v_r.at[r], {"blk": to})

    def q_copy(r):
        to = towards(r)
        return remote(piece(2, to), qT.at[:, place(blk, HALF, HALF)], q_s.at[r], q_r.at[r], {"blk": to})

    def kk_copy(r):
        half = kT.at[pl.ds(0, HD), key_lanes(lax.rem(blk + NB - r, NB), core)]
        return remote(half, half, kk_s.at[r], kk_r.at[r], {"blk": sibling})

    def vv_copy(r):
        half = vT.at[:, key_lanes(lax.rem(blk + NB - r, NB), core)]
        return remote(half, half, vv_s.at[r], vv_r.at[r], {"blk": sibling})

    def do_copy(r):
        to = lax.rem(dp + r, ND)
        return remote(
            do_rows.at[place(to, SENT, 32), :], do_mine.at[place(dp, SENT, 32), :], do_s.at[r], do_r.at[r], {"dp": to}
        )

    def dt_copy(r):
        to = towards(r)
        src = do_own.at[place(to // 2, HD, 16), place(lax.rem(to, 2), HALF, HALF)]
        return remote(src, doT.at[:, place(blk, HALF, HALF)], dt_s.at[r], dt_r.at[r], {"blk": to})

    mine_at = (place(head, HD, 16), place(core, HALF, HALF))

    def c_copy(r):
        to = towards(r)
        return remote(ctxT.at[:, place(to, HALF, HALF)], ctx_own.at[mine_at], c_s.at[r], c_r.at[r], {"blk": to})

    def dq_copy(r):
        to = towards(r)
        return remote(dqT.at[:, place(to, HALF, HALF)], dq_own.at[mine_at], dq_s.at[r], dq_r.at[r], {"blk": to})

    def x_copy(block):
        lanes = key_lanes(block, 1 - core)
        return remote(
            part.at[:, :, lanes], partner.at[:, :, place(block, HALF, HALF)], x_s.at[block], x_r.at[block],
            {"blk": sibling},
        )

    def kv_copy(block):
        r = lax.rem(block + NB - blk, NB)
        return remote(
            summed.at[:, :, place(block, HALF, HALF)], dkv_own.at[:, mine_at[0], mine_at[1]],
            kv_s.at[r], kv_r.at[r], {"blk": block},
        )

    def g_copy(r):
        to = lax.rem(dp + r, ND)
        return remote(
            grad.at[place(to, SENT, 32), :], grad_mine.at[place(dp, SENT, 32), :], r_s.at[r], r_r.at[r], {"dp": to}
        )

    def grad_copy():
        src = grad_mine.at[:, pl.ds(pl.multiple_of((1 - core) * wide, LANES), wide)]
        return remote(src, grad_far, one_s.at[0], one_r.at[0], {"blk": sibling})

    def ctx_copy():
        return remote(ctx_own, ctx_far, one_s.at[2], one_r.at[2], {"blk": sibling})

    def l_copy(r):
        to = lax.rem(y + r, NY)
        return remote(
            pair.at[:, place(to, HD, 16), :], lanes_in.at[r], l_s.at[r], l_r.at[r], {"dp": z_hi * NY + to}
        )

    def z_copy():
        return remote(lane_out, z_in, one_s.at[1], one_r.at[1], {"dp": (1 - z_hi) * NY + y})

    def b_copy(i):
        return remote(
            turned.at[place(i, HD, 16), :], blocks_in.at[head], b_s.at[i], b_r.at[head], {"blk": NB // 2 * core + i}
        )

    def b_wait(i):
        return remote(turned.at[place(i, HD, 16), :], blocks_in.at[i], b_s.at[i], b_r.at[i], {"blk": sibling})

    each(1, ND, lambda r: code_copy(r).start())

    def send_keys(r):
        page_copy(r).start()
        k_copy(r).start()

    each(1, NB, send_keys)
    each(1, NB, lambda r: v_copy(r).start())
    mine = [
        pltpu.make_async_copy(piece(0, blk), kT.at[pl.ds(0, HD), key_lanes(blk, core)], local.at[0]),
        pltpu.make_async_copy(piece(1, blk), vT.at[:, key_lanes(blk, core)], local.at[1]),
        pltpu.make_async_copy(piece(2, blk), qT.at[:, place(blk, HALF, HALF)], local.at[2]),
    ]
    for copy in mine:
        copy.start()
    for copy in mine:
        copy.wait()
    kk_copy(0).start()
    vv_copy(0).start()

    loads[3].wait()
    loads[4].wait()
    each(1, ND, lambda r: code_copy(r).wait_recv())
    asked = jnp.broadcast_to(codes[...].astype(F32), (ND, PORTION, LANES)).reshape(ND * PORTION, LANES)
    spot = dp * PORTION + lax.rem(lax.broadcasted_iota(jnp.int32, asked.shape, 0), PORTION)
    asked = jnp.where(lax.broadcasted_iota(jnp.int32, asked.shape, 1) == spot, asked, 0.0)
    base = ((blk * ND + dp) * llm.shape[0]).astype(F32)
    asked = jnp.broadcast_to(jnp.sum(asked, axis=1, keepdims=True) - base, asked.shape).astype(BF16)
    tok = lax.broadcasted_iota(jnp.int32, (TOK, ND * PORTION), 0)
    spread = (tok // MERGE == lax.broadcasted_iota(jnp.int32, (TOK, ND * PORTION), 1)).astype(BF16)
    row = dot(spread, asked)
    lane = lax.broadcasted_iota(jnp.int32, (TOK, LANES), 1).astype(F32)
    turn_of = lax.rem(lax.broadcasted_iota(jnp.int32, (TOK, LANES), 0), MERGE)
    rows = jnp.zeros((TOK, width), F32)
    for m in range(MERGE):
        hot = jnp.where((row == lane) & (turn_of == m), 1.0, 0.0).astype(BF16)
        rows = rows + dot(hot[:, : llm.shape[0]], llm[:, m * width : (m + 1) * width])
    rows = rows.astype(BF16)
    grad[...] = rows
    do_rows[...] = dot_t(rows, w[...]).astype(BF16)
    each(1, ND, lambda r: do_copy(r).start())
    do_mine[place(dp, SENT, 32), :] = do_rows[place(dp, SENT, 32), :]

    def send_query(n):
        to = 2 * (NX * lax.rem(z_lo + n // (2 * NX), 2) + lax.rem(x_at + n // 2, NX)) + lax.rem(core + n, 2)
        q_copy(lax.rem(to + NB - blk, NB)).start()

    each(1, NB, send_query)

    def relay_key(r):
        k_copy(r).wait_recv()
        kk_copy(r).start()
        page_copy(r).wait_recv()

    def key_block(r):
        block = lax.rem(sibling + NB - r, NB)
        cols = place(block, TOK, TOK)
        mark = (lax.broadcasted_iota(jnp.int32, (NB, LANES), 0).astype(F32) == pages[block]).astype(BF16)
        page[:, place(block, HALF, HALF)] = mark
        kT[HD:DEEP, key_lanes(block, 0)] = mark
        kT[HD:DEEP, key_lanes(block, 1)] = mark
        krow[cols, :] = dot_t(big, kT[:, cols]).astype(BF16)

    def relay_value(r):
        v_copy(r).wait_recv()
        vv_copy(r).start()

    def key_blocks(first):
        each(first, first + 4, lambda r: kk_copy(r).wait_recv())
        for n in range(4):
            key_block(first + n)

    each(1, 5, relay_key)
    each(5, 9, relay_key)
    key_blocks(1)
    each(9, 13, relay_key)
    key_blocks(5)
    each(13, NB, relay_key)
    key_blocks(9)
    each(1, 3, relay_value)
    each(13, NB, lambda r: kk_copy(r).wait_recv())
    kk_copy(0).wait_recv()
    for n in (13, 14, 15, 0):
        key_block(n)


    def chunk_at(i):
        return NX * lax.rem(z_lo + i // NX, 2) + lax.rem(x_at + CHUNKS - i, NX)

    def wait_q(i):
        for e in (0, 1):
            r = lax.rem(blk + NB - 2 * chunk_at(i) - e, NB)

            @pl.when(r != 0)
            def _():
                q_copy(r).wait_recv()

    def query(i):
        cols = place(chunk_at(i), CHUNK, CHUNK)
        far = (1.0 - page[:, cols].astype(F32)) * FAR
        return jnp.concatenate([qT[:, cols], far.astype(BF16)], axis=0)

    def mix(cur, now, nxt, then, top):
        qx = query(then)
        cols = place(chunk_at(now), CHUNK, CHUNK)
        new = jnp.full((8, CHUNK), -3e38, F32)
        total = jnp.zeros((8, CHUNK), F32)
        out = jnp.zeros((HD, CHUNK), F32)
        for j in range(SEQ // TILE):
            rows = pl.ds(j * TILE, TILE)
            s = dot(krow[rows, :], qx)
            nxt[rows, :] = s
            new = jnp.maximum(new, jnp.max(s.reshape(TILE // 8, 8, CHUNK), axis=0))
            if cur is not None:
                p = jnp.exp2(cur[rows, :] * EXP2 - top)
                total = total + jnp.sum(p.reshape(TILE // 8, 8, CHUNK), axis=0)
                p = p.astype(BF16)
                ps[rows, cols] = p
                out = out + dot(vT[:, rows], p)
        if cur is not None:
            for e in (0, 1):
                at = place(2 * now + e, TOK, TOK)
                vrow[at, :] = dot_t(big, vT[:, at]).astype(BF16)
            inv = 1.0 / jnp.sum(total, axis=0, keepdims=True)
            ctxT[:, cols] = (out * inv).astype(BF16)
            stat[0:1, cols] = inv
        return jnp.max(new, axis=0, keepdims=True) * EXP2

    def send_context(i):
        for e in (0, 1):
            r = lax.rem(2 * chunk_at(i) + e + NB - blk, NB)

            @pl.when(r != 0)
            def _():
                c_copy(r).start()

    each(3, NB, relay_value)
    wait_q(0)
    top = mix(None, 0, sa, 0, None)

    each(0, NB, lambda r: vv_copy(r).wait_recv())

    def forward(i, top):
        wait_q(2 * i + 1)
        top = mix(sa, 2 * i, sb, 2 * i + 1, top)

        @pl.when(i > 0)
        def _():
            send_context(2 * i - 1)

        @pl.when(i < CHUNKS // 2 - 1)
        def _():
            wait_q(2 * i + 2)

        top = mix(sb, 2 * i + 1, sa, lax.rem(2 * i + 2, CHUNKS), top)
        send_context(2 * i)

        @pl.when(i == 0)
        def _():
            each(1, ND, lambda r: do_copy(r).wait_recv())
            for n in range(HF // LANES):
                lanes = slice(n * LANES, (n + 1) * LANES)
                do_own[pl.ds(n * LANES, LANES), :] = dot_t(ident, do_mine[:, lanes]).astype(BF16)
            each(1, NB, lambda r: dt_copy(r).start())
            pltpu.make_async_copy(
                do_own.at[mine_at], doT.at[:, place(blk, HALF, HALF)], local.at[4]
            ).start()
        @pl.when(i == 1)
        def _():
            each(1, ND, lambda r: g_copy(r).start())
            grad_mine[place(dp, SENT, 32), :] = grad[place(dp, SENT, 32), :]

        return top

    lax.fori_loop(0, CHUNKS // 2, forward, top)
    send_context(CHUNKS - 1)
    own_context = pltpu.make_async_copy(ctxT.at[:, place(blk, HALF, HALF)], ctx_own.at[mine_at], local.at[5])
    own_context.start()
    pltpu.make_async_copy(do_own.at[mine_at], doT.at[:, place(blk, HALF, HALF)], local.at[4]).wait()
    each(1, NB, lambda r: dt_copy(r).wait_recv())

    def middle(i):
        cols = place(i, CHUNK, CHUNK)
        inv = stat[0:1, cols]
        dof = doT[:, cols].astype(F32)
        stat[1:2, cols] = jnp.sum(dof * ctxT[:, cols].astype(F32), axis=0, keepdims=True)
        don[cols, :] = dot_t(big, (dof * inv).astype(BF16)).astype(BF16)
        qn[cols, :] = dot_t(big, (qT[:, cols].astype(F32) * inv).astype(BF16)).astype(BF16)
        dqa[:, cols] = jnp.zeros((HD, CHUNK), F32)

    each(0, CHUNKS, middle)

    def chip_at(j):
        return lax.rem(head + 1 + j, PAIRS)

    def cross(j):
        for e in (0, 1):
            x_copy(2 * chip_at(j) + e).start()

    def add_up(j):
        for e in (0, 1):
            block = 2 * chip_at(j) + e
            x_copy(block).wait_recv()
            at = place(block, HALF, HALF)
            summed[:, :, at] = (
                part[:, :, key_lanes(block, core)].astype(F32) + partner[:, :, at].astype(F32)
            ).astype(BF16)

    def hand_out(j):
        for e in (0, 1):
            kv_copy(2 * chip_at(j) + e).start()

    def pass_context():
        own_context.wait()
        each(1, NB, lambda r: c_copy(r).wait_recv())
        ctx_copy().start()
        each(1, ND, lambda r: g_copy(r).wait_recv())
        grad_copy().start()

    def weight_part():
        ctx_copy().wait_recv()
        grad_copy().wait_recv()
        near = grad_mine[:, pl.ds(pl.multiple_of(core * wide, LANES), wide)]
        for n in range(HF // LANES):
            at = pl.ds(n * LANES, LANES)
            term = dot(ctx_own[at, :], near) + dot(ctx_far[at, :], grad_far[...])
            for g in (0, LANES // 2):
                at = n * LANES + g
                pair[at // (HF // 2), pl.ds(at % (HF // 2), LANES // 2), :] = term[g : g + LANES // 2].astype(BF16)

    def weight_lanes():
        each(1, NY, lambda r: l_copy(r).start())

    def weight_deep():
        total = pair[:, place(y, HD, 16), :].astype(F32)
        for r in range(1, NY):
            l_copy(r).wait_recv()
            total = total + lanes_in[r].astype(F32)
        far = jnp.where(z_hi == 0, total[1], total[0])
        lane_out[...] = far.astype(BF16)
        lane_sum[...] = jnp.where(z_hi == 0, total[0], total[1])

    def weight_far():
        z_copy().start()

    def backward(j):
        @pl.when(j > 0)
        def _():
            cross(j - 1)

        pl.when(j == 3)(weight_lanes)
        pl.when(j == PAIRS - 1)(weight_far)
        rows = place(chip_at(j), PAIR, PAIR)
        values = vrow[rows, :]
        for i in range(CHUNKS):
            cols = pl.ds(i * CHUNK, CHUNK)
            dp_part = dot(values, doT[:, cols])
            ds[:, cols] = (ps[rows, cols].astype(F32) * (dp_part - stat[1:2, cols])).astype(BF16)
        dv = dot(ps[rows, :], don[...])
        dk = dot(ds[...], qn[...])
        dqa[...] += dot(kT[0:HD, rows], ds[...])
        part[0, :, rows] = dot_t(small, (dk * SCALE).astype(BF16)).astype(BF16)
        part[1, :, rows] = dot_t(small, dv.astype(BF16)).astype(BF16)

        @pl.when(j > 1)
        def _():
            hand_out(j - 2)

        @pl.when(j > 0)
        def _():
            add_up(j - 1)

        pl.when(j == 1)(pass_context)
        pl.when(j == 2)(weight_part)

        pl.when(j == PAIRS - 2)(weight_deep)

    each(0, PAIRS, backward)
    cross(PAIRS - 1)
    hand_out(PAIRS - 2)
    dqT[...] = (dqa[...] * (stat[0:1, :] * SCALE)).astype(BF16)
    add_up(PAIRS - 1)
    each(1, NB, lambda r: dq_copy(r).start())
    own_dq = pltpu.make_async_copy(dqT.at[:, place(blk, HALF, HALF)], dq_own.at[mine_at], local.at[6])
    own_dq.start()
    kv_copy(sibling).start()
    own_dkv = pltpu.make_async_copy(
        summed.at[:, :, place(blk, HALF, HALF)], dkv_own.at[:, mine_at[0], mine_at[1]], local.at[7]
    )
    own_dkv.start()

    z_copy().wait_recv()
    total = (lane_sum[...] + z_in[...].astype(F32)).astype(BF16)
    for i in range(wide // LANES):
        turned[pl.ds(i * LANES, LANES), :] = dot_t(ident, total[:, i * LANES : (i + 1) * LANES]).astype(BF16)

    def b_send(i):
        @pl.when(NB // 2 * core + i != blk)
        def _():
            b_copy(i).start()

    each(0, NB // 2, b_send)
    source_core = blk // (NB // 2)

    @pl.when(source_core == core)
    def _():
        blocks_in[pl.ds(head, 1)] = turned[place(lax.rem(blk, NB // 2), HD, 16), :][None]

    own_dkv.wait()

    def kv_arrived(r):
        kv_copy(lax.rem(blk + r, NB)).wait_recv()

    each(1, NB, kv_arrived)
    own_dq.wait()
    each(1, NB, lambda r: dq_copy(r).wait_recv())

    def b_recv(i):
        @pl.when(2 * i + source_core != blk)
        def _():
            b_wait(i).wait_recv()

    each(0, NB // 2, b_recv)
    def b_sent(i):
        @pl.when(NB // 2 * core + i != blk)
        def _():
            b_copy(i).wait_send()

    each(0, NB // 2, b_sent)

    def sent(r):
        for copy in (page_copy, k_copy, v_copy, q_copy, dt_copy, c_copy, dq_copy):
            copy(r).wait_send()
        kv_copy(lax.rem(blk + r, NB)).wait_send()

    each(1, NB, sent)

    def sent_over(r):
        kk_copy(r).wait_send()
        vv_copy(r).wait_send()
        x_copy(r).wait_send()

    each(0, NB, sent_over)
    each(1, NY, lambda r: l_copy(r).wait_send())
    grad_copy().wait_send()
    ctx_copy().wait_send()
    z_copy().wait_send()

    def sent_dp(r):
        for copy in (code_copy, do_copy, g_copy):
            copy(r).wait_send()

    each(1, ND, sent_dp)


def finish_kernel(dq, dkv, blocks, q_out, k_out, v_out, w_out):
    big = eye(TOK)
    q_out[...] = dot_t(big, dq[...]).astype(BF16)
    k_out[...] = dot_t(big, dkv[0]).astype(BF16)
    v_out[...] = dot_t(big, dkv[1]).astype(BF16)
    whole = blocks[0].astype(F32)
    for i in range(1, NB // 2):
        whole = whole + blocks[i].astype(F32)
    w_out[...] = whole


def finish(dq, dkv, blocks):
    return pl.pallas_call(
        finish_kernel,
        out_shape=[jax.ShapeDtypeStruct((TOK, HF), BF16)] * 3 + [jax.ShapeDtypeStruct((HD, HD), F32)],
        in_specs=[pl.BlockSpec(memory_space=VM)] * 3,
        out_specs=[pl.BlockSpec(memory_space=VM)] * 4,
        compiler_params=pltpu.CompilerParams(vmem_limit_bytes=8 * 2**20),
    )(dq, dkv, blocks)


def layer(q, k, v, w, llm, sources, first_block):
    dma = pltpu.SemaphoreType.DMA
    wide = w.shape[1] // 2
    nb, nd = [dma((NB,))] * 2, [dma((ND,))] * 2
    return pl.pallas_call(
        layer_kernel,
        out_shape=[
            jax.ShapeDtypeStruct((HF, TOK), BF16),
            jax.ShapeDtypeStruct((2, HF, TOK), BF16),
            jax.ShapeDtypeStruct((NB // 2, HD, HD), BF16),
        ],
        in_specs=[pl.BlockSpec(memory_space=pltpu.HBM)] * 6 + [pl.BlockSpec(memory_space=VM)],
        out_specs=[pl.BlockSpec(memory_space=VM)] * 3,
        scratch_shapes=[
            VM(q.shape, BF16), VM(k.shape, BF16), VM(v.shape, BF16), VM(w.shape, BF16), VM(llm.shape, BF16),
            VM(sources.shape, jnp.int32),
            VM((3, HF, TOK), BF16), VM((HF, TOK), BF16), VM((ND, 1, LANES), jnp.int32),
            VM((TOK, HF), BF16), VM((TOK, HF), BF16), VM((TOK, w.shape[1]), BF16), VM((TOK, w.shape[1]), BF16),
            VM((TOK, wide), BF16),
            VM((1, LANES), jnp.int32), VM((1, LANES), F32), VM((NB, 1, LANES), F32),
            VM((HD, QUERIES), BF16), VM((DEEP, SEQ), BF16), VM((HD, SEQ), BF16), VM((HD, QUERIES), BF16),
            VM((NB, QUERIES), BF16), VM((SEQ, DEEP), BF16), VM((SEQ, HD), BF16),
            VM((SEQ, CHUNK), F32), VM((SEQ, CHUNK), F32), VM((SEQ, QUERIES), BF16), VM((PAIR, QUERIES), BF16),
            VM((QUERIES, HD), BF16), VM((QUERIES, HD), BF16), VM((8, QUERIES), F32), VM((HD, QUERIES), F32),
            VM((HD, QUERIES), BF16), VM((HD, QUERIES), BF16),
            VM((2, HD, SEQ), BF16), VM((2, HD, QUERIES), BF16), VM((2, HD, QUERIES), BF16),
            VM((HF, TOK), BF16),
            VM((HF, TOK), BF16), VM((2, HF // 2, wide), BF16), VM((NY, 2, HD, wide), BF16),
            VM((HD, wide), F32), VM((HD, wide), BF16), VM((HD, wide), BF16), VM((wide, HD), BF16),
            *nd, *nb, *nb, *nb, *nb, *nd, *nb, *nb, *nb,
            *nb, *nb, *nb, *nb, *nd, *nd, *nd, dma((3,)), dma((3,)), dma((8,)), dma((6,)),
        ],
        compiler_params=pltpu.CompilerParams(
            collective_id=0, has_side_effects=True, vmem_limit_bytes=48 * 2**20
        ),
    )(q, k, v, w, llm, sources, first_block)


def body(saved_query, saved_key, saved_value, out_weight, llm_grad, row_source, page_start, page_size):
    stay = [
        pltpu.with_memory_space_constraint(x, pltpu.HBM)
        for x in (saved_query[0], saved_key[0], saved_value[0], out_weight, llm_grad, row_source)
    ]
    turned = layer(*stay, page_start)
    query_grad, key_grad, value_grad, weight_grad = finish(*turned)
    return (query_grad[None], key_grad[None], value_grad[None], weight_grad)


def solution(mesh):
    in_specs = (
        P("dp", "blk", None),
        P("dp", "blk", None),
        P("dp", "blk", None),
        P(),
        P(("blk", "dp"), None),
        P("dp", "blk"),
        P("dp", "blk"),
        P("dp", "blk"),
    )
    out_specs = (P("dp", "blk", None), P("dp", "blk", None), P("dp", "blk", None), P("blk", "dp"))
    return jax.shard_map(body, mesh=mesh, in_specs=in_specs, out_specs=out_specs, check_vma=False)
```

```python
import math

import jax
import jax.numpy as jnp
from jax import lax
from jax.experimental import pallas as pl
from jax.experimental.pallas import tpu as pltpu
from jax.sharding import PartitionSpec as P

HEADS = 8
HD = 80
MERGE = 4
TOK = 256
HF = HEADS * HD
NB = 16
ND = 8
NY = 4
NX = 4
YFIRST = 384
PORTION = TOK // MERGE // ND
SENT = TOK // ND
LANES = 128
HALF = TOK // 2
SEQ = NB * TOK
QUERIES = SEQ // 2
CHUNK = 256
CHUNKS = QUERIES // CHUNK
TILE = 512
PAIR = 2 * TOK
PAIRS = SEQ // PAIR
DEEP = HD + NB
SCALE = 1.0 / math.sqrt(HD)
EXP2 = SCALE / math.log(2.0)
F32, BF16 = jnp.float32, jnp.bfloat16
FAR = -1e30
VM = pltpu.VMEM


def eye(n):
    return (lax.broadcasted_iota(jnp.int32, (n, n), 0) == lax.broadcasted_iota(jnp.int32, (n, n), 1)).astype(BF16)


def dot(a, b):
    return lax.dot_general(a, b, (((1,), (0,)), ((), ())), preferred_element_type=F32)


def dot_t(a, b):
    return lax.dot_general(a, b, (((1,), (1,)), ((), ())), preferred_element_type=F32)


def each(low, high, act):
    def step(r, _):
        act(r)
        return 0

    lax.fori_loop(low, high, step, 0)


def place(index, size, align):
    return pl.ds(pl.multiple_of(index * size, align), size)


def remote(src, dst, send, recv, where):
    return pltpu.make_async_remote_copy(
        src_ref=src, dst_ref=dst, send_sem=send, recv_sem=recv, device_id=where
    )


def layer_kernel(
    q_hbm, k_hbm, v_hbm, w_hbm, llm_hbm, sources_hbm, first_block,
    dq_own, dkv_own, blocks_in,
    q, k, v, w, llm, sources,
    own, do_own, codes, do_rows, do_mine, grad, grad_mine, grad_far, code_own, page_own, pages,
    qT, kT, vT, doT, page, krow, vrow, sa, sb, ps, ds, don, qn, stat, dqa, ctxT, dqT,
    part, partner, summed, ctx_own,
    ctx_far, pair, lanes_in, lane_sum, lane_out, z_in, deep_in, deep, last_in, turned,
    code_s, code_r, page_s, page_r, q_s, q_r, k_s, k_r, v_s, v_r, do_s, do_r, dt_s, dt_r, kk_s, kk_r, vv_s, vv_r,
    c_s, c_r, dq_s, dq_r, x_s, x_r, kv_s, kv_r, r_s, r_r, l_s, l_r, n_s, n_r, b_s, b_r, one_s, one_r, local, load,
):
    blk, dp = lax.axis_index("blk"), lax.axis_index("dp")
    core = lax.rem(blk, 2)
    sibling = blk + 1 - 2 * core
    head = blk // 2
    width = w.shape[1]
    wide = width // 2
    z_hi, y = dp // NY, lax.rem(dp, NY)
    z_lo, x_at = head // NX, lax.rem(head, NX)

    arguments = ((k_hbm, k), (v_hbm, v), (q_hbm, q), (llm_hbm, llm), (w_hbm, w), (sources_hbm, sources))
    loads = [pltpu.make_async_copy(src, dst, load.at[n]) for n, (src, dst) in enumerate(arguments)]
    for copy in loads:
        copy.start()

    barrier = pltpu.get_barrier_semaphore()
    each(1, ND, lambda r: pl.semaphore_signal(barrier, inc=1, device_id={"dp": lax.rem(dp + r, ND)}))
    each(1, NB, lambda r: pl.semaphore_signal(barrier, inc=1, device_id={"blk": lax.rem(blk + r, NB)}))
    ident = eye(LANES)
    big = eye(TOK)
    small = eye(HD)
    for n, x in enumerate((k, v, q)):
        loads[n].wait()
        for i in range(HF // LANES):
            own[n, pl.ds(i * LANES, LANES), :] = dot_t(ident, x[:, i * LANES : (i + 1) * LANES]).astype(BF16)
    loads[5].wait()
    code_own[...] = jnp.concatenate([sources[...], sources[...]], axis=1)
    codes[pl.ds(dp, 1)] = code_own[...][None]
    page_own[...] = jnp.broadcast_to(first_block[...].astype(F32), (1, LANES))
    pages[pl.ds(blk, 1)] = page_own[...][None]
    pl.semaphore_wait(barrier, NB + ND - 2)

    def towards(r):
        return lax.rem(blk + r, NB)

    def piece(n, to):
        return own.at[n, place(to // 2, HD, 16), place(lax.rem(to, 2), HALF, HALF)]

    def code_copy(r):
        to = lax.rem(dp + r, ND)
        return remote(code_own, codes.at[dp], code_s.at[r], code_r.at[r], {"dp": to})

    def page_copy(r):
        return remote(page_own, pages.at[blk], page_s.at[r], page_r.at[r], {"blk": towards(r)})

    def key_lanes(block, side):
        return pl.ds(pl.multiple_of(block * TOK + side * HALF, HALF), HALF)

    def k_copy(r):
        to = towards(r)
        dst = kT.at[pl.ds(0, HD), key_lanes(blk, lax.rem(to, 2))]
        return remote(piece(0, to), dst, k_s.at[r], k_r.at[r], {"blk": to})

    def v_copy(r):
        to = towards(r)
        return remote(piece(1, to), vT.at[:, key_lanes(blk, lax.rem(to, 2))], v_s.at[r], v_r.at[r], {"blk": to})

    def q_copy(r):
        to = towards(r)
        return remote(piece(2, to), qT.at[:, place(blk, HALF, HALF)], q_s.at[r], q_r.at[r], {"blk": to})

    def kk_copy(r):
        half = kT.at[pl.ds(0, HD), key_lanes(lax.rem(blk + NB - r, NB), core)]
        return remote(half, half, kk_s.at[r], kk_r.at[r], {"blk": sibling})

    def vv_copy(r):
        half = vT.at[:, key_lanes(lax.rem(blk + NB - r, NB), core)]
        return remote(half, half, vv_s.at[r], vv_r.at[r], {"blk": sibling})

    def do_copy(r):
        to = lax.rem(dp + r, ND)
        return remote(
            do_rows.at[place(to, SENT, 32), :], do_mine.at[place(dp, SENT, 32), :], do_s.at[r], do_r.at[r], {"dp": to}
        )

    def dt_copy(r):
        to = towards(r)
        src = do_own.at[place(to // 2, HD, 16), place(lax.rem(to, 2), HALF, HALF)]
        return remote(src, doT.at[:, place(blk, HALF, HALF)], dt_s.at[r], dt_r.at[r], {"blk": to})

    mine_at = (place(head, HD, 16), place(core, HALF, HALF))

    def c_copy(r):
        to = towards(r)
        return remote(ctxT.at[:, place(to, HALF, HALF)], ctx_own.at[mine_at], c_s.at[r], c_r.at[r], {"blk": to})

    def dq_copy(r):
        to = towards(r)
        return remote(dqT.at[:, place(to, HALF, HALF)], dq_own.at[mine_at], dq_s.at[r], dq_r.at[r], {"blk": to})

    def x_copy(block):
        lanes = key_lanes(block, 1 - core)
        return remote(
            part.at[:, :, lanes], partner.at[:, :, place(block, HALF, HALF)], x_s.at[block], x_r.at[block],
            {"blk": sibling},
        )

    def kv_copy(block):
        r = lax.rem(block + NB - blk, NB)
        return remote(
            summed.at[:, :, place(block, HALF, HALF)], dkv_own.at[:, mine_at[0], mine_at[1]],
            kv_s.at[r], kv_r.at[r], {"blk": block},
        )

    def g_copy(r):
        to = lax.rem(dp + r, ND)
        return remote(
            grad.at[place(to, SENT, 32), :], grad_mine.at[place(dp, SENT, 32), :], r_s.at[r], r_r.at[r], {"dp": to}
        )

    def grad_copy():
        src = grad_mine.at[:, pl.ds(pl.multiple_of((1 - core) * wide, LANES), wide)]
        return remote(src, grad_far, one_s.at[0], one_r.at[0], {"blk": sibling})

    def ctx_copy():
        return remote(ctx_own, ctx_far, one_s.at[2], one_r.at[2], {"blk": sibling})

    def l_copy(r):
        to = lax.rem(y + r, NY)
        src = pair.at[:, place(to, HD, 16), pl.ds(0, YFIRST)]
        return remote(src, lanes_in.at[r], l_s.at[r], l_r.at[r], {"dp": z_hi * NY + to})

    def z_copy():
        return remote(lane_out, z_in, one_s.at[1], one_r.at[1], {"dp": (1 - z_hi) * NY + y})

    def m_copy():
        src = pair.at[1 - z_hi, :, pl.ds(YFIRST, wide - YFIRST)]
        return remote(src, deep_in, one_s.at[3], one_r.at[3], {"dp": (1 - z_hi) * NY + y})

    def n_copy(r):
        to = lax.rem(y + r, NY)
        return remote(deep.at[place(to, HD, 16), :], last_in.at[r], n_s.at[r], n_r.at[r], {"dp": z_hi * NY + to})

    def b_copy(i):
        return remote(
            turned.at[place(i, HD, 16), :], blocks_in.at[head], b_s.at[i], b_r.at[head], {"blk": NB // 2 * core + i}
        )

    def b_wait(i):
        return remote(turned.at[place(i, HD, 16), :], blocks_in.at[i], b_s.at[i], b_r.at[i], {"blk": sibling})

    each(1, ND, lambda r: code_copy(r).start())

    def send_keys(r):
        page_copy(r).start()
        k_copy(r).start()

    each(1, NB, send_keys)
    each(1, NB, lambda r: v_copy(r).start())
    mine = [
        pltpu.make_async_copy(piece(0, blk), kT.at[pl.ds(0, HD), key_lanes(blk, core)], local.at[0]),
        pltpu.make_async_copy(piece(1, blk), vT.at[:, key_lanes(blk, core)], local.at[1]),
        pltpu.make_async_copy(piece(2, blk), qT.at[:, place(blk, HALF, HALF)], local.at[2]),
    ]
    for copy in mine:
        copy.start()
    for copy in mine:
        copy.wait()
    kk_copy(0).start()
    vv_copy(0).start()

    loads[3].wait()
    loads[4].wait()
    each(1, ND, lambda r: code_copy(r).wait_recv())
    asked = jnp.broadcast_to(codes[...].astype(F32), (ND, PORTION, LANES)).reshape(ND * PORTION, LANES)
    spot = dp * PORTION + lax.rem(lax.broadcasted_iota(jnp.int32, asked.shape, 0), PORTION)
    asked = jnp.where(lax.broadcasted_iota(jnp.int32, asked.shape, 1) == spot, asked, 0.0)
    base = ((blk * ND + dp) * llm.shape[0]).astype(F32)
    asked = jnp.broadcast_to(jnp.sum(asked, axis=1, keepdims=True) - base, asked.shape).astype(BF16)
    tok = lax.broadcasted_iota(jnp.int32, (TOK, ND * PORTION), 0)
    spread = (tok // MERGE == lax.broadcasted_iota(jnp.int32, (TOK, ND * PORTION), 1)).astype(BF16)
    row = dot(spread, asked)
    lane = lax.broadcasted_iota(jnp.int32, (TOK, LANES), 1).astype(F32)
    turn_of = lax.rem(lax.broadcasted_iota(jnp.int32, (TOK, LANES), 0), MERGE)
    rows = jnp.zeros((TOK, width), F32)
    for m in range(MERGE):
        hot = jnp.where((row == lane) & (turn_of == m), 1.0, 0.0).astype(BF16)
        rows = rows + dot(hot[:, : llm.shape[0]], llm[:, m * width : (m + 1) * width])
    rows = rows.astype(BF16)
    grad[...] = rows
    do_rows[...] = dot_t(rows, w[...]).astype(BF16)
    each(1, ND, lambda r: do_copy(r).start())
    do_mine[place(dp, SENT, 32), :] = do_rows[place(dp, SENT, 32), :]

    def send_query(n):
        to = 2 * (NX * lax.rem(z_lo + n // (2 * NX), 2) + lax.rem(x_at + n // 2, NX)) + lax.rem(core + n, 2)
        q_copy(lax.rem(to + NB - blk, NB)).start()

    each(1, NB, send_query)

    def relay_key(r):
        k_copy(r).wait_recv()
        kk_copy(r).start()
        page_copy(r).wait_recv()

    def key_block(r):
        block = lax.rem(sibling + NB - r, NB)
        cols = place(block, TOK, TOK)
        mark = (lax.broadcasted_iota(jnp.int32, (NB, LANES), 0).astype(F32) == pages[block]).astype(BF16)
        page[:, place(block, HALF, HALF)] = mark
        kT[HD:DEEP, key_lanes(block, 0)] = mark
        kT[HD:DEEP, key_lanes(block, 1)] = mark
        krow[cols, :] = dot_t(big, kT[:, cols]).astype(BF16)

    def relay_value(r):
        v_copy(r).wait_recv()
        vv_copy(r).start()

    each(1, NB, relay_key)
    each(1, 5, relay_value)
    each(0, NB, lambda r: kk_copy(r).wait_recv())
    for n in range(NB):
        key_block(n)


    def chunk_at(i):
        return NX * lax.rem(z_lo + i // NX, 2) + lax.rem(x_at + CHUNKS - i, NX)

    def wait_q(i):
        for e in (0, 1):
            r = lax.rem(blk + NB - 2 * chunk_at(i) - e, NB)

            @pl.when(r != 0)
            def _():
                q_copy(r).wait_recv()

    def query(i):
        cols = place(chunk_at(i), CHUNK, CHUNK)
        far = (1.0 - page[:, cols].astype(F32)) * FAR
        return jnp.concatenate([qT[:, cols], far.astype(BF16)], axis=0)

    def mix(cur, now, nxt, then, top):
        qx = query(then)
        cols = place(chunk_at(now), CHUNK, CHUNK)
        new = jnp.full((8, CHUNK), -3e38, F32)
        total = jnp.zeros((8, CHUNK), F32)
        out = jnp.zeros((HD, CHUNK), F32)
        for j in range(SEQ // TILE):
            rows = pl.ds(j * TILE, TILE)
            s = dot(krow[rows, :], qx)
            nxt[rows, :] = s
            new = jnp.maximum(new, jnp.max(s.reshape(TILE // 8, 8, CHUNK), axis=0))
            if cur is not None:
                p = jnp.exp2(cur[rows, :] * EXP2 - top)
                total = total + jnp.sum(p.reshape(TILE // 8, 8, CHUNK), axis=0)
                p = p.astype(BF16)
                ps[rows, cols] = p
                out = out + dot(vT[:, rows], p)
        if cur is not None:
            for e in (0, 1):
                at = place(2 * now + e, TOK, TOK)
                vrow[at, :] = dot_t(big, vT[:, at]).astype(BF16)
            inv = 1.0 / jnp.sum(total, axis=0, keepdims=True)
            ctxT[:, cols] = (out * inv).astype(BF16)
            stat[0:1, cols] = inv
        return jnp.max(new, axis=0, keepdims=True) * EXP2

    def send_context(i):
        for e in (0, 1):
            r = lax.rem(2 * chunk_at(i) + e + NB - blk, NB)

            @pl.when(r != 0)
            def _():
                c_copy(r).start()

    each(5, NB, relay_value)
    wait_q(0)
    top = mix(None, 0, sa, 0, None)

    each(0, NB, lambda r: vv_copy(r).wait_recv())

    def forward(i, top):
        wait_q(2 * i + 1)
        top = mix(sa, 2 * i, sb, 2 * i + 1, top)

        @pl.when(i > 0)
        def _():
            send_context(2 * i - 1)

        @pl.when(i < CHUNKS // 2 - 1)
        def _():
            wait_q(2 * i + 2)

        top = mix(sb, 2 * i + 1, sa, lax.rem(2 * i + 2, CHUNKS), top)
        send_context(2 * i)

        @pl.when(i == 0)
        def _():
            each(1, ND, lambda r: do_copy(r).wait_recv())
            for n in range(HF // LANES):
                lanes = slice(n * LANES, (n + 1) * LANES)
                do_own[pl.ds(n * LANES, LANES), :] = dot_t(ident, do_mine[:, lanes]).astype(BF16)
            each(1, NB, lambda r: dt_copy(r).start())
            pltpu.make_async_copy(
                do_own.at[mine_at], doT.at[:, place(blk, HALF, HALF)], local.at[4]
            ).start()
        @pl.when(i == 1)
        def _():
            each(1, ND, lambda r: g_copy(r).start())
            grad_mine[place(dp, SENT, 32), :] = grad[place(dp, SENT, 32), :]

        return top

    lax.fori_loop(0, CHUNKS // 2, forward, top)
    send_context(CHUNKS - 1)
    own_context = pltpu.make_async_copy(ctxT.at[:, place(blk, HALF, HALF)], ctx_own.at[mine_at], local.at[5])
    own_context.start()
    pltpu.make_async_copy(do_own.at[mine_at], doT.at[:, place(blk, HALF, HALF)], local.at[4]).wait()
    each(1, NB, lambda r: dt_copy(r).wait_recv())

    def middle(i):
        cols = place(i, CHUNK, CHUNK)
        inv = stat[0:1, cols]
        dof = doT[:, cols].astype(F32)
        stat[1:2, cols] = jnp.sum(dof * ctxT[:, cols].astype(F32), axis=0, keepdims=True)
        don[cols, :] = dot_t(big, (dof * inv).astype(BF16)).astype(BF16)
        qn[cols, :] = dot_t(big, (qT[:, cols].astype(F32) * inv).astype(BF16)).astype(BF16)
        dqa[:, cols] = jnp.zeros((HD, CHUNK), F32)

    for i in range(CHUNKS):
        middle(i)

    def chip_at(j):
        return lax.rem(head + 1 + j, PAIRS)

    def cross(j):
        for e in (0, 1):
            x_copy(2 * chip_at(j) + e).start()

    def add_up(j):
        for e in (0, 1):
            block = 2 * chip_at(j) + e
            x_copy(block).wait_recv()
            at = place(block, HALF, HALF)
            summed[:, :, at] = (
                part[:, :, key_lanes(block, core)].astype(F32) + partner[:, :, at].astype(F32)
            ).astype(BF16)

    def hand_out(j):
        for e in (0, 1):
            kv_copy(2 * chip_at(j) + e).start()

    def pass_context():
        own_context.wait()
        each(1, NB, lambda r: c_copy(r).wait_recv())
        ctx_copy().start()
        each(1, ND, lambda r: g_copy(r).wait_recv())
        grad_copy().start()

    def weight_part():
        ctx_copy().wait_recv()
        grad_copy().wait_recv()
        near = grad_mine[:, pl.ds(pl.multiple_of(core * wide, LANES), wide)]
        for n in range(HF // LANES):
            at = pl.ds(n * LANES, LANES)
            term = dot(ctx_own[at, :], near) + dot(ctx_far[at, :], grad_far[...])
            for g in (0, LANES // 2):
                at = n * LANES + g
                pair[at // (HF // 2), pl.ds(at % (HF // 2), LANES // 2), :] = term[g : g + LANES // 2].astype(BF16)

    def weight_lanes():
        m_copy().start()
        each(1, NY, lambda r: l_copy(r).start())

    def weight_deep():
        m_copy().wait_recv()
        deep[...] = (pair[z_hi, :, YFIRST:].astype(F32) + deep_in[...].astype(F32)).astype(BF16)
        total = pair[:, place(y, HD, 16), :YFIRST].astype(F32)
        for r in range(1, NY):
            l_copy(r).wait_recv()
            total = total + lanes_in[r].astype(F32)
        far = jnp.where(z_hi == 0, total[1], total[0])
        lane_out[...] = far.astype(BF16)
        lane_sum[...] = jnp.where(z_hi == 0, total[0], total[1])

    def weight_far():
        z_copy().start()
        each(1, NY, lambda r: n_copy(r).start())

    def backward(j):
        @pl.when(j > 0)
        def _():
            cross(j - 1)

        pl.when(j == 3)(weight_lanes)
        pl.when(j == PAIRS - 1)(weight_far)
        rows = place(chip_at(j), PAIR, PAIR)
        values = vrow[rows, :]
        for i in range(CHUNKS):
            cols = pl.ds(i * CHUNK, CHUNK)
            dp_part = dot(values, doT[:, cols])
            ds[:, cols] = (ps[rows, cols].astype(F32) * (dp_part - stat[1:2, cols])).astype(BF16)
        dv = dot(ps[rows, :], don[...])
        dk = dot(ds[...], qn[...])
        dqa[...] += dot(kT[0:HD, rows], ds[...])
        part[0, :, rows] = dot_t(small, (dk * SCALE).astype(BF16)).astype(BF16)
        part[1, :, rows] = dot_t(small, dv.astype(BF16)).astype(BF16)

        @pl.when(j > 1)
        def _():
            hand_out(j - 2)

        @pl.when(j > 0)
        def _():
            add_up(j - 1)

        pl.when(j == 1)(pass_context)
        pl.when(j == 2)(weight_part)

        pl.when(j == PAIRS - 2)(weight_deep)

    each(0, PAIRS, backward)
    cross(PAIRS - 1)
    hand_out(PAIRS - 2)
    dqT[...] = (dqa[...] * (stat[0:1, :] * SCALE)).astype(BF16)
    add_up(PAIRS - 1)
    each(1, NB, lambda r: dq_copy(r).start())
    own_dq = pltpu.make_async_copy(dqT.at[:, place(blk, HALF, HALF)], dq_own.at[mine_at], local.at[6])
    own_dq.start()
    kv_copy(sibling).start()
    own_dkv = pltpu.make_async_copy(
        summed.at[:, :, place(blk, HALF, HALF)], dkv_own.at[:, mine_at[0], mine_at[1]], local.at[7]
    )
    own_dkv.start()

    z_copy().wait_recv()
    rest = deep[place(y, HD, 16), :].astype(F32)
    for r in range(1, NY):
        n_copy(r).wait_recv()
        rest = rest + last_in[r].astype(F32)
    total = jnp.concatenate([lane_sum[...] + z_in[...].astype(F32), rest], axis=1).astype(BF16)
    for i in range(wide // LANES):
        turned[pl.ds(i * LANES, LANES), :] = dot_t(ident, total[:, i * LANES : (i + 1) * LANES]).astype(BF16)

    def b_send(i):
        @pl.when(NB // 2 * core + i != blk)
        def _():
            b_copy(i).start()

    each(0, NB // 2, b_send)
    source_core = blk // (NB // 2)

    @pl.when(source_core == core)
    def _():
        blocks_in[pl.ds(head, 1)] = turned[place(lax.rem(blk, NB // 2), HD, 16), :][None]

    own_dkv.wait()

    def kv_arrived(r):
        kv_copy(lax.rem(blk + r, NB)).wait_recv()

    each(1, NB, kv_arrived)
    own_dq.wait()
    each(1, NB, lambda r: dq_copy(r).wait_recv())

    def b_recv(i):
        @pl.when(2 * i + source_core != blk)
        def _():
            b_wait(i).wait_recv()

    each(0, NB // 2, b_recv)
    def b_sent(i):
        @pl.when(NB // 2 * core + i != blk)
        def _():
            b_copy(i).wait_send()

    each(0, NB // 2, b_sent)

    def sent(r):
        for copy in (page_copy, k_copy, v_copy, q_copy, dt_copy, c_copy, dq_copy):
            copy(r).wait_send()
        kv_copy(lax.rem(blk + r, NB)).wait_send()

    each(1, NB, sent)

    def sent_over(r):
        kk_copy(r).wait_send()
        vv_copy(r).wait_send()
        x_copy(r).wait_send()

    each(0, NB, sent_over)
    each(1, NY, lambda r: l_copy(r).wait_send())
    each(1, NY, lambda r: n_copy(r).wait_send())
    m_copy().wait_send()
    grad_copy().wait_send()
    ctx_copy().wait_send()
    z_copy().wait_send()

    def sent_dp(r):
        for copy in (code_copy, do_copy, g_copy):
            copy(r).wait_send()

    each(1, ND, sent_dp)


def finish_kernel(dq, dkv, blocks, q_out, k_out, v_out, w_out):
    big = eye(TOK)
    q_out[...] = dot_t(big, dq[...]).astype(BF16)
    k_out[...] = dot_t(big, dkv[0]).astype(BF16)
    v_out[...] = dot_t(big, dkv[1]).astype(BF16)
    whole = blocks[0].astype(F32)
    for i in range(1, NB // 2):
        whole = whole + blocks[i].astype(F32)
    w_out[...] = whole


def finish(dq, dkv, blocks):
    return pl.pallas_call(
        finish_kernel,
        out_shape=[jax.ShapeDtypeStruct((TOK, HF), BF16)] * 3 + [jax.ShapeDtypeStruct((HD, HD), F32)],
        in_specs=[pl.BlockSpec(memory_space=VM)] * 3,
        out_specs=[pl.BlockSpec(memory_space=VM)] * 4,
        compiler_params=pltpu.CompilerParams(vmem_limit_bytes=8 * 2**20),
    )(dq, dkv, blocks)


def layer(q, k, v, w, llm, sources, first_block):
    dma = pltpu.SemaphoreType.DMA
    wide = w.shape[1] // 2
    nb, nd = [dma((NB,))] * 2, [dma((ND,))] * 2
    return pl.pallas_call(
        layer_kernel,
        out_shape=[
            jax.ShapeDtypeStruct((HF, TOK), BF16),
            jax.ShapeDtypeStruct((2, HF, TOK), BF16),
            jax.ShapeDtypeStruct((NB // 2, HD, HD), BF16),
        ],
        in_specs=[pl.BlockSpec(memory_space=pltpu.HBM)] * 6 + [pl.BlockSpec(memory_space=VM)],
        out_specs=[pl.BlockSpec(memory_space=VM)] * 3,
        scratch_shapes=[
            VM(q.shape, BF16), VM(k.shape, BF16), VM(v.shape, BF16), VM(w.shape, BF16), VM(llm.shape, BF16),
            VM(sources.shape, jnp.int32),
            VM((3, HF, TOK), BF16), VM((HF, TOK), BF16), VM((ND, 1, LANES), jnp.int32),
            VM((TOK, HF), BF16), VM((TOK, HF), BF16), VM((TOK, w.shape[1]), BF16), VM((TOK, w.shape[1]), BF16),
            VM((TOK, wide), BF16),
            VM((1, LANES), jnp.int32), VM((1, LANES), F32), VM((NB, 1, LANES), F32),
            VM((HD, QUERIES), BF16), VM((DEEP, SEQ), BF16), VM((HD, SEQ), BF16), VM((HD, QUERIES), BF16),
            VM((NB, QUERIES), BF16), VM((SEQ, DEEP), BF16), VM((SEQ, HD), BF16),
            VM((SEQ, CHUNK), F32), VM((SEQ, CHUNK), F32), VM((SEQ, QUERIES), BF16), VM((PAIR, QUERIES), BF16),
            VM((QUERIES, HD), BF16), VM((QUERIES, HD), BF16), VM((8, QUERIES), F32), VM((HD, QUERIES), F32),
            VM((HD, QUERIES), BF16), VM((HD, QUERIES), BF16),
            VM((2, HD, SEQ), BF16), VM((2, HD, QUERIES), BF16), VM((2, HD, QUERIES), BF16),
            VM((HF, TOK), BF16),
            VM((HF, TOK), BF16), VM((2, HF // 2, wide), BF16), VM((NY, 2, HD, YFIRST), BF16),
            VM((HD, YFIRST), F32), VM((HD, YFIRST), BF16), VM((HD, YFIRST), BF16),
            VM((HF // 2, wide - YFIRST), BF16), VM((HF // 2, wide - YFIRST), BF16), VM((NY, HD, wide - YFIRST), BF16),
            VM((wide, HD), BF16),
            *nd, *nb, *nb, *nb, *nb, *nd, *nb, *nb, *nb,
            *nb, *nb, *nb, *nb, *nd, *nd, *nd, *nd, dma((4,)), dma((4,)), dma((8,)), dma((6,)),
        ],
        compiler_params=pltpu.CompilerParams(
            collective_id=0, has_side_effects=True, vmem_limit_bytes=48 * 2**20
        ),
    )(q, k, v, w, llm, sources, first_block)


def body(saved_query, saved_key, saved_value, out_weight, llm_grad, row_source, page_start, page_size):
    stay = [
        pltpu.with_memory_space_constraint(x, pltpu.HBM)
        for x in (saved_query[0], saved_key[0], saved_value[0], out_weight, llm_grad, row_source)
    ]
    turned = layer(*stay, page_start)
    query_grad, key_grad, value_grad, weight_grad = finish(*turned)
    return (query_grad[None], key_grad[None], value_grad[None], weight_grad)


def solution(mesh):
    in_specs = (
        P("dp", "blk", None),
        P("dp", "blk", None),
        P("dp", "blk", None),
        P(),
        P(("blk", "dp"), None),
        P("dp", "blk"),
        P("dp", "blk"),
        P("dp", "blk"),
    )
    out_specs = (P("dp", "blk", None), P("dp", "blk", None), P("dp", "blk", None), P("blk", "dp"))
    return jax.shard_map(body, mesh=mesh, in_specs=in_specs, out_specs=out_specs, check_vma=False)
```

```python
import math

import jax
import jax.numpy as jnp
from jax import lax
from jax.experimental import pallas as pl
from jax.experimental.pallas import tpu as pltpu
from jax.sharding import PartitionSpec as P

HEADS = 8
HD = 80
MERGE = 4
TOK = 256
HF = HEADS * HD
NB = 16
ND = 8
NY = 4
NX = 4
YFIRST = 384
PORTION = TOK // MERGE // ND
SENT = TOK // ND
LANES = 128
HALF = TOK // 2
SEQ = NB * TOK
QUERIES = SEQ // 2
CHUNK = 256
CHUNKS = QUERIES // CHUNK
TILE = 512
PAIR = 2 * TOK
PAIRS = SEQ // PAIR
DEEP = HD + NB
SCALE = 1.0 / math.sqrt(HD)
EXP2 = SCALE / math.log(2.0)
F32, BF16 = jnp.float32, jnp.bfloat16
FAR = -1e30
VM = pltpu.VMEM


def eye(n):
    return (lax.broadcasted_iota(jnp.int32, (n, n), 0) == lax.broadcasted_iota(jnp.int32, (n, n), 1)).astype(BF16)


def dot(a, b):
    return lax.dot_general(a, b, (((1,), (0,)), ((), ())), preferred_element_type=F32)


def dot_t(a, b):
    return lax.dot_general(a, b, (((1,), (1,)), ((), ())), preferred_element_type=F32)


def each(low, high, act):
    def step(r, _):
        act(r)
        return 0

    lax.fori_loop(low, high, step, 0)


def place(index, size, align):
    return pl.ds(pl.multiple_of(index * size, align), size)


def remote(src, dst, send, recv, where):
    return pltpu.make_async_remote_copy(
        src_ref=src, dst_ref=dst, send_sem=send, recv_sem=recv, device_id=where
    )


def layer_kernel(
    q_hbm, k_hbm, v_hbm, w_hbm, llm_hbm, sources_hbm, first_block,
    dq_own, dkv_own, blocks_in,
    q, k, v, w, llm, sources,
    own, do_own, codes, do_rows, do_mine, grad, grad_near, grad_far, ahead, code_own, page_own, pages,
    qT, kT, vT, doT, page, krow, vrow, sa, sb, ps, ds, don, qn, stat, dqa, ctxT, dqT,
    part, partner, summed, ctx_own,
    ctx_far, pair, lanes_in, lane_sum, lane_out, z_in, deep_in, deep, last_in, turned,
    code_s, code_r, page_s, page_r, q_s, q_r, k_s, k_r, v_s, v_r, do_s, do_r, dt_s, dt_r, kk_s, kk_r, vv_s, vv_r,
    c_s, c_r, dq_s, dq_r, x_s, x_r, kv_s, kv_r, r_s, r_r, f_s, f_r, l_s, l_r, n_s, n_r, b_s, b_r, one_s, one_r, local, load,
):
    blk, dp = lax.axis_index("blk"), lax.axis_index("dp")
    core = lax.rem(blk, 2)
    sibling = blk + 1 - 2 * core
    head = blk // 2
    width = w.shape[1]
    wide = width // 2
    z_hi, y = dp // NY, lax.rem(dp, NY)
    z_lo, x_at = head // NX, lax.rem(head, NX)

    arguments = ((k_hbm, k), (v_hbm, v), (q_hbm, q), (w_hbm, w), (sources_hbm, sources))
    loads = [pltpu.make_async_copy(src, dst, load.at[n]) for n, (src, dst) in enumerate(arguments)]
    held = llm_hbm.shape[0]
    for m in range(MERGE):
        src = llm_hbm.at[:, pl.ds(m * w.shape[1], w.shape[1])]
        loads.append(pltpu.make_async_copy(src, llm.at[pl.ds(m * held, held), :], load.at[5 + m]))
    for copy in loads:
        copy.start()

    barrier = pltpu.get_barrier_semaphore()
    each(1, ND, lambda r: pl.semaphore_signal(barrier, inc=1, device_id={"dp": lax.rem(dp + r, ND)}))
    each(
        1, ND,
        lambda r: pl.semaphore_signal(barrier, inc=1, device_id={"blk": sibling, "dp": lax.rem(dp + r, ND)}),
    )
    each(1, NB, lambda r: pl.semaphore_signal(barrier, inc=1, device_id={"blk": lax.rem(blk + r, NB)}))
    ident = eye(LANES)
    big = eye(TOK)
    small = eye(HD)
    for n, x in enumerate((k, v, q)):
        loads[n].wait()
        for i in range(HF // LANES):
            own[n, pl.ds(i * LANES, LANES), :] = dot_t(ident, x[:, i * LANES : (i + 1) * LANES]).astype(BF16)
    loads[4].wait()
    code_own[...] = jnp.concatenate([sources[...], sources[...]], axis=1)
    codes[pl.ds(dp, 1)] = code_own[...][None]
    page_own[...] = jnp.broadcast_to(first_block[...].astype(F32), (1, LANES))
    pages[pl.ds(blk, 1)] = page_own[...][None]
    pl.semaphore_wait(barrier, NB + 2 * ND - 3)

    def towards(r):
        return lax.rem(blk + r, NB)

    def piece(n, to):
        return own.at[n, place(to // 2, HD, 16), place(lax.rem(to, 2), HALF, HALF)]

    def code_copy(r):
        to = lax.rem(dp + r, ND)
        return remote(code_own, codes.at[dp], code_s.at[r], code_r.at[r], {"dp": to})

    def page_copy(r):
        return remote(page_own, pages.at[blk], page_s.at[r], page_r.at[r], {"blk": towards(r)})

    def key_lanes(block, side):
        return pl.ds(pl.multiple_of(block * TOK + side * HALF, HALF), HALF)

    def k_copy(r):
        to = towards(r)
        dst = kT.at[pl.ds(0, HD), key_lanes(blk, lax.rem(to, 2))]
        return remote(piece(0, to), dst, k_s.at[r], k_r.at[r], {"blk": to})

    def v_copy(r):
        to = towards(r)
        return remote(piece(1, to), vT.at[:, key_lanes(blk, lax.rem(to, 2))], v_s.at[r], v_r.at[r], {"blk": to})

    def q_copy(r):
        to = towards(r)
        return remote(piece(2, to), qT.at[:, place(blk, HALF, HALF)], q_s.at[r], q_r.at[r], {"blk": to})

    def kk_copy(r):
        half = kT.at[pl.ds(0, HD), key_lanes(lax.rem(blk + NB - r, NB), core)]
        return remote(half, half, kk_s.at[r], kk_r.at[r], {"blk": sibling})

    def vv_copy(r):
        half = vT.at[:, key_lanes(lax.rem(blk + NB - r, NB), core)]
        return remote(half, half, vv_s.at[r], vv_r.at[r], {"blk": sibling})

    def do_copy(r):
        to = lax.rem(dp + r, ND)
        return remote(
            do_rows.at[place(to, SENT, 32), :], do_mine.at[place(dp, SENT, 32), :], do_s.at[r], do_r.at[r], {"dp": to}
        )

    def dt_copy(r):
        to = towards(r)
        src = do_own.at[place(to // 2, HD, 16), place(lax.rem(to, 2), HALF, HALF)]
        return remote(src, doT.at[:, place(blk, HALF, HALF)], dt_s.at[r], dt_r.at[r], {"blk": to})

    mine_at = (place(head, HD, 16), place(core, HALF, HALF))

    def c_copy(r):
        to = towards(r)
        return remote(ctxT.at[:, place(to, HALF, HALF)], ctx_own.at[mine_at], c_s.at[r], c_r.at[r], {"blk": to})

    def dq_copy(r):
        to = towards(r)
        return remote(dqT.at[:, place(to, HALF, HALF)], dq_own.at[mine_at], dq_s.at[r], dq_r.at[r], {"blk": to})

    def x_copy(block):
        lanes = key_lanes(block, 1 - core)
        return remote(
            part.at[:, :, lanes], partner.at[:, :, place(block, HALF, HALF)], x_s.at[block], x_r.at[block],
            {"blk": sibling},
        )

    def kv_copy(block):
        r = lax.rem(block + NB - blk, NB)
        return remote(
            summed.at[:, :, place(block, HALF, HALF)], dkv_own.at[:, mine_at[0], mine_at[1]],
            kv_s.at[r], kv_r.at[r], {"blk": block},
        )

    def half_of(r, side):
        return grad.at[place(lax.rem(dp + r, ND), SENT, 32), pl.ds(pl.multiple_of(side * wide, LANES), wide)]

    def near_copy(r):
        dst = grad_near.at[place(dp, SENT, 32), :]
        return remote(half_of(r, core), dst, r_s.at[r], r_r.at[r], {"dp": lax.rem(dp + r, ND)})

    def far_copy(r):
        dst = grad_far.at[place(dp, SENT, 32), :]
        to = {"blk": sibling, "dp": lax.rem(dp + r, ND)}
        return remote(half_of(r, 1 - core), dst, f_s.at[r], f_r.at[r], to)

    def ctx_copy():
        return remote(ctx_own, ctx_far, one_s.at[2], one_r.at[2], {"blk": sibling})

    def l_copy(r):
        to = lax.rem(y + r, NY)
        src = pair.at[:, place(to, HD, 16), pl.ds(0, YFIRST)]
        return remote(src, lanes_in.at[r], l_s.at[r], l_r.at[r], {"dp": z_hi * NY + to})

    def z_copy():
        return remote(lane_out, z_in, one_s.at[1], one_r.at[1], {"dp": (1 - z_hi) * NY + y})

    def m_copy():
        src = pair.at[1 - z_hi, :, pl.ds(YFIRST, wide - YFIRST)]
        return remote(src, deep_in, one_s.at[3], one_r.at[3], {"dp": (1 - z_hi) * NY + y})

    def n_copy(r):
        to = lax.rem(y + r, NY)
        return remote(deep.at[place(to, HD, 16), :], last_in.at[r], n_s.at[r], n_r.at[r], {"dp": z_hi * NY + to})

    def b_copy(i):
        return remote(
            turned.at[place(i, HD, 16), :], blocks_in.at[head], b_s.at[i], b_r.at[head], {"blk": NB // 2 * core + i}
        )

    def b_wait(i):
        return remote(turned.at[place(i, HD, 16), :], blocks_in.at[i], b_s.at[i], b_r.at[i], {"blk": sibling})

    each(1, ND, lambda r: code_copy(r).start())

    def send_keys(r):
        page_copy(r).start()
        k_copy(r).start()

    each(1, NB, send_keys)
    each(1, NB, lambda r: v_copy(r).start())
    mine = [
        pltpu.make_async_copy(piece(0, blk), kT.at[pl.ds(0, HD), key_lanes(blk, core)], local.at[0]),
        pltpu.make_async_copy(piece(1, blk), vT.at[:, key_lanes(blk, core)], local.at[1]),
        pltpu.make_async_copy(piece(2, blk), qT.at[:, place(blk, HALF, HALF)], local.at[2]),
    ]
    for copy in mine:
        copy.start()
    for copy in mine:
        copy.wait()
    kk_copy(0).start()
    vv_copy(0).start()

    for copy in (loads[3], *loads[5:]):
        copy.wait()
    ahead[...] = dot_t(llm[...], w[...]).astype(BF16)
    each(1, ND, lambda r: code_copy(r).wait_recv())
    asked = jnp.broadcast_to(codes[...].astype(F32), (ND, PORTION, LANES)).reshape(ND * PORTION, LANES)
    spot = dp * PORTION + lax.rem(lax.broadcasted_iota(jnp.int32, asked.shape, 0), PORTION)
    asked = jnp.where(lax.broadcasted_iota(jnp.int32, asked.shape, 1) == spot, asked, 0.0)
    base = ((blk * ND + dp) * held).astype(F32)
    asked = jnp.broadcast_to(jnp.sum(asked, axis=1, keepdims=True) - base, asked.shape).astype(BF16)
    tok = lax.broadcasted_iota(jnp.int32, (TOK, ND * PORTION), 0)
    spread = (tok // MERGE == lax.broadcasted_iota(jnp.int32, (TOK, ND * PORTION), 1)).astype(BF16)
    row = dot(spread, asked)
    row = jnp.concatenate([row, row], axis=1)
    spot = lax.broadcasted_iota(jnp.int32, row.shape, 1)
    turn_of = lax.rem(lax.broadcasted_iota(jnp.int32, row.shape, 0), MERGE)
    hot = jnp.where((row == lax.rem(spot, held).astype(F32)) & (turn_of == spot // held), 1.0, 0.0).astype(BF16)
    do_rows[...] = dot(hot, ahead[...]).astype(BF16)

    def send_query(n):
        to = 2 * (NX * lax.rem(z_lo + n // (2 * NX), 2) + lax.rem(x_at + n // 2, NX)) + lax.rem(core + n, 2)
        q_copy(lax.rem(to + NB - blk, NB)).start()


    def relay_key(r):
        k_copy(r).wait_recv()
        kk_copy(r).start()
        page_copy(r).wait_recv()

    def key_block(r):
        block = lax.rem(sibling + NB - r, NB)
        cols = place(block, TOK, TOK)
        mark = (lax.broadcasted_iota(jnp.int32, (NB, LANES), 0).astype(F32) == pages[block]).astype(BF16)
        page[:, place(block, HALF, HALF)] = mark
        kT[HD:DEEP, key_lanes(block, 0)] = mark
        kT[HD:DEEP, key_lanes(block, 1)] = mark
        krow[cols, :] = dot_t(big, kT[:, cols]).astype(BF16)

    def relay_value(r):
        v_copy(r).wait_recv()
        vv_copy(r).start()

    each(1, NB // 2, relay_key)
    each(1, ND, lambda r: do_copy(r).start())
    do_mine[place(dp, SENT, 32), :] = do_rows[place(dp, SENT, 32), :]
    each(1, NB, send_query)
    each(NB // 2, NB, relay_key)
    each(0, NB, lambda r: kk_copy(r).wait_recv())
    for n in range(NB):
        key_block(n)


    def chunk_at(i):
        return NX * lax.rem(z_lo + i // NX, 2) + lax.rem(x_at + CHUNKS - i, NX)

    def wait_q(i):
        for e in (0, 1):
            r = lax.rem(blk + NB - 2 * chunk_at(i) - e, NB)

            @pl.when(r != 0)
            def _():
                q_copy(r).wait_recv()

    def query(i):
        cols = place(chunk_at(i), CHUNK, CHUNK)
        far = (1.0 - page[:, cols].astype(F32)) * FAR
        return jnp.concatenate([qT[:, cols], far.astype(BF16)], axis=0)

    def mix(cur, now, nxt, then, top):
        qx = query(then)
        cols = place(chunk_at(now), CHUNK, CHUNK)
        new = jnp.full((8, CHUNK), -3e38, F32)
        total = jnp.zeros((8, CHUNK), F32)
        out = jnp.zeros((HD, CHUNK), F32)
        for j in range(SEQ // TILE):
            rows = pl.ds(j * TILE, TILE)
            s = dot(krow[rows, :], qx)
            nxt[rows, :] = s
            new = jnp.maximum(new, jnp.max(s.reshape(TILE // 8, 8, CHUNK), axis=0))
            if cur is not None:
                p = jnp.exp2(cur[rows, :] * EXP2 - top)
                total = total + jnp.sum(p.reshape(TILE // 8, 8, CHUNK), axis=0)
                p = p.astype(BF16)
                ps[rows, cols] = p
                out = out + dot(vT[:, rows], p)
        if cur is not None:
            for e in (0, 1):
                at = place(2 * now + e, TOK, TOK)
                vrow[at, :] = dot_t(big, vT[:, at]).astype(BF16)
            inv = 1.0 / jnp.sum(total, axis=0, keepdims=True)
            ctxT[:, cols] = (out * inv).astype(BF16)
            stat[0:1, cols] = inv
        return jnp.max(new, axis=0, keepdims=True) * EXP2

    def send_context(i):
        for e in (0, 1):
            r = lax.rem(2 * chunk_at(i) + e + NB - blk, NB)

            @pl.when(r != 0)
            def _():
                c_copy(r).start()

    each(1, NB // 2, relay_value)
    wait_q(0)
    top = mix(None, 0, sa, 0, None)
    each(NB // 2, NB, relay_value)

    grad[...] = dot(hot, llm[...]).astype(BF16)
    each(0, NB, lambda r: vv_copy(r).wait_recv())

    def forward(i, top):
        wait_q(2 * i + 1)
        top = mix(sa, 2 * i, sb, 2 * i + 1, top)

        @pl.when(i > 0)
        def _():
            send_context(2 * i - 1)

        @pl.when(i < CHUNKS // 2 - 1)
        def _():
            wait_q(2 * i + 2)

        top = mix(sb, 2 * i + 1, sa, lax.rem(2 * i + 2, CHUNKS), top)
        send_context(2 * i)

        @pl.when(i == 0)
        def _():
            each(1, ND, lambda r: do_copy(r).wait_recv())
            for n in range(HF // LANES):
                lanes = slice(n * LANES, (n + 1) * LANES)
                do_own[pl.ds(n * LANES, LANES), :] = dot_t(ident, do_mine[:, lanes]).astype(BF16)
            each(1, NB, lambda r: dt_copy(r).start())
            pltpu.make_async_copy(
                do_own.at[mine_at], doT.at[:, place(blk, HALF, HALF)], local.at[4]
            ).start()
        @pl.when(i == 1)
        def _():
            def send_rows(r):
                near_copy(r).start()
                far_copy(r).start()

            each(1, ND, send_rows)
            far_copy(0).start()
            pltpu.make_async_copy(half_of(0, core), grad_near.at[place(dp, SENT, 32), :], local.at[3]).start()

        return top

    lax.fori_loop(0, CHUNKS // 2, forward, top)
    send_context(CHUNKS - 1)
    own_context = pltpu.make_async_copy(ctxT.at[:, place(blk, HALF, HALF)], ctx_own.at[mine_at], local.at[5])
    own_context.start()
    pltpu.make_async_copy(do_own.at[mine_at], doT.at[:, place(blk, HALF, HALF)], local.at[4]).wait()
    each(1, NB, lambda r: dt_copy(r).wait_recv())

    def middle(i):
        cols = place(i, CHUNK, CHUNK)
        inv = stat[0:1, cols]
        dof = doT[:, cols].astype(F32)
        stat[1:2, cols] = jnp.sum(dof * ctxT[:, cols].astype(F32), axis=0, keepdims=True)
        don[cols, :] = dot_t(big, (dof * inv).astype(BF16)).astype(BF16)
        qn[cols, :] = dot_t(big, (qT[:, cols].astype(F32) * inv).astype(BF16)).astype(BF16)
        dqa[:, cols] = jnp.zeros((HD, CHUNK), F32)

    for i in range(CHUNKS):
        middle(i)

    def chip_at(j):
        return lax.rem(head + 1 + j, PAIRS)

    def cross(j):
        for e in (0, 1):
            x_copy(2 * chip_at(j) + e).start()

    def add_up(j):
        for e in (0, 1):
            block = 2 * chip_at(j) + e
            x_copy(block).wait_recv()
            at = place(block, HALF, HALF)
            summed[:, :, at] = (
                part[:, :, key_lanes(block, core)].astype(F32) + partner[:, :, at].astype(F32)
            ).astype(BF16)

    def hand_out(j):
        for e in (0, 1):
            kv_copy(2 * chip_at(j) + e).start()

    def pass_context():
        own_context.wait()
        each(1, NB, lambda r: c_copy(r).wait_recv())
        ctx_copy().start()

    def weight_part():
        ctx_copy().wait_recv()
        pltpu.make_async_copy(half_of(0, core), grad_near.at[place(dp, SENT, 32), :], local.at[3]).wait()
        each(1, ND, lambda r: near_copy(r).wait_recv())
        each(0, ND, lambda r: far_copy(r).wait_recv())
        near = grad_near[...]
        for n in range(HF // LANES):
            at = pl.ds(n * LANES, LANES)
            term = dot(ctx_own[at, :], near) + dot(ctx_far[at, :], grad_far[...])
            for g in (0, LANES // 2):
                at = n * LANES + g
                pair[at // (HF // 2), pl.ds(at % (HF // 2), LANES // 2), :] = term[g : g + LANES // 2].astype(BF16)

    def weight_lanes():
        m_copy().start()
        each(1, NY, lambda r: l_copy(r).start())

    def weight_deep():
        m_copy().wait_recv()
        deep[...] = (pair[z_hi, :, YFIRST:].astype(F32) + deep_in[...].astype(F32)).astype(BF16)
        total = pair[:, place(y, HD, 16), :YFIRST].astype(F32)
        for r in range(1, NY):
            l_copy(r).wait_recv()
            total = total + lanes_in[r].astype(F32)
        far = jnp.where(z_hi == 0, total[1], total[0])
        lane_out[...] = far.astype(BF16)
        lane_sum[...] = jnp.where(z_hi == 0, total[0], total[1])

    def weight_far():
        z_copy().start()
        each(1, NY, lambda r: n_copy(r).start())

    def backward(j):
        @pl.when(j > 0)
        def _():
            cross(j - 1)

        pl.when(j == 3)(weight_lanes)
        pl.when(j == PAIRS - 1)(weight_far)

        rows = place(chip_at(j), PAIR, PAIR)
        values = vrow[rows, :]
        for i in range(CHUNKS):
            cols = pl.ds(i * CHUNK, CHUNK)
            dp_part = dot(values, doT[:, cols])
            ds[:, cols] = (ps[rows, cols].astype(F32) * (dp_part - stat[1:2, cols])).astype(BF16)
        dv = dot(ps[rows, :], don[...])
        dk = dot(ds[...], qn[...])
        dqa[...] += dot(kT[0:HD, rows], ds[...])
        part[0, :, rows] = dot_t(small, (dk * SCALE).astype(BF16)).astype(BF16)
        part[1, :, rows] = dot_t(small, dv.astype(BF16)).astype(BF16)

        @pl.when(j > 1)
        def _():
            hand_out(j - 2)

        @pl.when(j > 0)
        def _():
            add_up(j - 1)

        pl.when(j == 1)(pass_context)
        pl.when(j == 2)(weight_part)
        pl.when(j == PAIRS - 2)(weight_deep)


    each(0, PAIRS, backward)
    cross(PAIRS - 1)
    hand_out(PAIRS - 2)
    dqT[...] = (dqa[...] * (stat[0:1, :] * SCALE)).astype(BF16)
    each(1, NB, lambda r: dq_copy(r).start())
    own_dq = pltpu.make_async_copy(dqT.at[:, place(blk, HALF, HALF)], dq_own.at[mine_at], local.at[6])
    own_dq.start()
    add_up(PAIRS - 1)
    kv_copy(sibling).start()
    own_dkv = pltpu.make_async_copy(
        summed.at[:, :, place(blk, HALF, HALF)], dkv_own.at[:, mine_at[0], mine_at[1]], local.at[7]
    )
    own_dkv.start()

    z_copy().wait_recv()
    rest = deep[place(y, HD, 16), :].astype(F32)
    for r in range(1, NY):
        n_copy(r).wait_recv()
        rest = rest + last_in[r].astype(F32)
    total = jnp.concatenate([lane_sum[...] + z_in[...].astype(F32), rest], axis=1).astype(BF16)
    for i in range(wide // LANES):
        turned[pl.ds(i * LANES, LANES), :] = dot_t(ident, total[:, i * LANES : (i + 1) * LANES]).astype(BF16)

    def b_send(i):
        @pl.when(NB // 2 * core + i != blk)
        def _():
            b_copy(i).start()

    each(0, NB // 2, b_send)
    source_core = blk // (NB // 2)

    @pl.when(source_core == core)
    def _():
        blocks_in[pl.ds(head, 1)] = turned[place(lax.rem(blk, NB // 2), HD, 16), :][None]

    own_dkv.wait()

    def kv_arrived(r):
        kv_copy(lax.rem(blk + r, NB)).wait_recv()

    each(1, NB, kv_arrived)
    own_dq.wait()
    each(1, NB, lambda r: dq_copy(r).wait_recv())

    def b_recv(i):
        @pl.when(2 * i + source_core != blk)
        def _():
            b_wait(i).wait_recv()

    each(0, NB // 2, b_recv)
    def b_sent(i):
        @pl.when(NB // 2 * core + i != blk)
        def _():
            b_copy(i).wait_send()

    each(0, NB // 2, b_sent)

    def sent(r):
        for copy in (page_copy, k_copy, v_copy, q_copy, dt_copy, c_copy, dq_copy):
            copy(r).wait_send()
        kv_copy(lax.rem(blk + r, NB)).wait_send()

    each(1, NB, sent)

    def sent_over(r):
        kk_copy(r).wait_send()
        vv_copy(r).wait_send()
        x_copy(r).wait_send()

    each(0, NB, sent_over)
    each(1, NY, lambda r: l_copy(r).wait_send())
    each(0, ND, lambda r: far_copy(r).wait_send())
    each(1, NY, lambda r: n_copy(r).wait_send())
    m_copy().wait_send()
    ctx_copy().wait_send()
    z_copy().wait_send()

    def sent_dp(r):
        for copy in (code_copy, do_copy, near_copy):
            copy(r).wait_send()

    each(1, ND, sent_dp)


def finish_kernel(dq, dkv, blocks, q_out, k_out, v_out, w_out):
    big = eye(TOK)
    q_out[...] = dot_t(big, dq[...]).astype(BF16)
    k_out[...] = dot_t(big, dkv[0]).astype(BF16)
    v_out[...] = dot_t(big, dkv[1]).astype(BF16)
    whole = blocks[0].astype(F32)
    for i in range(1, NB // 2):
        whole = whole + blocks[i].astype(F32)
    w_out[...] = whole


def finish(dq, dkv, blocks):
    return pl.pallas_call(
        finish_kernel,
        out_shape=[jax.ShapeDtypeStruct((TOK, HF), BF16)] * 3 + [jax.ShapeDtypeStruct((HD, HD), F32)],
        in_specs=[pl.BlockSpec(memory_space=VM)] * 3,
        out_specs=[pl.BlockSpec(memory_space=VM)] * 4,
        compiler_params=pltpu.CompilerParams(vmem_limit_bytes=8 * 2**20),
    )(dq, dkv, blocks)


def layer(q, k, v, w, llm, sources, first_block):
    dma = pltpu.SemaphoreType.DMA
    wide = w.shape[1] // 2
    nb, nd = [dma((NB,))] * 2, [dma((ND,))] * 2
    return pl.pallas_call(
        layer_kernel,
        out_shape=[
            jax.ShapeDtypeStruct((HF, TOK), BF16),
            jax.ShapeDtypeStruct((2, HF, TOK), BF16),
            jax.ShapeDtypeStruct((NB // 2, HD, HD), BF16),
        ],
        in_specs=[pl.BlockSpec(memory_space=pltpu.HBM)] * 6 + [pl.BlockSpec(memory_space=VM)],
        out_specs=[pl.BlockSpec(memory_space=VM)] * 3,
        scratch_shapes=[
            VM(q.shape, BF16), VM(k.shape, BF16), VM(v.shape, BF16), VM(w.shape, BF16), VM((TOK, w.shape[1]), BF16),
            VM(sources.shape, jnp.int32),
            VM((3, HF, TOK), BF16), VM((HF, TOK), BF16), VM((ND, 1, LANES), jnp.int32),
            VM((TOK, HF), BF16), VM((TOK, HF), BF16), VM((TOK, w.shape[1]), BF16), VM((TOK, wide), BF16),
            VM((TOK, wide), BF16), VM((TOK, HF), BF16),
            VM((1, LANES), jnp.int32), VM((1, LANES), F32), VM((NB, 1, LANES), F32),
            VM((HD, QUERIES), BF16), VM((DEEP, SEQ), BF16), VM((HD, SEQ), BF16), VM((HD, QUERIES), BF16),
            VM((NB, QUERIES), BF16), VM((SEQ, DEEP), BF16), VM((SEQ, HD), BF16),
            VM((SEQ, CHUNK), F32), VM((SEQ, CHUNK), F32), VM((SEQ, QUERIES), BF16), VM((PAIR, QUERIES), BF16),
            VM((QUERIES, HD), BF16), VM((QUERIES, HD), BF16), VM((8, QUERIES), F32), VM((HD, QUERIES), F32),
            VM((HD, QUERIES), BF16), VM((HD, QUERIES), BF16),
            VM((2, HD, SEQ), BF16), VM((2, HD, QUERIES), BF16), VM((2, HD, QUERIES), BF16),
            VM((HF, TOK), BF16),
            VM((HF, TOK), BF16), VM((2, HF // 2, wide), BF16), VM((NY, 2, HD, YFIRST), BF16),
            VM((HD, YFIRST), F32), VM((HD, YFIRST), BF16), VM((HD, YFIRST), BF16),
            VM((HF // 2, wide - YFIRST), BF16), VM((HF // 2, wide - YFIRST), BF16), VM((NY, HD, wide - YFIRST), BF16),
            VM((wide, HD), BF16),
            *nd, *nb, *nb, *nb, *nb, *nd, *nb, *nb, *nb,
            *nb, *nb, *nb, *nb, *nd, *nd, *nd, *nd, *nd, dma((4,)), dma((4,)), dma((8,)), dma((5 + MERGE,)),
        ],
        compiler_params=pltpu.CompilerParams(
            collective_id=0, has_side_effects=True, vmem_limit_bytes=48 * 2**20
        ),
    )(q, k, v, w, llm, sources, first_block)


def body(saved_query, saved_key, saved_value, out_weight, llm_grad, row_source, page_start, page_size):
    stay = [
        pltpu.with_memory_space_constraint(x, pltpu.HBM)
        for x in (saved_query[0], saved_key[0], saved_value[0], out_weight, llm_grad, row_source)
    ]
    turned = layer(*stay, page_start)
    query_grad, key_grad, value_grad, weight_grad = finish(*turned)
    return (query_grad[None], key_grad[None], value_grad[None], weight_grad)


def solution(mesh):
    in_specs = (
        P("dp", "blk", None),
        P("dp", "blk", None),
        P("dp", "blk", None),
        P(),
        P(("blk", "dp"), None),
        P("dp", "blk"),
        P("dp", "blk"),
        P("dp", "blk"),
    )
    out_specs = (P("dp", "blk", None), P("dp", "blk", None), P("dp", "blk", None), P("blk", "dp"))
    return jax.shard_map(body, mesh=mesh, in_specs=in_specs, out_specs=out_specs, check_vma=False)
```

```python
import math

import jax
import jax.numpy as jnp
from jax import lax
from jax.experimental import pallas as pl
from jax.experimental.pallas import tpu as pltpu
from jax.sharding import PartitionSpec as P

HEADS = 8
HD = 80
MERGE = 4
TOK = 256
HF = HEADS * HD
NB = 16
ND = 8
NY = 4
NX = 4
YFIRST = 384
PORTION = TOK // MERGE // ND
SENT = TOK // ND
LANES = 128
HALF = TOK // 2
SEQ = NB * TOK
QUERIES = SEQ // 2
CHUNK = 256
CHUNKS = QUERIES // CHUNK
TILE = 512
PAIR = 2 * TOK
PAIRS = SEQ // PAIR
DEEP = HD + NB
SCALE = 1.0 / math.sqrt(HD)
EXP2 = SCALE / math.log(2.0)
F32, BF16 = jnp.float32, jnp.bfloat16
FAR = -1e30
VM = pltpu.VMEM


def eye(n):
    return (lax.broadcasted_iota(jnp.int32, (n, n), 0) == lax.broadcasted_iota(jnp.int32, (n, n), 1)).astype(BF16)


def dot(a, b):
    return lax.dot_general(a, b, (((1,), (0,)), ((), ())), preferred_element_type=F32)


def dot_t(a, b):
    return lax.dot_general(a, b, (((1,), (1,)), ((), ())), preferred_element_type=F32)


def each(low, high, act):
    def step(r, _):
        act(r)
        return 0

    lax.fori_loop(low, high, step, 0)


def place(index, size, align):
    return pl.ds(pl.multiple_of(index * size, align), size)


def remote(src, dst, send, recv, where):
    return pltpu.make_async_remote_copy(
        src_ref=src, dst_ref=dst, send_sem=send, recv_sem=recv, device_id=where
    )


def layer_kernel(
    q_hbm, k_hbm, v_hbm, w_hbm, llm_hbm, sources_hbm, first_block,
    dq_own, dkv_own, blocks_in,
    q, k, v, w, llm, sources,
    own, do_own, codes, do_rows, do_mine, grad, grad_near, grad_far, ahead, code_own, page_own, pages,
    qT, kT, vT, doT, page, krow, vrow, sa, sb, ps, ds, don, qn, stat, dqa, ctxT, dqT,
    part, partner, summed, ctx_own,
    ctx_far, pair, lanes_in, lane_sum, lane_out, z_in, deep_in, deep, last_in, turned,
    code_s, code_r, page_s, page_r, q_s, q_r, k_s, k_r, v_s, v_r, do_s, do_r, dt_s, dt_r, kk_s, kk_r, vv_s, vv_r,
    c_s, c_r, dq_s, dq_r, x_s, x_r, kv_s, kv_r, r_s, r_r, f_s, f_r, l_s, l_r, n_s, n_r, b_s, b_r, one_s, one_r, local, load,
):
    blk, dp = lax.axis_index("blk"), lax.axis_index("dp")
    core = lax.rem(blk, 2)
    sibling = blk + 1 - 2 * core
    head = blk // 2
    width = w.shape[1]
    wide = width // 2
    z_hi, y = dp // NY, lax.rem(dp, NY)
    z_lo, x_at = head // NX, lax.rem(head, NX)

    arguments = ((k_hbm, k), (v_hbm, v), (q_hbm, q), (w_hbm, w), (sources_hbm, sources))
    loads = [pltpu.make_async_copy(src, dst, load.at[n]) for n, (src, dst) in enumerate(arguments)]
    held = llm_hbm.shape[0]
    for m in range(MERGE):
        src = llm_hbm.at[:, pl.ds(m * w.shape[1], w.shape[1])]
        loads.append(pltpu.make_async_copy(src, llm.at[pl.ds(m * held, held), :], load.at[5 + m]))
    for copy in loads:
        copy.start()

    barrier = pltpu.get_barrier_semaphore()
    each(1, ND, lambda r: pl.semaphore_signal(barrier, inc=1, device_id={"dp": lax.rem(dp + r, ND)}))
    each(
        1, ND,
        lambda r: pl.semaphore_signal(barrier, inc=1, device_id={"blk": sibling, "dp": lax.rem(dp + r, ND)}),
    )
    each(1, NB, lambda r: pl.semaphore_signal(barrier, inc=1, device_id={"blk": lax.rem(blk + r, NB)}))
    ident = eye(LANES)
    big = eye(TOK)
    small = eye(HD)
    for n, x in enumerate((k, v, q)):
        loads[n].wait()
        for i in range(HF // LANES):
            own[n, pl.ds(i * LANES, LANES), :] = dot_t(ident, x[:, i * LANES : (i + 1) * LANES]).astype(BF16)
    loads[4].wait()
    code_own[...] = jnp.concatenate([sources[...], sources[...]], axis=1)
    codes[pl.ds(dp, 1)] = code_own[...][None]
    page_own[...] = jnp.broadcast_to(first_block[...].astype(F32), (1, LANES))
    pages[pl.ds(blk, 1)] = page_own[...][None]
    pl.semaphore_wait(barrier, NB + 2 * ND - 3)

    def towards(r):
        return lax.rem(blk + r, NB)

    def piece(n, to):
        return own.at[n, place(to // 2, HD, 16), place(lax.rem(to, 2), HALF, HALF)]

    def code_copy(r):
        to = lax.rem(dp + r, ND)
        return remote(code_own, codes.at[dp], code_s.at[r], code_r.at[r], {"dp": to})

    def page_copy(r):
        return remote(page_own, pages.at[blk], page_s.at[r], page_r.at[r], {"blk": towards(r)})

    def key_lanes(block, side):
        return pl.ds(pl.multiple_of(block * TOK + side * HALF, HALF), HALF)

    def k_copy(r):
        to = towards(r)
        dst = kT.at[pl.ds(0, HD), key_lanes(blk, lax.rem(to, 2))]
        return remote(piece(0, to), dst, k_s.at[r], k_r.at[r], {"blk": to})

    def v_copy(r):
        to = towards(r)
        return remote(piece(1, to), vT.at[:, key_lanes(blk, lax.rem(to, 2))], v_s.at[r], v_r.at[r], {"blk": to})

    def q_copy(r):
        to = towards(r)
        return remote(piece(2, to), qT.at[:, place(blk, HALF, HALF)], q_s.at[r], q_r.at[r], {"blk": to})

    def kk_copy(r):
        half = kT.at[pl.ds(0, HD), key_lanes(lax.rem(blk + NB - r, NB), core)]
        return remote(half, half, kk_s.at[r], kk_r.at[r], {"blk": sibling})

    def vv_copy(r):
        half = vT.at[:, key_lanes(lax.rem(blk + NB - r, NB), core)]
        return remote(half, half, vv_s.at[r], vv_r.at[r], {"blk": sibling})

    def do_copy(r):
        to = lax.rem(dp + r, ND)
        return remote(
            do_rows.at[place(to, SENT, 32), :], do_mine.at[place(dp, SENT, 32), :], do_s.at[r], do_r.at[r], {"dp": to}
        )

    def dt_copy(r):
        to = towards(r)
        src = do_own.at[place(to // 2, HD, 16), place(lax.rem(to, 2), HALF, HALF)]
        return remote(src, doT.at[:, place(blk, HALF, HALF)], dt_s.at[r], dt_r.at[r], {"blk": to})

    mine_at = (place(head, HD, 16), place(core, HALF, HALF))

    def c_copy(r):
        to = towards(r)
        return remote(ctxT.at[:, place(to, HALF, HALF)], ctx_own.at[mine_at], c_s.at[r], c_r.at[r], {"blk": to})

    def dq_copy(r):
        to = towards(r)
        return remote(dqT.at[:, place(to, HALF, HALF)], dq_own.at[mine_at], dq_s.at[r], dq_r.at[r], {"blk": to})

    def x_copy(block):
        lanes = key_lanes(block, 1 - core)
        return remote(
            part.at[:, :, lanes], partner.at[:, :, place(block, HALF, HALF)], x_s.at[block], x_r.at[block],
            {"blk": sibling},
        )

    def kv_copy(block):
        r = lax.rem(block + NB - blk, NB)
        return remote(
            summed.at[:, :, place(block, HALF, HALF)], dkv_own.at[:, mine_at[0], mine_at[1]],
            kv_s.at[r], kv_r.at[r], {"blk": block},
        )

    def half_of(r, side):
        return grad.at[place(lax.rem(dp + r, ND), SENT, 32), pl.ds(pl.multiple_of(side * wide, LANES), wide)]

    def near_copy(r):
        dst = grad_near.at[place(dp, SENT, 32), :]
        return remote(half_of(r, core), dst, r_s.at[r], r_r.at[r], {"dp": lax.rem(dp + r, ND)})

    def far_copy(r):
        dst = grad_far.at[place(dp, SENT, 32), :]
        to = {"blk": sibling, "dp": lax.rem(dp + r, ND)}
        return remote(half_of(r, 1 - core), dst, f_s.at[r], f_r.at[r], to)

    def ctx_copy():
        return remote(ctx_own, ctx_far, one_s.at[2], one_r.at[2], {"blk": sibling})

    def l_copy(r):
        to = lax.rem(y + r, NY)
        src = pair.at[:, place(to, HD, 16), pl.ds(0, YFIRST)]
        return remote(src, lanes_in.at[r], l_s.at[r], l_r.at[r], {"dp": z_hi * NY + to})

    def z_copy():
        return remote(lane_out, z_in, one_s.at[1], one_r.at[1], {"dp": (1 - z_hi) * NY + y})

    def m_copy():
        src = pair.at[1 - z_hi, :, pl.ds(YFIRST, wide - YFIRST)]
        return remote(src, deep_in, one_s.at[3], one_r.at[3], {"dp": (1 - z_hi) * NY + y})

    def n_copy(r):
        to = lax.rem(y + r, NY)
        return remote(deep.at[place(to, HD, 16), :], last_in.at[r], n_s.at[r], n_r.at[r], {"dp": z_hi * NY + to})

    def b_copy(i):
        return remote(
            turned.at[place(i, HD, 16), :], blocks_in.at[head], b_s.at[i], b_r.at[head], {"blk": NB // 2 * core + i}
        )

    def b_wait(i):
        return remote(turned.at[place(i, HD, 16), :], blocks_in.at[i], b_s.at[i], b_r.at[i], {"blk": sibling})

    each(1, ND, lambda r: code_copy(r).start())

    def send_keys(r):
        page_copy(r).start()
        k_copy(r).start()

    each(1, NB, send_keys)
    each(1, NB, lambda r: v_copy(r).start())
    mine = [
        pltpu.make_async_copy(piece(0, blk), kT.at[pl.ds(0, HD), key_lanes(blk, core)], local.at[0]),
        pltpu.make_async_copy(piece(1, blk), vT.at[:, key_lanes(blk, core)], local.at[1]),
        pltpu.make_async_copy(piece(2, blk), qT.at[:, place(blk, HALF, HALF)], local.at[2]),
    ]
    for copy in mine:
        copy.start()
    for copy in mine:
        copy.wait()
    kk_copy(0).start()
    vv_copy(0).start()

    for copy in (loads[3], *loads[5:]):
        copy.wait()
    ahead[...] = dot_t(llm[...], w[...]).astype(BF16)
    each(1, ND, lambda r: code_copy(r).wait_recv())
    asked = jnp.broadcast_to(codes[...].astype(F32), (ND, PORTION, LANES)).reshape(ND * PORTION, LANES)
    spot = dp * PORTION + lax.rem(lax.broadcasted_iota(jnp.int32, asked.shape, 0), PORTION)
    asked = jnp.where(lax.broadcasted_iota(jnp.int32, asked.shape, 1) == spot, asked, 0.0)
    base = ((blk * ND + dp) * held).astype(F32)
    asked = jnp.broadcast_to(jnp.sum(asked, axis=1, keepdims=True) - base, asked.shape).astype(BF16)
    tok = lax.broadcasted_iota(jnp.int32, (TOK, ND * PORTION), 0)
    spread = (tok // MERGE == lax.broadcasted_iota(jnp.int32, (TOK, ND * PORTION), 1)).astype(BF16)
    row = dot(spread, asked)
    row = jnp.concatenate([row, row], axis=1)
    spot = lax.broadcasted_iota(jnp.int32, row.shape, 1)
    turn_of = lax.rem(lax.broadcasted_iota(jnp.int32, row.shape, 0), MERGE)
    hot = jnp.where((row == lax.rem(spot, held).astype(F32)) & (turn_of == spot // held), 1.0, 0.0).astype(BF16)
    do_rows[...] = dot(hot, ahead[...]).astype(BF16)

    def send_query(n):
        far = (n // 2 + 2) // NX
        to = 2 * (NX * lax.rem(z_lo + far, 2) + lax.rem(x_at + n // 2 + 2 * NX - 2 * far, NX)) + lax.rem(core + n, 2)
        q_copy(lax.rem(to + NB - blk, NB)).start()


    def relay_key(r):
        k_copy(r).wait_recv()
        kk_copy(r).start()
        page_copy(r).wait_recv()

    def key_block(r):
        block = lax.rem(sibling + NB - r, NB)
        cols = place(block, TOK, TOK)
        mark = (lax.broadcasted_iota(jnp.int32, (NB, LANES), 0).astype(F32) == pages[block]).astype(BF16)
        page[:, place(block, HALF, HALF)] = mark
        kT[HD:DEEP, key_lanes(block, 0)] = mark
        kT[HD:DEEP, key_lanes(block, 1)] = mark
        krow[cols, :] = dot_t(big, kT[:, cols]).astype(BF16)

    def relay_value(r):
        v_copy(r).wait_recv()
        vv_copy(r).start()

    each(1, NB // 2, relay_key)
    each(1, ND, lambda r: do_copy(r).start())
    do_mine[place(dp, SENT, 32), :] = do_rows[place(dp, SENT, 32), :]
    each(1, NB, send_query)
    each(NB // 2, NB, relay_key)
    each(0, NB, lambda r: kk_copy(r).wait_recv())
    for n in range(NB):
        key_block(n)


    def chunk_at(i):
        far = (i + 2) // NX
        return NX * lax.rem(z_lo + far, 2) + lax.rem(x_at + CHUNKS + 2 * far - i, NX)

    def wait_q(i):
        for e in (0, 1):
            r = lax.rem(blk + NB - 2 * chunk_at(i) - e, NB)

            @pl.when(r != 0)
            def _():
                q_copy(r).wait_recv()

    def query(i):
        cols = place(chunk_at(i), CHUNK, CHUNK)
        far = (1.0 - page[:, cols].astype(F32)) * FAR
        return jnp.concatenate([qT[:, cols], far.astype(BF16)], axis=0)

    def mix(cur, now, nxt, then, top):
        qx = query(then)
        cols = place(chunk_at(now), CHUNK, CHUNK)
        new = jnp.full((8, CHUNK), -3e38, F32)
        total = jnp.zeros((8, CHUNK), F32)
        out = jnp.zeros((HD, CHUNK), F32)
        for j in range(SEQ // TILE):
            rows = pl.ds(j * TILE, TILE)
            s = dot(krow[rows, :], qx)
            nxt[rows, :] = s
            new = jnp.maximum(new, jnp.max(s.reshape(TILE // 8, 8, CHUNK), axis=0))
            if cur is not None:
                p = jnp.exp2(cur[rows, :] * EXP2 - top)
                total = total + jnp.sum(p.reshape(TILE // 8, 8, CHUNK), axis=0)
                p = p.astype(BF16)
                ps[rows, cols] = p
                out = out + dot(vT[:, rows], p)
        if cur is not None:
            for e in (0, 1):
                at = place(2 * now + e, TOK, TOK)
                vrow[at, :] = dot_t(big, vT[:, at]).astype(BF16)
            inv = 1.0 / jnp.sum(total, axis=0, keepdims=True)
            ctxT[:, cols] = (out * inv).astype(BF16)
            stat[0:1, cols] = inv
        return jnp.max(new, axis=0, keepdims=True) * EXP2

    def send_context(i):
        for e in (0, 1):
            r = lax.rem(2 * chunk_at(i) + e + NB - blk, NB)

            @pl.when(r != 0)
            def _():
                c_copy(r).start()

    each(1, NB // 2, relay_value)
    wait_q(0)
    top = mix(None, 0, sa, 0, None)
    each(NB // 2, NB, relay_value)

    grad[...] = dot(hot, llm[...]).astype(BF16)
    each(0, NB, lambda r: vv_copy(r).wait_recv())

    def forward(i, top):
        wait_q(2 * i + 1)
        top = mix(sa, 2 * i, sb, 2 * i + 1, top)

        @pl.when(i > 0)
        def _():
            send_context(2 * i - 1)

        @pl.when(i < CHUNKS // 2 - 1)
        def _():
            wait_q(2 * i + 2)

        top = mix(sb, 2 * i + 1, sa, lax.rem(2 * i + 2, CHUNKS), top)
        send_context(2 * i)

        @pl.when(i == 0)
        def _():
            each(1, ND, lambda r: do_copy(r).wait_recv())
            for n in range(HF // LANES):
                lanes = slice(n * LANES, (n + 1) * LANES)
                do_own[pl.ds(n * LANES, LANES), :] = dot_t(ident, do_mine[:, lanes]).astype(BF16)
            each(1, NB, lambda r: dt_copy(r).start())
            pltpu.make_async_copy(
                do_own.at[mine_at], doT.at[:, place(blk, HALF, HALF)], local.at[4]
            ).start()
        @pl.when(i == 1)
        def _():
            def send_rows(r):
                near_copy(r).start()
                far_copy(r).start()

            each(1, ND, send_rows)
            far_copy(0).start()
            pltpu.make_async_copy(half_of(0, core), grad_near.at[place(dp, SENT, 32), :], local.at[3]).start()

        return top

    lax.fori_loop(0, CHUNKS // 2, forward, top)
    send_context(CHUNKS - 1)
    own_context = pltpu.make_async_copy(ctxT.at[:, place(blk, HALF, HALF)], ctx_own.at[mine_at], local.at[5])
    own_context.start()
    pltpu.make_async_copy(do_own.at[mine_at], doT.at[:, place(blk, HALF, HALF)], local.at[4]).wait()
    each(1, NB, lambda r: dt_copy(r).wait_recv())

    def middle(i):
        cols = place(i, CHUNK, CHUNK)
        inv = stat[0:1, cols]
        dof = doT[:, cols].astype(F32)
        stat[1:2, cols] = jnp.sum(dof * ctxT[:, cols].astype(F32), axis=0, keepdims=True)
        don[cols, :] = dot_t(big, (dof * inv).astype(BF16)).astype(BF16)
        qn[cols, :] = dot_t(big, (qT[:, cols].astype(F32) * inv).astype(BF16)).astype(BF16)
        dqa[:, cols] = jnp.zeros((HD, CHUNK), F32)

    for i in range(CHUNKS):
        middle(i)

    def chip_at(j):
        return lax.rem(head + 1 + j, PAIRS)

    def cross(j):
        for e in (0, 1):
            x_copy(2 * chip_at(j) + e).start()

    def add_up(j):
        for e in (0, 1):
            block = 2 * chip_at(j) + e
            x_copy(block).wait_recv()
            at = place(block, HALF, HALF)
            summed[:, :, at] = (
                part[:, :, key_lanes(block, core)].astype(F32) + partner[:, :, at].astype(F32)
            ).astype(BF16)

    def hand_out(j):
        for e in (0, 1):
            kv_copy(2 * chip_at(j) + e).start()

    def pass_context():
        own_context.wait()
        each(1, NB, lambda r: c_copy(r).wait_recv())
        ctx_copy().start()

    def weight_part():
        ctx_copy().wait_recv()
        pltpu.make_async_copy(half_of(0, core), grad_near.at[place(dp, SENT, 32), :], local.at[3]).wait()
        each(1, ND, lambda r: near_copy(r).wait_recv())
        each(0, ND, lambda r: far_copy(r).wait_recv())
        near = grad_near[...]
        for n in range(HF // LANES):
            at = pl.ds(n * LANES, LANES)
            term = dot(ctx_own[at, :], near) + dot(ctx_far[at, :], grad_far[...])
            for g in (0, LANES // 2):
                at = n * LANES + g
                pair[at // (HF // 2), pl.ds(at % (HF // 2), LANES // 2), :] = term[g : g + LANES // 2].astype(BF16)

    def weight_lanes():
        m_copy().start()
        each(1, NY, lambda r: l_copy(r).start())

    def weight_deep():
        m_copy().wait_recv()
        deep[...] = (pair[z_hi, :, YFIRST:].astype(F32) + deep_in[...].astype(F32)).astype(BF16)
        total = pair[:, place(y, HD, 16), :YFIRST].astype(F32)
        for r in range(1, NY):
            l_copy(r).wait_recv()
            total = total + lanes_in[r].astype(F32)
        far = jnp.where(z_hi == 0, total[1], total[0])
        lane_out[...] = far.astype(BF16)
        lane_sum[...] = jnp.where(z_hi == 0, total[0], total[1])

    def weight_far():
        z_copy().start()
        each(1, NY, lambda r: n_copy(r).start())

    def backward(j):
        @pl.when(j > 0)
        def _():
            cross(j - 1)

        pl.when(j == 3)(weight_lanes)
        pl.when(j == PAIRS - 1)(weight_far)

        rows = place(chip_at(j), PAIR, PAIR)
        values = vrow[rows, :]
        for i in range(CHUNKS):
            cols = pl.ds(i * CHUNK, CHUNK)
            dp_part = dot(values, doT[:, cols])
            ds[:, cols] = (ps[rows, cols].astype(F32) * (dp_part - stat[1:2, cols])).astype(BF16)
        dv = dot(ps[rows, :], don[...])
        dk = dot(ds[...], qn[...])
        dqa[...] += dot(kT[0:HD, rows], ds[...])
        part[0, :, rows] = dot_t(small, (dk * SCALE).astype(BF16)).astype(BF16)
        part[1, :, rows] = dot_t(small, dv.astype(BF16)).astype(BF16)

        @pl.when(j > 1)
        def _():
            hand_out(j - 2)

        @pl.when(j > 0)
        def _():
            add_up(j - 1)

        pl.when(j == 1)(pass_context)
        pl.when(j == 2)(weight_part)
        pl.when(j == PAIRS - 2)(weight_deep)


    each(0, PAIRS, backward)
    cross(PAIRS - 1)
    hand_out(PAIRS - 2)
    dqT[...] = (dqa[...] * (stat[0:1, :] * SCALE)).astype(BF16)
    each(1, NB, lambda r: dq_copy(r).start())
    own_dq = pltpu.make_async_copy(dqT.at[:, place(blk, HALF, HALF)], dq_own.at[mine_at], local.at[6])
    own_dq.start()
    add_up(PAIRS - 1)
    kv_copy(sibling).start()
    own_dkv = pltpu.make_async_copy(
        summed.at[:, :, place(blk, HALF, HALF)], dkv_own.at[:, mine_at[0], mine_at[1]], local.at[7]
    )
    own_dkv.start()

    def sent_early(r):
        for copy in (page_copy, k_copy, v_copy, q_copy, dt_copy, c_copy):
            copy(r).wait_send()

    each(1, NB, sent_early)

    def sent_over(r):
        kk_copy(r).wait_send()
        vv_copy(r).wait_send()
        x_copy(r).wait_send()

    each(0, NB, sent_over)
    each(0, ND, lambda r: far_copy(r).wait_send())
    each(1, NY, lambda r: l_copy(r).wait_send())
    m_copy().wait_send()
    ctx_copy().wait_send()

    def sent_dp(r):
        for copy in (code_copy, do_copy, near_copy):
            copy(r).wait_send()

    each(1, ND, sent_dp)
    z_copy().wait_recv()
    rest = deep[place(y, HD, 16), :].astype(F32)
    for r in range(1, NY):
        n_copy(r).wait_recv()
        rest = rest + last_in[r].astype(F32)
    total = jnp.concatenate([lane_sum[...] + z_in[...].astype(F32), rest], axis=1).astype(BF16)
    for i in range(wide // LANES):
        turned[pl.ds(i * LANES, LANES), :] = dot_t(ident, total[:, i * LANES : (i + 1) * LANES]).astype(BF16)

    def b_send(i):
        @pl.when(NB // 2 * core + i != blk)
        def _():
            b_copy(i).start()

    each(0, NB // 2, b_send)
    source_core = blk // (NB // 2)

    @pl.when(source_core == core)
    def _():
        blocks_in[pl.ds(head, 1)] = turned[place(lax.rem(blk, NB // 2), HD, 16), :][None]

    own_dkv.wait()

    def kv_arrived(r):
        kv_copy(lax.rem(blk + r, NB)).wait_recv()

    each(1, NB, kv_arrived)
    own_dq.wait()
    each(1, NB, lambda r: dq_copy(r).wait_recv())

    def b_recv(i):
        @pl.when(2 * i + source_core != blk)
        def _():
            b_wait(i).wait_recv()

    each(0, NB // 2, b_recv)
    def b_sent(i):
        @pl.when(NB // 2 * core + i != blk)
        def _():
            b_copy(i).wait_send()

    each(0, NB // 2, b_sent)

    def sent(r):
        dq_copy(r).wait_send()
        kv_copy(lax.rem(blk + r, NB)).wait_send()

    each(1, NB, sent)
    each(1, NY, lambda r: n_copy(r).wait_send())
    z_copy().wait_send()


def finish_kernel(dq, dkv, blocks, q_out, k_out, v_out, w_out):
    big = eye(TOK)
    q_out[...] = dot_t(big, dq[...]).astype(BF16)
    k_out[...] = dot_t(big, dkv[0]).astype(BF16)
    v_out[...] = dot_t(big, dkv[1]).astype(BF16)
    whole = blocks[0].astype(F32)
    for i in range(1, NB // 2):
        whole = whole + blocks[i].astype(F32)
    w_out[...] = whole


def finish(dq, dkv, blocks):
    return pl.pallas_call(
        finish_kernel,
        out_shape=[jax.ShapeDtypeStruct((TOK, HF), BF16)] * 3 + [jax.ShapeDtypeStruct((HD, HD), F32)],
        in_specs=[pl.BlockSpec(memory_space=VM)] * 3,
        out_specs=[pl.BlockSpec(memory_space=VM)] * 4,
        compiler_params=pltpu.CompilerParams(vmem_limit_bytes=8 * 2**20),
    )(dq, dkv, blocks)


def layer(q, k, v, w, llm, sources, first_block):
    dma = pltpu.SemaphoreType.DMA
    wide = w.shape[1] // 2
    nb, nd = [dma((NB,))] * 2, [dma((ND,))] * 2
    return pl.pallas_call(
        layer_kernel,
        out_shape=[
            jax.ShapeDtypeStruct((HF, TOK), BF16),
            jax.ShapeDtypeStruct((2, HF, TOK), BF16),
            jax.ShapeDtypeStruct((NB // 2, HD, HD), BF16),
        ],
        in_specs=[pl.BlockSpec(memory_space=pltpu.HBM)] * 6 + [pl.BlockSpec(memory_space=VM)],
        out_specs=[pl.BlockSpec(memory_space=VM)] * 3,
        scratch_shapes=[
            VM(q.shape, BF16), VM(k.shape, BF16), VM(v.shape, BF16), VM(w.shape, BF16), VM((TOK, w.shape[1]), BF16),
            VM(sources.shape, jnp.int32),
            VM((3, HF, TOK), BF16), VM((HF, TOK), BF16), VM((ND, 1, LANES), jnp.int32),
            VM((TOK, HF), BF16), VM((TOK, HF), BF16), VM((TOK, w.shape[1]), BF16), VM((TOK, wide), BF16),
            VM((TOK, wide), BF16), VM((TOK, HF), BF16),
            VM((1, LANES), jnp.int32), VM((1, LANES), F32), VM((NB, 1, LANES), F32),
            VM((HD, QUERIES), BF16), VM((DEEP, SEQ), BF16), VM((HD, SEQ), BF16), VM((HD, QUERIES), BF16),
            VM((NB, QUERIES), BF16), VM((SEQ, DEEP), BF16), VM((SEQ, HD), BF16),
            VM((SEQ, CHUNK), F32), VM((SEQ, CHUNK), F32), VM((SEQ, QUERIES), BF16), VM((PAIR, QUERIES), BF16),
            VM((QUERIES, HD), BF16), VM((QUERIES, HD), BF16), VM((8, QUERIES), F32), VM((HD, QUERIES), F32),
            VM((HD, QUERIES), BF16), VM((HD, QUERIES), BF16),
            VM((2, HD, SEQ), BF16), VM((2, HD, QUERIES), BF16), VM((2, HD, QUERIES), BF16),
            VM((HF, TOK), BF16),
            VM((HF, TOK), BF16), VM((2, HF // 2, wide), BF16), VM((NY, 2, HD, YFIRST), BF16),
            VM((HD, YFIRST), F32), VM((HD, YFIRST), BF16), VM((HD, YFIRST), BF16),
            VM((HF // 2, wide - YFIRST), BF16), VM((HF // 2, wide - YFIRST), BF16), VM((NY, HD, wide - YFIRST), BF16),
            VM((wide, HD), BF16),
            *nd, *nb, *nb, *nb, *nb, *nd, *nb, *nb, *nb,
            *nb, *nb, *nb, *nb, *nd, *nd, *nd, *nd, *nd, dma((4,)), dma((4,)), dma((8,)), dma((5 + MERGE,)),
        ],
        compiler_params=pltpu.CompilerParams(
            collective_id=0, has_side_effects=True, vmem_limit_bytes=48 * 2**20
        ),
    )(q, k, v, w, llm, sources, first_block)


def body(saved_query, saved_key, saved_value, out_weight, llm_grad, row_source, page_start, page_size):
    stay = [
        pltpu.with_memory_space_constraint(x, pltpu.HBM)
        for x in (saved_query[0], saved_key[0], saved_value[0], out_weight, llm_grad, row_source)
    ]
    turned = layer(*stay, page_start)
    query_grad, key_grad, value_grad, weight_grad = finish(*turned)
    return (query_grad[None], key_grad[None], value_grad[None], weight_grad)


def solution(mesh):
    in_specs = (
        P("dp", "blk", None),
        P("dp", "blk", None),
        P("dp", "blk", None),
        P(),
        P(("blk", "dp"), None),
        P("dp", "blk"),
        P("dp", "blk"),
        P("dp", "blk"),
    )
    out_specs = (P("dp", "blk", None), P("dp", "blk", None), P("dp", "blk", None), P("blk", "dp"))
    return jax.shard_map(body, mesh=mesh, in_specs=in_specs, out_specs=out_specs, check_vma=False)
```

```python
import math

import jax
import jax.numpy as jnp
from jax import lax
from jax.experimental import pallas as pl
from jax.experimental.pallas import tpu as pltpu
from jax.sharding import PartitionSpec as P

HEADS = 8
HD = 80
MERGE = 4
TOK = 256
HF = HEADS * HD
NB = 16
ND = 8
NY = 4
NX = 4
YFIRST = 384
PORTION = TOK // MERGE // ND
SENT = TOK // ND
LANES = 128
HALF = TOK // 2
SEQ = NB * TOK
QUERIES = SEQ // 2
CHUNK = 256
CHUNKS = QUERIES // CHUNK
TILE = 512
PAIR = 2 * TOK
PAIRS = SEQ // PAIR
DEEP = HD + NB
SCALE = 1.0 / math.sqrt(HD)
EXP2 = SCALE / math.log(2.0)
F32, BF16 = jnp.float32, jnp.bfloat16
FAR = -1e30
VM = pltpu.VMEM


def eye(n):
    return (lax.broadcasted_iota(jnp.int32, (n, n), 0) == lax.broadcasted_iota(jnp.int32, (n, n), 1)).astype(BF16)


def dot(a, b):
    return lax.dot_general(a, b, (((1,), (0,)), ((), ())), preferred_element_type=F32)


def dot_t(a, b):
    return lax.dot_general(a, b, (((1,), (1,)), ((), ())), preferred_element_type=F32)


def each(low, high, act):
    def step(r, _):
        act(r)
        return 0

    lax.fori_loop(low, high, step, 0)


def place(index, size, align):
    return pl.ds(pl.multiple_of(index * size, align), size)


def remote(src, dst, send, recv, where):
    return pltpu.make_async_remote_copy(
        src_ref=src, dst_ref=dst, send_sem=send, recv_sem=recv, device_id=where
    )


def layer_kernel(
    q_hbm, k_hbm, v_hbm, w_hbm, llm_hbm, sources_hbm, first_block,
    dq_own, dkv_own, blocks_in,
    q, k, v, w, llm, sources,
    own, do_own, codes, do_rows, do_mine, grad, grad_near, grad_far, ahead, code_own, page_own, pages,
    qT, kT, vT, doT, page, krow, vrow, sa, sb, ps, ds, don, qn, stat, dqa, ctxT, dqT,
    part, partner, summed, ctx_own,
    ctx_far, pair, lanes_in, lane_sum, lane_out, z_in, deep_in, deep, last_in, turned,
    code_s, code_r, page_s, page_r, q_s, q_r, k_s, k_r, v_s, v_r, do_s, do_r, dt_s, dt_r, kk_s, kk_r, vv_s, vv_r,
    c_s, c_r, dq_s, dq_r, x_s, x_r, kv_s, kv_r, r_s, r_r, f_s, f_r, l_s, l_r, n_s, n_r, b_s, b_r, one_s, one_r, local, load,
):
    blk, dp = lax.axis_index("blk"), lax.axis_index("dp")
    core = lax.rem(blk, 2)
    sibling = blk + 1 - 2 * core
    head = blk // 2
    width = w.shape[1]
    wide = width // 2
    z_hi, y = dp // NY, lax.rem(dp, NY)
    z_lo, x_at = head // NX, lax.rem(head, NX)

    arguments = ((k_hbm, k), (v_hbm, v), (q_hbm, q), (w_hbm, w), (sources_hbm, sources))
    loads = [pltpu.make_async_copy(src, dst, load.at[n]) for n, (src, dst) in enumerate(arguments)]
    held = llm_hbm.shape[0]
    for m in range(MERGE):
        src = llm_hbm.at[:, pl.ds(m * w.shape[1], w.shape[1])]
        loads.append(pltpu.make_async_copy(src, llm.at[pl.ds(m * held, held), :], load.at[5 + m]))
    for copy in loads:
        copy.start()

    barrier = pltpu.get_barrier_semaphore()
    each(1, ND, lambda r: pl.semaphore_signal(barrier, inc=1, device_id={"dp": lax.rem(dp + r, ND)}))
    each(
        1, ND,
        lambda r: pl.semaphore_signal(barrier, inc=1, device_id={"blk": sibling, "dp": lax.rem(dp + r, ND)}),
    )
    each(1, NB, lambda r: pl.semaphore_signal(barrier, inc=1, device_id={"blk": lax.rem(blk + r, NB)}))
    ident = eye(LANES)
    big = eye(TOK)
    small = eye(HD)
    for n, x in enumerate((k, v, q)):
        loads[n].wait()
        for i in range(HF // LANES):
            own[n, pl.ds(i * LANES, LANES), :] = dot_t(ident, x[:, i * LANES : (i + 1) * LANES]).astype(BF16)
    loads[4].wait()
    code_own[...] = jnp.concatenate([sources[...], sources[...]], axis=1)
    codes[pl.ds(dp, 1)] = code_own[...][None]
    page_own[...] = jnp.broadcast_to(first_block[...].astype(F32), (1, LANES))
    pages[pl.ds(blk, 1)] = page_own[...][None]
    pl.semaphore_wait(barrier, NB + 2 * ND - 3)

    def towards(r):
        return lax.rem(blk + r, NB)

    def piece(n, to):
        return own.at[n, place(to // 2, HD, 16), place(lax.rem(to, 2), HALF, HALF)]

    def code_copy(r):
        to = lax.rem(dp + r, ND)
        return remote(code_own, codes.at[dp], code_s.at[r], code_r.at[r], {"dp": to})

    def page_copy(r):
        return remote(page_own, pages.at[blk], page_s.at[r], page_r.at[r], {"blk": towards(r)})

    def key_lanes(block, side):
        return pl.ds(pl.multiple_of(block * TOK + side * HALF, HALF), HALF)

    def k_copy(r):
        to = towards(r)
        dst = kT.at[pl.ds(0, HD), key_lanes(blk, lax.rem(to, 2))]
        return remote(piece(0, to), dst, k_s.at[r], k_r.at[r], {"blk": to})

    def v_copy(r):
        to = towards(r)
        return remote(piece(1, to), vT.at[:, key_lanes(blk, lax.rem(to, 2))], v_s.at[r], v_r.at[r], {"blk": to})

    def q_copy(r):
        to = towards(r)
        return remote(piece(2, to), qT.at[:, place(blk, HALF, HALF)], q_s.at[r], q_r.at[r], {"blk": to})

    def kk_copy(r):
        half = kT.at[pl.ds(0, HD), key_lanes(lax.rem(blk + NB - r, NB), core)]
        return remote(half, half, kk_s.at[r], kk_r.at[r], {"blk": sibling})

    def vv_copy(r):
        half = vT.at[:, key_lanes(lax.rem(blk + NB - r, NB), core)]
        return remote(half, half, vv_s.at[r], vv_r.at[r], {"blk": sibling})

    def do_copy(r):
        to = lax.rem(dp + r, ND)
        return remote(
            do_rows.at[place(to, SENT, 32), :], do_mine.at[place(dp, SENT, 32), :], do_s.at[r], do_r.at[r], {"dp": to}
        )

    def dt_copy(r):
        to = towards(r)
        src = do_own.at[place(to // 2, HD, 16), place(lax.rem(to, 2), HALF, HALF)]
        return remote(src, doT.at[:, place(blk, HALF, HALF)], dt_s.at[r], dt_r.at[r], {"blk": to})

    mine_at = (place(head, HD, 16), place(core, HALF, HALF))

    def c_copy(r):
        to = towards(r)
        return remote(ctxT.at[:, place(to, HALF, HALF)], ctx_own.at[mine_at], c_s.at[r], c_r.at[r], {"blk": to})

    def dq_copy(r):
        to = towards(r)
        return remote(dqT.at[:, place(to, HALF, HALF)], dq_own.at[mine_at], dq_s.at[r], dq_r.at[r], {"blk": to})

    def x_copy(block):
        lanes = key_lanes(block, 1 - core)
        return remote(
            part.at[:, :, lanes], partner.at[:, :, place(block, HALF, HALF)], x_s.at[block], x_r.at[block],
            {"blk": sibling},
        )

    def kv_copy(block):
        r = lax.rem(block + NB - blk, NB)
        return remote(
            summed.at[:, :, place(block, HALF, HALF)], dkv_own.at[:, mine_at[0], mine_at[1]],
            kv_s.at[r], kv_r.at[r], {"blk": block},
        )

    def half_of(r, side):
        return grad.at[place(lax.rem(dp + r, ND), SENT, 32), pl.ds(pl.multiple_of(side * wide, LANES), wide)]

    def near_copy(r):
        dst = grad_near.at[place(dp, SENT, 32), :]
        return remote(half_of(r, core), dst, r_s.at[r], r_r.at[r], {"dp": lax.rem(dp + r, ND)})

    def far_copy(r):
        dst = grad_far.at[place(dp, SENT, 32), :]
        to = {"blk": sibling, "dp": lax.rem(dp + r, ND)}
        return remote(half_of(r, 1 - core), dst, f_s.at[r], f_r.at[r], to)

    def ctx_copy():
        return remote(ctx_own, ctx_far, one_s.at[2], one_r.at[2], {"blk": sibling})

    def l_copy(r):
        to = lax.rem(y + r, NY)
        src = pair.at[:, place(to, HD, 16), pl.ds(0, YFIRST)]
        return remote(src, lanes_in.at[r], l_s.at[r], l_r.at[r], {"dp": z_hi * NY + to})

    def z_copy():
        return remote(lane_out, z_in, one_s.at[1], one_r.at[1], {"dp": (1 - z_hi) * NY + y})

    def m_copy():
        src = pair.at[1 - z_hi, :, pl.ds(YFIRST, wide - YFIRST)]
        return remote(src, deep_in, one_s.at[3], one_r.at[3], {"dp": (1 - z_hi) * NY + y})

    def n_copy(r):
        to = lax.rem(y + r, NY)
        return remote(deep.at[place(to, HD, 16), :], last_in.at[r], n_s.at[r], n_r.at[r], {"dp": z_hi * NY + to})

    def b_copy(i):
        return remote(
            turned.at[place(i, HD, 16), :], blocks_in.at[head], b_s.at[i], b_r.at[head], {"blk": NB // 2 * core + i}
        )

    def b_wait(i):
        return remote(turned.at[place(i, HD, 16), :], blocks_in.at[i], b_s.at[i], b_r.at[i], {"blk": sibling})

    each(1, ND, lambda r: code_copy(r).start())

    def send_keys(r):
        page_copy(r).start()
        k_copy(r).start()

    each(1, NB, send_keys)
    each(1, NB, lambda r: v_copy(r).start())
    mine = [
        pltpu.make_async_copy(piece(0, blk), kT.at[pl.ds(0, HD), key_lanes(blk, core)], local.at[0]),
        pltpu.make_async_copy(piece(1, blk), vT.at[:, key_lanes(blk, core)], local.at[1]),
        pltpu.make_async_copy(piece(2, blk), qT.at[:, place(blk, HALF, HALF)], local.at[2]),
    ]
    for copy in mine:
        copy.start()
    for copy in mine:
        copy.wait()
    kk_copy(0).start()
    vv_copy(0).start()

    for copy in (loads[3], *loads[5:]):
        copy.wait()
    ahead[...] = dot_t(llm[...], w[...]).astype(BF16)
    each(1, ND, lambda r: code_copy(r).wait_recv())
    asked = jnp.broadcast_to(codes[...].astype(F32), (ND, PORTION, LANES)).reshape(ND * PORTION, LANES)
    spot = dp * PORTION + lax.rem(lax.broadcasted_iota(jnp.int32, asked.shape, 0), PORTION)
    asked = jnp.where(lax.broadcasted_iota(jnp.int32, asked.shape, 1) == spot, asked, 0.0)
    base = ((blk * ND + dp) * held).astype(F32)
    asked = jnp.broadcast_to(jnp.sum(asked, axis=1, keepdims=True) - base, asked.shape).astype(BF16)
    tok = lax.broadcasted_iota(jnp.int32, (TOK, ND * PORTION), 0)
    spread = (tok // MERGE == lax.broadcasted_iota(jnp.int32, (TOK, ND * PORTION), 1)).astype(BF16)
    row = dot(spread, asked)
    row = jnp.concatenate([row, row], axis=1)
    spot = lax.broadcasted_iota(jnp.int32, row.shape, 1)
    turn_of = lax.rem(lax.broadcasted_iota(jnp.int32, row.shape, 0), MERGE)
    hot = jnp.where((row == lax.rem(spot, held).astype(F32)) & (turn_of == spot // held), 1.0, 0.0).astype(BF16)
    do_rows[...] = dot(hot, ahead[...]).astype(BF16)

    def send_query(n):
        to = 2 * (NX * lax.rem(z_lo + n // (2 * NX), 2) + lax.rem(x_at + n // 2, NX)) + lax.rem(core + n, 2)
        q_copy(lax.rem(to + NB - blk, NB)).start()


    def relay_key(r):
        k_copy(r).wait_recv()
        kk_copy(r).start()
        page_copy(r).wait_recv()

    def key_block(r):
        block = lax.rem(sibling + NB - r, NB)
        cols = place(block, TOK, TOK)
        mark = (lax.broadcasted_iota(jnp.int32, (NB, LANES), 0).astype(F32) == pages[block]).astype(BF16)
        page[:, place(block, HALF, HALF)] = mark
        kT[HD:DEEP, key_lanes(block, 0)] = mark
        kT[HD:DEEP, key_lanes(block, 1)] = mark
        krow[cols, :] = dot_t(big, kT[:, cols]).astype(BF16)

    def relay_value(r):
        v_copy(r).wait_recv()
        vv_copy(r).start()

    each(1, NB // 2, relay_key)
    each(1, ND, lambda r: do_copy(r).start())
    do_mine[place(dp, SENT, 32), :] = do_rows[place(dp, SENT, 32), :]
    each(1, NB, send_query)
    each(NB // 2, NB, relay_key)
    each(0, NB, lambda r: kk_copy(r).wait_recv())
    for n in range(NB):
        key_block(n)


    def chunk_at(i):
        return NX * lax.rem(z_lo + i // NX, 2) + lax.rem(x_at + CHUNKS - i, NX)

    def wait_q(i):
        for e in (0, 1):
            r = lax.rem(blk + NB - 2 * chunk_at(i) - e, NB)

            @pl.when(r != 0)
            def _():
                q_copy(r).wait_recv()

    def query(i):
        cols = place(chunk_at(i), CHUNK, CHUNK)
        far = (1.0 - page[:, cols].astype(F32)) * FAR
        return jnp.concatenate([qT[:, cols], far.astype(BF16)], axis=0)

    def mix(cur, now, nxt, then, top):
        qx = query(then)
        cols = place(chunk_at(now), CHUNK, CHUNK)
        new = jnp.full((8, CHUNK), -3e38, F32)
        total = jnp.zeros((8, CHUNK), F32)
        out = jnp.zeros((HD, CHUNK), F32)
        for j in range(SEQ // TILE):
            rows = pl.ds(j * TILE, TILE)
            s = dot(krow[rows, :], qx)
            nxt[rows, :] = s
            new = jnp.maximum(new, jnp.max(s.reshape(TILE // 8, 8, CHUNK), axis=0))
            if cur is not None:
                p = jnp.exp2(cur[rows, :] * EXP2 - top)
                total = total + jnp.sum(p.reshape(TILE // 8, 8, CHUNK), axis=0)
                p = p.astype(BF16)
                ps[rows, cols] = p
                out = out + dot(vT[:, rows], p)
        if cur is not None:
            for e in (0, 1):
                at = place(2 * now + e, TOK, TOK)
                vrow[at, :] = dot_t(big, vT[:, at]).astype(BF16)
            inv = 1.0 / jnp.sum(total, axis=0, keepdims=True)
            ctxT[:, cols] = (out * inv).astype(BF16)
            stat[0:1, cols] = inv
        return jnp.max(new, axis=0, keepdims=True) * EXP2

    def send_context(i):
        for e in (0, 1):
            r = lax.rem(2 * chunk_at(i) + e + NB - blk, NB)

            @pl.when(r != 0)
            def _():
                c_copy(r).start()

    each(1, NB // 2, relay_value)
    wait_q(0)
    top = mix(None, 0, sa, 0, None)
    each(NB // 2, NB, relay_value)

    grad[...] = dot(hot, llm[...]).astype(BF16)
    each(0, NB, lambda r: vv_copy(r).wait_recv())

    def forward(i, top):
        wait_q(2 * i + 1)
        top = mix(sa, 2 * i, sb, 2 * i + 1, top)

        @pl.when(i > 0)
        def _():
            send_context(2 * i - 1)

        @pl.when(i < CHUNKS // 2 - 1)
        def _():
            wait_q(2 * i + 2)

        top = mix(sb, 2 * i + 1, sa, lax.rem(2 * i + 2, CHUNKS), top)
        send_context(2 * i)

        @pl.when(i == 0)
        def _():
            each(1, ND, lambda r: do_copy(r).wait_recv())
            for n in range(HF // LANES):
                lanes = slice(n * LANES, (n + 1) * LANES)
                do_own[pl.ds(n * LANES, LANES), :] = dot_t(ident, do_mine[:, lanes]).astype(BF16)
            each(1, NB, lambda r: dt_copy(r).start())
            pltpu.make_async_copy(
                do_own.at[mine_at], doT.at[:, place(blk, HALF, HALF)], local.at[4]
            ).start()
        @pl.when(i == 1)
        def _():
            def send_rows(r):
                near_copy(r).start()
                far_copy(r).start()

            each(1, ND, send_rows)
            far_copy(0).start()
            pltpu.make_async_copy(half_of(0, core), grad_near.at[place(dp, SENT, 32), :], local.at[3]).start()

        return top

    lax.fori_loop(0, CHUNKS // 2, forward, top)
    send_context(CHUNKS - 1)
    own_context = pltpu.make_async_copy(ctxT.at[:, place(blk, HALF, HALF)], ctx_own.at[mine_at], local.at[5])
    own_context.start()
    pltpu.make_async_copy(do_own.at[mine_at], doT.at[:, place(blk, HALF, HALF)], local.at[4]).wait()
    each(1, NB, lambda r: dt_copy(r).wait_recv())

    def middle(i):
        cols = place(i, CHUNK, CHUNK)
        inv = stat[0:1, cols]
        dof = doT[:, cols].astype(F32)
        stat[1:2, cols] = jnp.sum(dof * ctxT[:, cols].astype(F32), axis=0, keepdims=True)
        don[cols, :] = dot_t(big, (dof * inv).astype(BF16)).astype(BF16)
        qn[cols, :] = dot_t(big, (qT[:, cols].astype(F32) * inv).astype(BF16)).astype(BF16)
        dqa[:, cols] = jnp.zeros((HD, CHUNK), F32)

    for i in range(CHUNKS):
        middle(i)

    def chip_at(j):
        return lax.rem(head + 1 + j, PAIRS)

    def cross(j):
        for e in (0, 1):
            x_copy(2 * chip_at(j) + e).start()

    def add_up(j):
        for e in (0, 1):
            block = 2 * chip_at(j) + e
            x_copy(block).wait_recv()
            at = place(block, HALF, HALF)
            summed[:, :, at] = (
                part[:, :, key_lanes(block, core)].astype(F32) + partner[:, :, at].astype(F32)
            ).astype(BF16)

    def hand_out(j):
        for e in (0, 1):
            kv_copy(2 * chip_at(j) + e).start()

    def pass_context():
        own_context.wait()
        each(1, NB, lambda r: c_copy(r).wait_recv())
        ctx_copy().start()

    def weight_part():
        ctx_copy().wait_recv()
        pltpu.make_async_copy(half_of(0, core), grad_near.at[place(dp, SENT, 32), :], local.at[3]).wait()
        each(1, ND, lambda r: near_copy(r).wait_recv())
        each(0, ND, lambda r: far_copy(r).wait_recv())
        near = grad_near[...]
        for n in range(HF // LANES):
            at = pl.ds(n * LANES, LANES)
            term = dot(ctx_own[at, :], near) + dot(ctx_far[at, :], grad_far[...])
            for g in (0, LANES // 2):
                at = n * LANES + g
                pair[at // (HF // 2), pl.ds(at % (HF // 2), LANES // 2), :] = term[g : g + LANES // 2].astype(BF16)

    def weight_lanes():
        m_copy().start()
        each(1, NY, lambda r: l_copy(r).start())

    def weight_deep():
        m_copy().wait_recv()
        deep[...] = (pair[z_hi, :, YFIRST:].astype(F32) + deep_in[...].astype(F32)).astype(BF16)
        total = pair[:, place(y, HD, 16), :YFIRST].astype(F32)
        for r in range(1, NY):
            l_copy(r).wait_recv()
            total = total + lanes_in[r].astype(F32)
        far = jnp.where(z_hi == 0, total[1], total[0])
        lane_out[...] = far.astype(BF16)
        lane_sum[...] = jnp.where(z_hi == 0, total[0], total[1])

    def weight_far():
        z_copy().start()
        each(1, NY, lambda r: n_copy(r).start())

    def backward(j):
        @pl.when(j > 0)
        def _():
            cross(j - 1)

        pl.when(j == 3)(weight_lanes)
        pl.when(j == PAIRS - 1)(weight_far)

        rows = place(chip_at(j), PAIR, PAIR)
        values = vrow[rows, :]
        for i in range(CHUNKS):
            cols = pl.ds(i * CHUNK, CHUNK)
            dp_part = dot(values, doT[:, cols])
            ds[:, cols] = (ps[rows, cols].astype(F32) * (dp_part - stat[1:2, cols])).astype(BF16)
        dv = dot(ps[rows, :], don[...])
        dk = dot(ds[...], qn[...])
        dqa[...] += dot(kT[0:HD, rows], ds[...])
        part[0, :, rows] = dot_t(small, (dk * SCALE).astype(BF16)).astype(BF16)
        part[1, :, rows] = dot_t(small, dv.astype(BF16)).astype(BF16)

        @pl.when(j > 1)
        def _():
            hand_out(j - 2)

        @pl.when(j > 0)
        def _():
            add_up(j - 1)

        pl.when(j == 1)(pass_context)
        pl.when(j == 2)(weight_part)
        pl.when(j == PAIRS - 2)(weight_deep)


    each(0, PAIRS, backward)
    cross(PAIRS - 1)
    hand_out(PAIRS - 2)
    dqT[...] = (dqa[...] * (stat[0:1, :] * SCALE)).astype(BF16)
    each(1, NB, lambda r: dq_copy(r).start())
    own_dq = pltpu.make_async_copy(dqT.at[:, place(blk, HALF, HALF)], dq_own.at[mine_at], local.at[6])
    own_dq.start()
    add_up(PAIRS - 1)
    kv_copy(sibling).start()
    own_dkv = pltpu.make_async_copy(
        summed.at[:, :, place(blk, HALF, HALF)], dkv_own.at[:, mine_at[0], mine_at[1]], local.at[7]
    )
    own_dkv.start()

    def sent_early(r):
        for copy in (page_copy, k_copy, v_copy, q_copy, dt_copy, c_copy):
            copy(r).wait_send()

    each(1, NB, sent_early)

    def sent_over(r):
        kk_copy(r).wait_send()
        vv_copy(r).wait_send()
        x_copy(r).wait_send()

    each(0, NB, sent_over)
    each(0, ND, lambda r: far_copy(r).wait_send())
    each(1, NY, lambda r: l_copy(r).wait_send())
    m_copy().wait_send()
    ctx_copy().wait_send()

    def sent_dp(r):
        for copy in (code_copy, do_copy, near_copy):
            copy(r).wait_send()

    each(1, ND, sent_dp)
    z_copy().wait_recv()
    rest = deep[place(y, HD, 16), :].astype(F32)
    for r in range(1, NY):
        n_copy(r).wait_recv()
        rest = rest + last_in[r].astype(F32)
    total = jnp.concatenate([lane_sum[...] + z_in[...].astype(F32), rest], axis=1).astype(BF16)
    for i in range(wide // LANES):
        turned[pl.ds(i * LANES, LANES), :] = dot_t(ident, total[:, i * LANES : (i + 1) * LANES]).astype(BF16)

    def b_send(i):
        @pl.when(NB // 2 * core + i != blk)
        def _():
            b_copy(i).start()

    each(0, NB // 2, b_send)
    source_core = blk // (NB // 2)

    @pl.when(source_core == core)
    def _():
        blocks_in[pl.ds(head, 1)] = turned[place(lax.rem(blk, NB // 2), HD, 16), :][None]

    own_dkv.wait()

    def kv_arrived(r):
        kv_copy(lax.rem(blk + r, NB)).wait_recv()

    each(1, NB, kv_arrived)
    own_dq.wait()
    each(1, NB, lambda r: dq_copy(r).wait_recv())

    def b_recv(i):
        @pl.when(2 * i + source_core != blk)
        def _():
            b_wait(i).wait_recv()

    each(0, NB // 2, b_recv)
    def b_sent(i):
        @pl.when(NB // 2 * core + i != blk)
        def _():
            b_copy(i).wait_send()

    each(0, NB // 2, b_sent)

    def sent(r):
        dq_copy(r).wait_send()
        kv_copy(lax.rem(blk + r, NB)).wait_send()

    each(1, NB, sent)
    each(1, NY, lambda r: n_copy(r).wait_send())
    z_copy().wait_send()


def finish_kernel(dq, dkv, blocks, q_out, k_out, v_out, w_out):
    big = eye(TOK)
    q_out[...] = dot_t(big, dq[...]).astype(BF16)
    k_out[...] = dot_t(big, dkv[0]).astype(BF16)
    v_out[...] = dot_t(big, dkv[1]).astype(BF16)
    whole = blocks[0].astype(F32)
    for i in range(1, NB // 2):
        whole = whole + blocks[i].astype(F32)
    w_out[...] = whole


def finish(dq, dkv, blocks):
    return pl.pallas_call(
        finish_kernel,
        out_shape=[jax.ShapeDtypeStruct((TOK, HF), BF16)] * 3 + [jax.ShapeDtypeStruct((HD, HD), F32)],
        in_specs=[pl.BlockSpec(memory_space=VM)] * 3,
        out_specs=[pl.BlockSpec(memory_space=VM)] * 4,
        compiler_params=pltpu.CompilerParams(vmem_limit_bytes=8 * 2**20),
    )(dq, dkv, blocks)


def layer(q, k, v, w, llm, sources, first_block):
    dma = pltpu.SemaphoreType.DMA
    wide = w.shape[1] // 2
    nb, nd = [dma((NB,))] * 2, [dma((ND,))] * 2
    return pl.pallas_call(
        layer_kernel,
        out_shape=[
            jax.ShapeDtypeStruct((HF, TOK), BF16),
            jax.ShapeDtypeStruct((2, HF, TOK), BF16),
            jax.ShapeDtypeStruct((NB // 2, HD, HD), BF16),
        ],
        in_specs=[pl.BlockSpec(memory_space=pltpu.HBM)] * 6 + [pl.BlockSpec(memory_space=VM)],
        out_specs=[pl.BlockSpec(memory_space=VM)] * 3,
        scratch_shapes=[
            VM(q.shape, BF16), VM(k.shape, BF16), VM(v.shape, BF16), VM(w.shape, BF16), VM((TOK, w.shape[1]), BF16),
            VM(sources.shape, jnp.int32),
            VM((3, HF, TOK), BF16), VM((HF, TOK), BF16), VM((ND, 1, LANES), jnp.int32),
            VM((TOK, HF), BF16), VM((TOK, HF), BF16), VM((TOK, w.shape[1]), BF16), VM((TOK, wide), BF16),
            VM((TOK, wide), BF16), VM((TOK, HF), BF16),
            VM((1, LANES), jnp.int32), VM((1, LANES), F32), VM((NB, 1, LANES), F32),
            VM((HD, QUERIES), BF16), VM((DEEP, SEQ), BF16), VM((HD, SEQ), BF16), VM((HD, QUERIES), BF16),
            VM((NB, QUERIES), BF16), VM((SEQ, DEEP), BF16), VM((SEQ, HD), BF16),
            VM((SEQ, CHUNK), F32), VM((SEQ, CHUNK), F32), VM((SEQ, QUERIES), BF16), VM((PAIR, QUERIES), BF16),
            VM((QUERIES, HD), BF16), VM((QUERIES, HD), BF16), VM((8, QUERIES), F32), VM((HD, QUERIES), F32),
            VM((HD, QUERIES), BF16), VM((HD, QUERIES), BF16),
            VM((2, HD, SEQ), BF16), VM((2, HD, QUERIES), BF16), VM((2, HD, QUERIES), BF16),
            VM((HF, TOK), BF16),
            VM((HF, TOK), BF16), VM((2, HF // 2, wide), BF16), VM((NY, 2, HD, YFIRST), BF16),
            VM((HD, YFIRST), F32), VM((HD, YFIRST), BF16), VM((HD, YFIRST), BF16),
            VM((HF // 2, wide - YFIRST), BF16), VM((HF // 2, wide - YFIRST), BF16), VM((NY, HD, wide - YFIRST), BF16),
            VM((wide, HD), BF16),
            *nd, *nb, *nb, *nb, *nb, *nd, *nb, *nb, *nb,
            *nb, *nb, *nb, *nb, *nd, *nd, *nd, *nd, *nd, dma((4,)), dma((4,)), dma((8,)), dma((5 + MERGE,)),
        ],
        compiler_params=pltpu.CompilerParams(
            collective_id=0, has_side_effects=True, vmem_limit_bytes=48 * 2**20
        ),
    )(q, k, v, w, llm, sources, first_block)


def body(saved_query, saved_key, saved_value, out_weight, llm_grad, row_source, page_start, page_size):
    stay = [
        pltpu.with_memory_space_constraint(x, pltpu.HBM)
        for x in (saved_query[0], saved_key[0], saved_value[0], out_weight, llm_grad, row_source)
    ]
    turned = layer(*stay, page_start)
    query_grad, key_grad, value_grad, weight_grad = finish(*turned)
    return (query_grad[None], key_grad[None], value_grad[None], weight_grad)


def solution(mesh):
    in_specs = (
        P("dp", "blk", None),
        P("dp", "blk", None),
        P("dp", "blk", None),
        P(),
        P(("blk", "dp"), None),
        P("dp", "blk"),
        P("dp", "blk"),
        P("dp", "blk"),
    )
    out_specs = (P("dp", "blk", None), P("dp", "blk", None), P("dp", "blk", None), P("blk", "dp"))
    return jax.shard_map(body, mesh=mesh, in_specs=in_specs, out_specs=out_specs, check_vma=False)
```

```python
import math

import jax
import jax.numpy as jnp
from jax import lax
from jax.experimental import pallas as pl
from jax.experimental.pallas import tpu as pltpu
from jax.sharding import PartitionSpec as P

HEADS = 8
HD = 80
MERGE = 4
TOK = 256
HF = HEADS * HD
NB = 16
ND = 8
NY = 4
NX = 4
YFIRST = 512
PORTION = TOK // MERGE // ND
SENT = TOK // ND
LANES = 128
HALF = TOK // 2
SEQ = NB * TOK
QUERIES = SEQ // 2
CHUNK = 256
CHUNKS = QUERIES // CHUNK
TILE = 512
PAIR = 2 * TOK
PAIRS = SEQ // PAIR
DEEP = HD + NB
SCALE = 1.0 / math.sqrt(HD)
EXP2 = SCALE / math.log(2.0)
F32, BF16 = jnp.float32, jnp.bfloat16
FAR = -1e30
VM = pltpu.VMEM


def eye(n):
    return (lax.broadcasted_iota(jnp.int32, (n, n), 0) == lax.broadcasted_iota(jnp.int32, (n, n), 1)).astype(BF16)


def dot(a, b):
    return lax.dot_general(a, b, (((1,), (0,)), ((), ())), preferred_element_type=F32)


def dot_t(a, b):
    return lax.dot_general(a, b, (((1,), (1,)), ((), ())), preferred_element_type=F32)


def each(low, high, act):
    def step(r, _):
        act(r)
        return 0

    lax.fori_loop(low, high, step, 0)


def place(index, size, align):
    return pl.ds(pl.multiple_of(index * size, align), size)


def remote(src, dst, send, recv, where):
    return pltpu.make_async_remote_copy(
        src_ref=src, dst_ref=dst, send_sem=send, recv_sem=recv, device_id=where
    )


def layer_kernel(
    q_hbm, k_hbm, v_hbm, w_hbm, llm_hbm, sources_hbm, first_block,
    dq_own, dkv_own, blocks_in,
    q, k, v, w, llm, sources,
    own, do_own, codes, do_rows, do_mine, grad, grad_near, grad_far, ahead, code_own, page_own, pages,
    qT, kT, vT, doT, page, krow, vrow, sa, sb, ps, ds, don, qn, stat, dqa, ctxT, dqT,
    part, partner, summed, ctx_own,
    ctx_far, pair, lanes_in, lane_sum, lane_out, z_in, deep_in, deep, last_in, turned,
    code_s, code_r, page_s, page_r, q_s, q_r, k_s, k_r, v_s, v_r, do_s, do_r, dt_s, dt_r, kk_s, kk_r, vv_s, vv_r,
    c_s, c_r, dq_s, dq_r, x_s, x_r, kv_s, kv_r, r_s, r_r, f_s, f_r, l_s, l_r, n_s, n_r, b_s, b_r, one_s, one_r, local, load,
):
    blk, dp = lax.axis_index("blk"), lax.axis_index("dp")
    core = lax.rem(blk, 2)
    sibling = blk + 1 - 2 * core
    head = blk // 2
    width = w.shape[1]
    wide = width // 2
    z_hi, y = dp // NY, lax.rem(dp, NY)
    z_lo, x_at = head // NX, lax.rem(head, NX)

    arguments = ((k_hbm, k), (v_hbm, v), (q_hbm, q), (w_hbm, w), (sources_hbm, sources))
    loads = [pltpu.make_async_copy(src, dst, load.at[n]) for n, (src, dst) in enumerate(arguments)]
    held = llm_hbm.shape[0]
    for m in range(MERGE):
        src = llm_hbm.at[:, pl.ds(m * w.shape[1], w.shape[1])]
        loads.append(pltpu.make_async_copy(src, llm.at[pl.ds(m * held, held), :], load.at[5 + m]))
    for copy in loads:
        copy.start()

    barrier = pltpu.get_barrier_semaphore()
    each(1, ND, lambda r: pl.semaphore_signal(barrier, inc=1, device_id={"dp": lax.rem(dp + r, ND)}))
    each(
        1, ND,
        lambda r: pl.semaphore_signal(barrier, inc=1, device_id={"blk": sibling, "dp": lax.rem(dp + r, ND)}),
    )
    each(1, NB, lambda r: pl.semaphore_signal(barrier, inc=1, device_id={"blk": lax.rem(blk + r, NB)}))
    ident = eye(LANES)
    big = eye(TOK)
    small = eye(HD)
    for n, x in enumerate((k, v, q)):
        loads[n].wait()
        for i in range(HF // LANES):
            own[n, pl.ds(i * LANES, LANES), :] = dot_t(ident, x[:, i * LANES : (i + 1) * LANES]).astype(BF16)
    loads[4].wait()
    code_own[...] = jnp.concatenate([sources[...], sources[...]], axis=1)
    codes[pl.ds(dp, 1)] = code_own[...][None]
    page_own[...] = jnp.broadcast_to(first_block[...].astype(F32), (1, LANES))
    pages[pl.ds(blk, 1)] = page_own[...][None]
    pl.semaphore_wait(barrier, NB + 2 * ND - 3)

    def towards(r):
        return lax.rem(blk + r, NB)

    def piece(n, to):
        return own.at[n, place(to // 2, HD, 16), place(lax.rem(to, 2), HALF, HALF)]

    def code_copy(r):
        to = lax.rem(dp + r, ND)
        return remote(code_own, codes.at[dp], code_s.at[r], code_r.at[r], {"dp": to})

    def page_copy(r):
        return remote(page_own, pages.at[blk], page_s.at[r], page_r.at[r], {"blk": towards(r)})

    def key_lanes(block, side):
        return pl.ds(pl.multiple_of(block * TOK + side * HALF, HALF), HALF)

    def k_copy(r):
        to = towards(r)
        dst = kT.at[pl.ds(0, HD), key_lanes(blk, lax.rem(to, 2))]
        return remote(piece(0, to), dst, k_s.at[r], k_r.at[r], {"blk": to})

    def v_copy(r):
        to = towards(r)
        return remote(piece(1, to), vT.at[:, key_lanes(blk, lax.rem(to, 2))], v_s.at[r], v_r.at[r], {"blk": to})

    def q_copy(r):
        to = towards(r)
        return remote(piece(2, to), qT.at[:, place(blk, HALF, HALF)], q_s.at[r], q_r.at[r], {"blk": to})

    def kk_copy(r):
        half = kT.at[pl.ds(0, HD), key_lanes(lax.rem(blk + NB - r, NB), core)]
        return remote(half, half, kk_s.at[r], kk_r.at[r], {"blk": sibling})

    def vv_copy(r):
        half = vT.at[:, key_lanes(lax.rem(blk + NB - r, NB), core)]
        return remote(half, half, vv_s.at[r], vv_r.at[r], {"blk": sibling})

    def do_copy(r):
        to = lax.rem(dp + r, ND)
        return remote(
            do_rows.at[place(to, SENT, 32), :], do_mine.at[place(dp, SENT, 32), :], do_s.at[r], do_r.at[r], {"dp": to}
        )

    def dt_copy(r):
        to = towards(r)
        src = do_own.at[place(to // 2, HD, 16), place(lax.rem(to, 2), HALF, HALF)]
        return remote(src, doT.at[:, place(blk, HALF, HALF)], dt_s.at[r], dt_r.at[r], {"blk": to})

    mine_at = (place(head, HD, 16), place(core, HALF, HALF))

    def c_copy(r):
        to = towards(r)
        return remote(ctxT.at[:, place(to, HALF, HALF)], ctx_own.at[mine_at], c_s.at[r], c_r.at[r], {"blk": to})

    def dq_copy(r):
        to = towards(r)
        return remote(dqT.at[:, place(to, HALF, HALF)], dq_own.at[mine_at], dq_s.at[r], dq_r.at[r], {"blk": to})

    def x_copy(block):
        lanes = key_lanes(block, 1 - core)
        return remote(
            part.at[:, :, lanes], partner.at[:, :, place(block, HALF, HALF)], x_s.at[block], x_r.at[block],
            {"blk": sibling},
        )

    def kv_copy(block):
        r = lax.rem(block + NB - blk, NB)
        return remote(
            summed.at[:, :, place(block, HALF, HALF)], dkv_own.at[:, mine_at[0], mine_at[1]],
            kv_s.at[r], kv_r.at[r], {"blk": block},
        )

    def half_of(r, side):
        return grad.at[place(lax.rem(dp + r, ND), SENT, 32), pl.ds(pl.multiple_of(side * wide, LANES), wide)]

    def near_copy(r):
        dst = grad_near.at[place(dp, SENT, 32), :]
        return remote(half_of(r, core), dst, r_s.at[r], r_r.at[r], {"dp": lax.rem(dp + r, ND)})

    def far_copy(r):
        dst = grad_far.at[place(dp, SENT, 32), :]
        to = {"blk": sibling, "dp": lax.rem(dp + r, ND)}
        return remote(half_of(r, 1 - core), dst, f_s.at[r], f_r.at[r], to)

    def ctx_copy():
        return remote(ctx_own, ctx_far, one_s.at[2], one_r.at[2], {"blk": sibling})

    def l_copy(r):
        to = lax.rem(y + r, NY)
        src = pair.at[:, place(to, HD, 16), pl.ds(0, YFIRST)]
        return remote(src, lanes_in.at[r], l_s.at[r], l_r.at[r], {"dp": z_hi * NY + to})

    def z_copy():
        return remote(lane_out, z_in, one_s.at[1], one_r.at[1], {"dp": (1 - z_hi) * NY + y})

    def m_copy():
        src = pair.at[1 - z_hi, :, pl.ds(YFIRST, wide - YFIRST)]
        return remote(src, deep_in, one_s.at[3], one_r.at[3], {"dp": (1 - z_hi) * NY + y})

    def n_copy(r):
        to = lax.rem(y + r, NY)
        return remote(deep.at[place(to, HD, 16), :], last_in.at[r], n_s.at[r], n_r.at[r], {"dp": z_hi * NY + to})

    def b_copy(i):
        return remote(
            turned.at[place(i, HD, 16), :], blocks_in.at[head], b_s.at[i], b_r.at[head], {"blk": NB // 2 * core + i}
        )

    def b_wait(i):
        return remote(turned.at[place(i, HD, 16), :], blocks_in.at[i], b_s.at[i], b_r.at[i], {"blk": sibling})

    each(1, ND, lambda r: code_copy(r).start())

    def send_keys(r):
        page_copy(r).start()
        k_copy(r).start()

    each(1, NB, send_keys)
    each(1, NB, lambda r: v_copy(r).start())
    mine = [
        pltpu.make_async_copy(piece(0, blk), kT.at[pl.ds(0, HD), key_lanes(blk, core)], local.at[0]),
        pltpu.make_async_copy(piece(1, blk), vT.at[:, key_lanes(blk, core)], local.at[1]),
        pltpu.make_async_copy(piece(2, blk), qT.at[:, place(blk, HALF, HALF)], local.at[2]),
    ]
    for copy in mine:
        copy.start()
    for copy in mine:
        copy.wait()
    kk_copy(0).start()
    vv_copy(0).start()

    for copy in (loads[3], *loads[5:]):
        copy.wait()
    ahead[...] = dot_t(llm[...], w[...]).astype(BF16)
    each(1, ND, lambda r: code_copy(r).wait_recv())
    asked = jnp.broadcast_to(codes[...].astype(F32), (ND, PORTION, LANES)).reshape(ND * PORTION, LANES)
    spot = dp * PORTION + lax.rem(lax.broadcasted_iota(jnp.int32, asked.shape, 0), PORTION)
    asked = jnp.where(lax.broadcasted_iota(jnp.int32, asked.shape, 1) == spot, asked, 0.0)
    base = ((blk * ND + dp) * held).astype(F32)
    asked = jnp.broadcast_to(jnp.sum(asked, axis=1, keepdims=True) - base, asked.shape).astype(BF16)
    tok = lax.broadcasted_iota(jnp.int32, (TOK, ND * PORTION), 0)
    spread = (tok // MERGE == lax.broadcasted_iota(jnp.int32, (TOK, ND * PORTION), 1)).astype(BF16)
    row = dot(spread, asked)
    row = jnp.concatenate([row, row], axis=1)
    spot = lax.broadcasted_iota(jnp.int32, row.shape, 1)
    turn_of = lax.rem(lax.broadcasted_iota(jnp.int32, row.shape, 0), MERGE)
    hot = jnp.where((row == lax.rem(spot, held).astype(F32)) & (turn_of == spot // held), 1.0, 0.0).astype(BF16)
    do_rows[...] = dot(hot, ahead[...]).astype(BF16)

    def send_query(n):
        to = 2 * (NX * lax.rem(z_lo + n // (2 * NX), 2) + lax.rem(x_at + n // 2, NX)) + lax.rem(core + n, 2)
        q_copy(lax.rem(to + NB - blk, NB)).start()


    def relay_key(r):
        k_copy(r).wait_recv()
        kk_copy(r).start()
        page_copy(r).wait_recv()

    def key_block(r):
        block = lax.rem(sibling + NB - r, NB)
        cols = place(block, TOK, TOK)
        mark = (lax.broadcasted_iota(jnp.int32, (NB, LANES), 0).astype(F32) == pages[block]).astype(BF16)
        page[:, place(block, HALF, HALF)] = mark
        kT[HD:DEEP, key_lanes(block, 0)] = mark
        kT[HD:DEEP, key_lanes(block, 1)] = mark
        krow[cols, :] = dot_t(big, kT[:, cols]).astype(BF16)

    def relay_value(r):
        v_copy(r).wait_recv()
        vv_copy(r).start()

    each(1, NB // 2, relay_key)
    each(1, ND, lambda r: do_copy(r).start())
    do_mine[place(dp, SENT, 32), :] = do_rows[place(dp, SENT, 32), :]
    each(1, NB, send_query)
    each(NB // 2, NB, relay_key)
    each(0, NB, lambda r: kk_copy(r).wait_recv())
    for n in range(NB):
        key_block(n)


    def chunk_at(i):
        return NX * lax.rem(z_lo + i // NX, 2) + lax.rem(x_at + CHUNKS - i, NX)

    def wait_q(i):
        for e in (0, 1):
            r = lax.rem(blk + NB - 2 * chunk_at(i) - e, NB)

            @pl.when(r != 0)
            def _():
                q_copy(r).wait_recv()

    def query(i):
        cols = place(chunk_at(i), CHUNK, CHUNK)
        far = (1.0 - page[:, cols].astype(F32)) * FAR
        return jnp.concatenate([qT[:, cols], far.astype(BF16)], axis=0)

    def mix(cur, now, nxt, then, top):
        qx = query(then)
        cols = place(chunk_at(now), CHUNK, CHUNK)
        new = jnp.full((8, CHUNK), -3e38, F32)
        total = jnp.zeros((8, CHUNK), F32)
        out = jnp.zeros((HD, CHUNK), F32)
        for j in range(SEQ // TILE):
            rows = pl.ds(j * TILE, TILE)
            s = dot(krow[rows, :], qx)
            nxt[rows, :] = s
            new = jnp.maximum(new, jnp.max(s.reshape(TILE // 8, 8, CHUNK), axis=0))
            if cur is not None:
                p = jnp.exp2(cur[rows, :] * EXP2 - top)
                total = total + jnp.sum(p.reshape(TILE // 8, 8, CHUNK), axis=0)
                p = p.astype(BF16)
                ps[rows, cols] = p
                out = out + dot(vT[:, rows], p)
        if cur is not None:
            for e in (0, 1):
                at = place(2 * now + e, TOK, TOK)
                vrow[at, :] = dot_t(big, vT[:, at]).astype(BF16)
            inv = 1.0 / jnp.sum(total, axis=0, keepdims=True)
            ctxT[:, cols] = (out * inv).astype(BF16)
            stat[0:1, cols] = inv
        return jnp.max(new, axis=0, keepdims=True) * EXP2

    def send_context(i):
        for e in (0, 1):
            r = lax.rem(2 * chunk_at(i) + e + NB - blk, NB)

            @pl.when(r != 0)
            def _():
                c_copy(r).start()

    each(1, NB // 2, relay_value)
    wait_q(0)
    top = mix(None, 0, sa, 0, None)
    each(NB // 2, NB, relay_value)

    grad[...] = dot(hot, llm[...]).astype(BF16)
    each(0, NB, lambda r: vv_copy(r).wait_recv())

    def forward(i, top):
        wait_q(2 * i + 1)
        top = mix(sa, 2 * i, sb, 2 * i + 1, top)

        @pl.when(i > 0)
        def _():
            send_context(2 * i - 1)

        @pl.when(i < CHUNKS // 2 - 1)
        def _():
            wait_q(2 * i + 2)

        top = mix(sb, 2 * i + 1, sa, lax.rem(2 * i + 2, CHUNKS), top)
        send_context(2 * i)

        @pl.when(i == 0)
        def _():
            each(1, ND, lambda r: do_copy(r).wait_recv())
            for n in range(HF // LANES):
                lanes = slice(n * LANES, (n + 1) * LANES)
                do_own[pl.ds(n * LANES, LANES), :] = dot_t(ident, do_mine[:, lanes]).astype(BF16)
            each(1, NB, lambda r: dt_copy(r).start())
            pltpu.make_async_copy(
                do_own.at[mine_at], doT.at[:, place(blk, HALF, HALF)], local.at[4]
            ).start()
        @pl.when(i == 1)
        def _():
            def send_rows(r):
                near_copy(r).start()
                far_copy(r).start()

            each(1, ND, send_rows)
            far_copy(0).start()
            pltpu.make_async_copy(half_of(0, core), grad_near.at[place(dp, SENT, 32), :], local.at[3]).start()

        return top

    lax.fori_loop(0, CHUNKS // 2, forward, top)
    send_context(CHUNKS - 1)
    own_context = pltpu.make_async_copy(ctxT.at[:, place(blk, HALF, HALF)], ctx_own.at[mine_at], local.at[5])
    own_context.start()
    pltpu.make_async_copy(do_own.at[mine_at], doT.at[:, place(blk, HALF, HALF)], local.at[4]).wait()
    each(1, NB, lambda r: dt_copy(r).wait_recv())

    def middle(i):
        cols = place(i, CHUNK, CHUNK)
        inv = stat[0:1, cols]
        dof = doT[:, cols].astype(F32)
        stat[1:2, cols] = jnp.sum(dof * ctxT[:, cols].astype(F32), axis=0, keepdims=True)
        don[cols, :] = dot_t(big, (dof * inv).astype(BF16)).astype(BF16)
        qn[cols, :] = dot_t(big, (qT[:, cols].astype(F32) * inv).astype(BF16)).astype(BF16)
        dqa[:, cols] = jnp.zeros((HD, CHUNK), F32)

    for i in range(CHUNKS):
        middle(i)

    def chip_at(j):
        return lax.rem(head + 1 + j, PAIRS)

    def cross(j):
        for e in (0, 1):
            x_copy(2 * chip_at(j) + e).start()

    def add_up(j):
        for e in (0, 1):
            block = 2 * chip_at(j) + e
            x_copy(block).wait_recv()
            at = place(block, HALF, HALF)
            summed[:, :, at] = (
                part[:, :, key_lanes(block, core)].astype(F32) + partner[:, :, at].astype(F32)
            ).astype(BF16)

    def hand_out(j):
        for e in (0, 1):
            kv_copy(2 * chip_at(j) + e).start()

    def pass_context():
        own_context.wait()
        each(1, NB, lambda r: c_copy(r).wait_recv())
        ctx_copy().start()

    def weight_part():
        ctx_copy().wait_recv()
        pltpu.make_async_copy(half_of(0, core), grad_near.at[place(dp, SENT, 32), :], local.at[3]).wait()
        each(1, ND, lambda r: near_copy(r).wait_recv())
        each(0, ND, lambda r: far_copy(r).wait_recv())
        near = grad_near[...]
        for n in range(HF // LANES):
            at = pl.ds(n * LANES, LANES)
            term = dot(ctx_own[at, :], near) + dot(ctx_far[at, :], grad_far[...])
            for g in (0, LANES // 2):
                at = n * LANES + g
                pair[at // (HF // 2), pl.ds(at % (HF // 2), LANES // 2), :] = term[g : g + LANES // 2].astype(BF16)

    def weight_lanes():
        m_copy().start()
        each(1, NY, lambda r: l_copy(r).start())

    def weight_deep():
        m_copy().wait_recv()
        deep[...] = (pair[z_hi, :, YFIRST:].astype(F32) + deep_in[...].astype(F32)).astype(BF16)
        total = pair[:, place(y, HD, 16), :YFIRST].astype(F32)
        for r in range(1, NY):
            l_copy(r).wait_recv()
            total = total + lanes_in[r].astype(F32)
        far = jnp.where(z_hi == 0, total[1], total[0])
        lane_out[...] = far.astype(BF16)
        lane_sum[...] = jnp.where(z_hi == 0, total[0], total[1])

    def weight_far():
        z_copy().start()
        each(1, NY, lambda r: n_copy(r).start())

    def backward(j):
        @pl.when(j > 0)
        def _():
            cross(j - 1)

        pl.when(j == 3)(weight_lanes)
        pl.when(j == PAIRS - 1)(weight_far)

        rows = place(chip_at(j), PAIR, PAIR)
        values = vrow[rows, :]
        for i in range(CHUNKS):
            cols = pl.ds(i * CHUNK, CHUNK)
            dp_part = dot(values, doT[:, cols])
            ds[:, cols] = (ps[rows, cols].astype(F32) * (dp_part - stat[1:2, cols])).astype(BF16)
        dv = dot(ps[rows, :], don[...])
        dk = dot(ds[...], qn[...])
        dqa[...] += dot(kT[0:HD, rows], ds[...])
        part[0, :, rows] = dot_t(small, (dk * SCALE).astype(BF16)).astype(BF16)
        part[1, :, rows] = dot_t(small, dv.astype(BF16)).astype(BF16)

        @pl.when(j > 1)
        def _():
            hand_out(j - 2)

        @pl.when(j > 0)
        def _():
            add_up(j - 1)

        pl.when(j == 1)(pass_context)
        pl.when(j == 2)(weight_part)
        pl.when(j == PAIRS - 2)(weight_deep)


    each(0, PAIRS, backward)
    cross(PAIRS - 1)
    hand_out(PAIRS - 2)
    dqT[...] = (dqa[...] * (stat[0:1, :] * SCALE)).astype(BF16)
    each(1, NB, lambda r: dq_copy(r).start())
    own_dq = pltpu.make_async_copy(dqT.at[:, place(blk, HALF, HALF)], dq_own.at[mine_at], local.at[6])
    own_dq.start()
    add_up(PAIRS - 1)
    kv_copy(sibling).start()
    own_dkv = pltpu.make_async_copy(
        summed.at[:, :, place(blk, HALF, HALF)], dkv_own.at[:, mine_at[0], mine_at[1]], local.at[7]
    )
    own_dkv.start()

    z_copy().wait_recv()
    rest = deep[place(y, HD, 16), :].astype(F32)
    for r in range(1, NY):
        n_copy(r).wait_recv()
        rest = rest + last_in[r].astype(F32)
    total = jnp.concatenate([lane_sum[...] + z_in[...].astype(F32), rest], axis=1).astype(BF16)
    for i in range(wide // LANES):
        turned[pl.ds(i * LANES, LANES), :] = dot_t(ident, total[:, i * LANES : (i + 1) * LANES]).astype(BF16)

    def b_send(i):
        @pl.when(NB // 2 * core + i != blk)
        def _():
            b_copy(i).start()

    each(0, NB // 2, b_send)
    source_core = blk // (NB // 2)

    @pl.when(source_core == core)
    def _():
        blocks_in[pl.ds(head, 1)] = turned[place(lax.rem(blk, NB // 2), HD, 16), :][None]

    own_dkv.wait()

    def kv_arrived(r):
        kv_copy(lax.rem(blk + r, NB)).wait_recv()

    each(1, NB, kv_arrived)
    own_dq.wait()
    each(1, NB, lambda r: dq_copy(r).wait_recv())

    def b_recv(i):
        @pl.when(2 * i + source_core != blk)
        def _():
            b_wait(i).wait_recv()

    each(0, NB // 2, b_recv)
    def b_sent(i):
        @pl.when(NB // 2 * core + i != blk)
        def _():
            b_copy(i).wait_send()

    each(0, NB // 2, b_sent)

    def sent(r):
        for copy in (page_copy, k_copy, v_copy, q_copy, dt_copy, c_copy, dq_copy):
            copy(r).wait_send()
        kv_copy(lax.rem(blk + r, NB)).wait_send()

    each(1, NB, sent)

    def sent_over(r):
        kk_copy(r).wait_send()
        vv_copy(r).wait_send()
        x_copy(r).wait_send()

    each(0, NB, sent_over)
    each(1, NY, lambda r: l_copy(r).wait_send())
    each(0, ND, lambda r: far_copy(r).wait_send())
    each(1, NY, lambda r: n_copy(r).wait_send())
    m_copy().wait_send()
    ctx_copy().wait_send()
    z_copy().wait_send()

    def sent_dp(r):
        for copy in (code_copy, do_copy, near_copy):
            copy(r).wait_send()

    each(1, ND, sent_dp)


def finish_kernel(dq, dkv, blocks, q_out, k_out, v_out, w_out):
    big = eye(TOK)
    q_out[...] = dot_t(big, dq[...]).astype(BF16)
    k_out[...] = dot_t(big, dkv[0]).astype(BF16)
    v_out[...] = dot_t(big, dkv[1]).astype(BF16)
    whole = blocks[0].astype(F32)
    for i in range(1, NB // 2):
        whole = whole + blocks[i].astype(F32)
    w_out[...] = whole


def finish(dq, dkv, blocks):
    return pl.pallas_call(
        finish_kernel,
        out_shape=[jax.ShapeDtypeStruct((TOK, HF), BF16)] * 3 + [jax.ShapeDtypeStruct((HD, HD), F32)],
        in_specs=[pl.BlockSpec(memory_space=VM)] * 3,
        out_specs=[pl.BlockSpec(memory_space=VM)] * 4,
        compiler_params=pltpu.CompilerParams(vmem_limit_bytes=8 * 2**20),
    )(dq, dkv, blocks)


def layer(q, k, v, w, llm, sources, first_block):
    dma = pltpu.SemaphoreType.DMA
    wide = w.shape[1] // 2
    nb, nd = [dma((NB,))] * 2, [dma((ND,))] * 2
    return pl.pallas_call(
        layer_kernel,
        out_shape=[
            jax.ShapeDtypeStruct((HF, TOK), BF16),
            jax.ShapeDtypeStruct((2, HF, TOK), BF16),
            jax.ShapeDtypeStruct((NB // 2, HD, HD), BF16),
        ],
        in_specs=[pl.BlockSpec(memory_space=pltpu.HBM)] * 6 + [pl.BlockSpec(memory_space=VM)],
        out_specs=[pl.BlockSpec(memory_space=VM)] * 3,
        scratch_shapes=[
            VM(q.shape, BF16), VM(k.shape, BF16), VM(v.shape, BF16), VM(w.shape, BF16), VM((TOK, w.shape[1]), BF16),
            VM(sources.shape, jnp.int32),
            VM((3, HF, TOK), BF16), VM((HF, TOK), BF16), VM((ND, 1, LANES), jnp.int32),
            VM((TOK, HF), BF16), VM((TOK, HF), BF16), VM((TOK, w.shape[1]), BF16), VM((TOK, wide), BF16),
            VM((TOK, wide), BF16), VM((TOK, HF), BF16),
            VM((1, LANES), jnp.int32), VM((1, LANES), F32), VM((NB, 1, LANES), F32),
            VM((HD, QUERIES), BF16), VM((DEEP, SEQ), BF16), VM((HD, SEQ), BF16), VM((HD, QUERIES), BF16),
            VM((NB, QUERIES), BF16), VM((SEQ, DEEP), BF16), VM((SEQ, HD), BF16),
            VM((SEQ, CHUNK), F32), VM((SEQ, CHUNK), F32), VM((SEQ, QUERIES), BF16), VM((PAIR, QUERIES), BF16),
            VM((QUERIES, HD), BF16), VM((QUERIES, HD), BF16), VM((8, QUERIES), F32), VM((HD, QUERIES), F32),
            VM((HD, QUERIES), BF16), VM((HD, QUERIES), BF16),
            VM((2, HD, SEQ), BF16), VM((2, HD, QUERIES), BF16), VM((2, HD, QUERIES), BF16),
            VM((HF, TOK), BF16),
            VM((HF, TOK), BF16), VM((2, HF // 2, wide), BF16), VM((NY, 2, HD, YFIRST), BF16),
            VM((HD, YFIRST), F32), VM((HD, YFIRST), BF16), VM((HD, YFIRST), BF16),
            VM((HF // 2, wide - YFIRST), BF16), VM((HF // 2, wide - YFIRST), BF16), VM((NY, HD, wide - YFIRST), BF16),
            VM((wide, HD), BF16),
            *nd, *nb, *nb, *nb, *nb, *nd, *nb, *nb, *nb,
            *nb, *nb, *nb, *nb, *nd, *nd, *nd, *nd, *nd, dma((4,)), dma((4,)), dma((8,)), dma((5 + MERGE,)),
        ],
        compiler_params=pltpu.CompilerParams(
            collective_id=0, has_side_effects=True, vmem_limit_bytes=48 * 2**20
        ),
    )(q, k, v, w, llm, sources, first_block)


def body(saved_query, saved_key, saved_value, out_weight, llm_grad, row_source, page_start, page_size):
    stay = [
        pltpu.with_memory_space_constraint(x, pltpu.HBM)
        for x in (saved_query[0], saved_key[0], saved_value[0], out_weight, llm_grad, row_source)
    ]
    turned = layer(*stay, page_start)
    query_grad, key_grad, value_grad, weight_grad = finish(*turned)
    return (query_grad[None], key_grad[None], value_grad[None], weight_grad)


def solution(mesh):
    in_specs = (
        P("dp", "blk", None),
        P("dp", "blk", None),
        P("dp", "blk", None),
        P(),
        P(("blk", "dp"), None),
        P("dp", "blk"),
        P("dp", "blk"),
        P("dp", "blk"),
    )
    out_specs = (P("dp", "blk", None), P("dp", "blk", None), P("dp", "blk", None), P("blk", "dp"))
    return jax.shard_map(body, mesh=mesh, in_specs=in_specs, out_specs=out_specs, check_vma=False)
```
